32 devices in a mesh: dp: 16 (over z, y, x), tensor: 2 (over core).
Axes of the slice: x: 2, y: 2, z: 4, core: 2. Of those that a mesh axis runs over, the one named last changes fastest.
Arguments:
- frames: bfloat16 [32, 512, 1536], P('dp', 'tensor'), may hold values from -6 to 6
- text_states: bfloat16 [32, 64, 1536], P('dp'), may hold values from -6 to 6
- norm_gain: bfloat16 [3, 1536], P(None, 'dp'), may hold values from 0.25 to 1.75
- norm_shift: bfloat16 [3, 1536], P(None, 'dp'), may hold values from -2.5 to 2.5
- self_project: bfloat16 [3, 1536, 1536], P(None, 'dp', 'tensor'), may hold values from -0.15625 to 0.15625
- self_output: bfloat16 [1536, 1536], P('tensor', 'dp'), may hold values from -0.625 to 0.625
- cross_query: bfloat16 [1536, 1536], P('dp', 'tensor'), may hold values from -0.15625 to 0.15625
- cross_memory: bfloat16 [2, 1536, 1536], P(None, 'dp', 'tensor'), may hold values from -0.15625 to 0.15625
- cross_output: bfloat16 [1536, 1536], P('tensor', 'dp'), may hold values from -0.4375 to 0.4375
- feed_input: bfloat16 [1536, 6144], P('dp', 'tensor'), may hold values from -0.15625 to 0.15625
- feed_output: bfloat16 [6144, 1536], P('tensor', 'dp'), may hold values from -0.078125 to 0.078125
- upstream: bfloat16 [32, 512, 1536], P('dp', 'tensor'), may hold values from -6 to 6
Outputs:
- layer_out: bfloat16 [32, 512, 1536], P('dp', 'tensor')
- input_grad: float32 [32, 512, 1536], P('dp', 'tensor')
- text_grad: float32 [32, 64, 1536], P('dp')
- gain_grad: float32 [3, 1536], P(None, 'dp')
- shift_grad: float32 [3, 1536], P(None, 'dp')
- self_project_grad: float32 [3, 1536, 1536], P(None, 'dp', 'tensor')
- self_output_grad: float32 [1536, 1536], P('tensor', 'dp')
- cross_query_grad: float32 [1536, 1536], P('dp', 'tensor')
- cross_memory_grad: float32 [2, 1536, 1536], P(None, 'dp', 'tensor')
- cross_output_grad: float32 [1536, 1536], P('tensor', 'dp')
- feed_input_grad: float32 [1536, 6144], P('dp', 'tensor')
- feed_output_grad: float32 [6144, 1536], P('tensor', 'dp')
The draws below stay inside these ranges and needn't reach their ends.
All inputs are finite; a program needn't handle non-finite values.
Results may differ from the reference program's by a relative error of at most 0.028.
Values may be sent and summed in bfloat16 or wider, within the bound.
No kernel may reach another device: no remote copies, remote signals or barrier semaphores. Data moves between devices by JAX's collectives and lax.ppermute only.
A program may use at most 256 MiB of HBM per device.

```python
import math
import jax
import jax.numpy as jnp
from jax import lax

D = 1536
HEADS = 24
HEAD_DIM = 64
FF = 6144
TEXT = 64
SEQ = 512
CLIPS = 32


def raised(entries, rng, source, target, blocks, factor):
    def block_of(dim):
        return (jnp.arange(entries.shape[dim]) // (entries.shape[dim] // blocks)).reshape((-1,) + (1,) * (entries.ndim - 1 - dim))

    first = jax.random.permutation(rng, blocks)[block_of(target)]
    far = (block_of(target) + blocks // 2) % blocks
    return jnp.where((block_of(source) == first) | (block_of(source) == far), factor * entries, entries)


def levels(stream_key, dims, pieces, smallest, high):
    loudness, own = 1.0, jax.random.fold_in(stream_key, 6)
    for position, parts in pieces:
        steps = jnp.exp(jax.random.uniform(jax.random.fold_in(own, position), (parts,), jnp.float32, smallest / len(pieces), high / len(pieces)))
        loudness = loudness * jnp.repeat(steps, dims[position] // parts).reshape([-1 if axis == position else 1 for axis in range(len(dims))])
    return loudness


def gaussian(rng, shape, scale, limit, shards=(), kind=jnp.bfloat16):
    gain = levels(rng, shape, shards, -0.22, 0.18) if shards else 1.0
    array = jax.random.normal(rng, shape, jnp.float32) * scale * gain
    return jnp.minimum(jnp.maximum(array, -limit), limit).astype(kind)


def heavy_noise(rng, extent, spread, bound, cuts, heavy, kind=jnp.bfloat16):
    entries = spread * jax.random.normal(rng, extent, jnp.float32)
    if cuts:
        entries = entries * levels(rng, extent, cuts, -0.22, 0.18)
    return jnp.clip(raised(entries, jax.random.fold_in(rng, 3), *heavy), -bound, bound).astype(kind)


def setup_inputs(seed: int = 0) -> dict:
    seeds = jax.random.split(jax.random.key(seed), 13)
    return {
        "frames": gaussian(seeds[0], (CLIPS, SEQ, D), 1.0, 6.0, ((0, 16), (1, 2))),
        "text_states": gaussian(seeds[1], (CLIPS, TEXT, D), 1.0, 6.0, ((0, 16),)),
        "norm_gain": jnp.clip(1.0 + 0.15 * jax.random.normal(seeds[2], (3, D), jnp.float32), 0.25, 1.75).astype(jnp.bfloat16),
        "norm_shift": gaussian(seeds[3], (3, D), 0.3, 2.5, ((1, 16),)),
        "self_project": gaussian(seeds[4], (3, D, D), D ** -0.5, 0.15625, ((1, 16), (2, 2))),
        "self_output": gaussian(seeds[5], (D, D), (D // 16) ** -0.5, 0.625, ((0, 2), (1, 16))),
        "cross_query": gaussian(seeds[6], (D, D), D ** -0.5, 0.15625, ((0, 16), (1, 2))),
        "cross_memory": gaussian(seeds[7], (2, D, D), D ** -0.5, 0.15625, ((1, 16), (2, 2))),
        "cross_output": gaussian(seeds[8], (D, D), (D // 8) ** -0.5, 0.4375, ((0, 2), (1, 16))),
        "feed_input": gaussian(seeds[9], (D, FF), D ** -0.5, 0.15625, ((0, 16), (1, 2))),
        "feed_output": gaussian(seeds[10], (FF, D), FF ** -0.5, 0.078125, ((0, 2), (1, 16))),
        "upstream": heavy_noise(seeds[11], (CLIPS, SEQ, D), 1.0, 6.0, ((0, 16), (1, 2)), (0, 2, 16, 2.0)),
    }


@jax.custom_vjp
def low(v):
    return lax.optimization_barrier(v.astype(jnp.bfloat16)).astype(jnp.float32)

@jax.custom_vjp
def low_back(v):
    return v

def low_keep(v):
    return (low(v), None)

def low_pass(kept, grad):
    return (grad,)

def back_keep(v):
    return (v, None)

def back_low(kept, grad):
    return (low(grad),)
low.defvjp(low_keep, low_pass)
low_back.defvjp(back_keep, back_low)
precise = lax.Precision.HIGHEST
epsilon = 1e-05

def rounded(value):
    return low_back(low(value))

def matmul(left_side, right_side):
    return jnp.dot(left_side, right_side, precision=precise, preferred_element_type=jnp.float32)

def norm_rows(values, gain_row, shift_row):
    row_mean = lax.optimization_barrier(jnp.mean(values, axis=-1, keepdims=True))
    centred = values - row_mean
    row_var = lax.optimization_barrier(jnp.mean(centred * centred, axis=-1, keepdims=True))
    return centred * lax.rsqrt(row_var + epsilon) * gain_row + shift_row

def causal_attention(queries, keys, values):
    length = queries.shape[0]
    block_size = min(512, length)
    scale = 1.0 / math.sqrt(HEAD_DIM)
    query_heads = queries.reshape(length, HEADS, HEAD_DIM)
    key_heads = keys.reshape(length, HEADS, HEAD_DIM)
    value_heads = values.reshape(length, HEADS, HEAD_DIM)

    def one_block(block_index):
        begin_row = (block_index * block_size).astype(jnp.int32)
        block_queries = lax.dynamic_slice_in_dim(query_heads, begin_row, block_size, 0)
        scores = low_back(jnp.einsum('qhd,khd->hqk', block_queries, key_heads, precision=precise) * scale)
        row_place = begin_row + jnp.arange(block_size, dtype=jnp.int32)
        col_place = jnp.arange(length, dtype=jnp.int32)
        allowed = col_place[None, :] <= row_place[:, None]
        scores = jnp.where(allowed[None], scores, -1e+30)
        chances = low(jax.nn.softmax(scores, axis=-1))
        return jnp.einsum('hqk,khd->qhd', chances, value_heads, precision=precise)
    blocks = lax.map(jax.checkpoint(one_block), jnp.arange(length // block_size, dtype=jnp.int32))
    return blocks.reshape(length, HEADS * HEAD_DIM)

def cross_attention(queries, keys, values):
    length = queries.shape[0]
    scale = 1.0 / math.sqrt(HEAD_DIM)
    query_heads = queries.reshape(length, HEADS, HEAD_DIM)
    key_heads = keys.reshape(keys.shape[0], HEADS, HEAD_DIM)
    value_heads = values.reshape(values.shape[0], HEADS, HEAD_DIM)
    scores = low_back(jnp.einsum('qhd,khd->hqk', query_heads, key_heads, precision=precise) * scale)
    chances = low(jax.nn.softmax(scores, axis=-1))
    attended = jnp.einsum('hqk,khd->qhd', chances, value_heads, precision=precise)
    return attended.reshape(length, HEADS * HEAD_DIM)

def one_clip(frame_rows, text_rows, weight_set):
    gains, shifts, project, self_out, cross_q, memory, cross_out, feed_in, feed_out = weight_set
    normed_one = low(norm_rows(frame_rows, gains[0], shifts[0]))
    queries = rounded(matmul(normed_one, project[0]))
    keys_self = rounded(matmul(normed_one, project[1]))
    values_self = rounded(matmul(normed_one, project[2]))
    attended = rounded(causal_attention(queries, keys_self, values_self))
    after_self = frame_rows + low_back(matmul(attended, self_out))
    normed_two = low(norm_rows(after_self, gains[1], shifts[1]))
    cross_queries = rounded(matmul(normed_two, cross_q))
    cross_keys = rounded(matmul(text_rows, memory[0]))
    cross_values = rounded(matmul(text_rows, memory[1]))
    cross_att = rounded(cross_attention(cross_queries, cross_keys, cross_values))
    after_cross = after_self + low_back(matmul(cross_att, cross_out))
    normed_three = low(norm_rows(after_cross, gains[2], shifts[2]))
    hidden = low(jax.nn.gelu(low_back(matmul(normed_three, feed_in)), approximate=False))
    return after_cross + low_back(matmul(hidden, feed_out))

def reference(frames, text_states, norm_gain, norm_shift, self_project, self_output, cross_query, cross_memory, cross_output, feed_input, feed_output, upstream):
    weight_set = (norm_gain.astype(jnp.float32), norm_shift.astype(jnp.float32), self_project.astype(jnp.float32), self_output.astype(jnp.float32), cross_query.astype(jnp.float32), cross_memory.astype(jnp.float32), cross_output.astype(jnp.float32), feed_input.astype(jnp.float32), feed_output.astype(jnp.float32))

    def forward(frame_all, text_all, weight_all):

        def clip_step(scan_carry, clip_pair):
            return (scan_carry, jax.checkpoint(one_clip)(clip_pair[0], clip_pair[1], weight_all))
        carry_end, outputs = lax.scan(clip_step, jnp.zeros((), jnp.float32), (frame_all, text_all))
        return outputs
    outputs, pull_back = jax.vjp(forward, frames.astype(jnp.float32), text_states.astype(jnp.float32), weight_set)
    frame_grad, text_grad, weight_grads = pull_back(upstream.astype(jnp.float32))
    return (outputs.astype(jnp.bfloat16), frame_grad, text_grad, weight_grads[0], weight_grads[1], weight_grads[2], weight_grads[3], weight_grads[4], weight_grads[5], weight_grads[6], weight_grads[7], weight_grads[8])
```

```python
import math

import jax
import jax.numpy as jnp
from jax import lax
from jax.sharding import Mesh
from jax.sharding import PartitionSpec as P

HEAD_DIM = 64
EPS = 1e-05
BF = jnp.bfloat16
F32 = jnp.float32
SWAP = [(0, 1), (1, 0)]


def mm(left, right):
    return jnp.dot(left, right, preferred_element_type=F32)


def mm_t(left, right):
    return lax.dot_general(left, right, (((1,), (1,)), ((), ())), preferred_element_type=F32)


def mm_rows(left, right):
    return lax.dot_general(left, right, (((0,), (0,)), ((), ())), preferred_element_type=F32)


def norm_stats(values):
    mean = jnp.mean(values, axis=-1, keepdims=True)
    centred = values - mean
    inv = lax.rsqrt(jnp.mean(centred * centred, axis=-1, keepdims=True) + EPS)
    return mean, inv


def norm_apply(values, stats, gain, shift):
    return ((values - stats[0]) * stats[1] * gain + shift).astype(BF)


def norm_back(values, stats, gain, grad):
    xhat = (values - stats[0]) * stats[1]
    scaled = grad * gain
    part = jnp.mean(scaled, axis=-1, keepdims=True)
    cross = jnp.mean(scaled * xhat, axis=-1, keepdims=True)
    value_grad = (scaled - part - xhat * cross) * stats[1]
    return value_grad, jnp.sum(grad * xhat, axis=0), jnp.sum(grad, axis=0)


def gelu_pair(pre):
    phi = 0.5 * (1.0 + lax.erf(pre * (1.0 / math.sqrt(2.0))))
    dens = jnp.exp(-0.5 * pre * pre) * (1.0 / math.sqrt(2.0 * math.pi))
    return (pre * phi).astype(BF), (phi + pre * dens).astype(BF)


def heads(matrix):
    return matrix.reshape(*matrix.shape[:-1], matrix.shape[-1] // HEAD_DIM, HEAD_DIM)


def flat(matrix):
    return matrix.reshape(*matrix.shape[:-2], -1)


SCALE = 1.0 / math.sqrt(HEAD_DIM)


def causal_scores(q, k):
    scores = jnp.einsum("bqhd,bkhd->bhqk", heads(q), heads(k), preferred_element_type=F32) * SCALE
    n = q.shape[1]
    allowed = jnp.arange(n)[None, :] <= jnp.arange(n)[:, None]
    return jnp.where(allowed, scores, -1e30)


def attend(q, k, v):
    scores = causal_scores(q, k)
    top = jnp.max(scores, axis=-1, keepdims=True)
    terms = jnp.exp(scores - top)
    total = jnp.sum(terms, axis=-1, keepdims=True)
    out = jnp.einsum(
        "bhqk,bkhd->bqhd", (terms / total).astype(BF), heads(v), preferred_element_type=F32
    )
    return flat(out).astype(BF), top + jnp.log(total)


def probs_back(chances, dp, q, k, grad):
    dot = jnp.sum(chances * dp, axis=-1, keepdims=True)
    ds = (chances * (dp - dot)).astype(BF)
    dv = jnp.einsum("bhqk,bqhd->bkhd", chances.astype(BF), grad, preferred_element_type=F32)
    dq = jnp.einsum("bhqk,bkhd->bqhd", ds, heads(k), preferred_element_type=F32) * SCALE
    dk = jnp.einsum("bhqk,bqhd->bkhd", ds, heads(q), preferred_element_type=F32) * SCALE
    return flat(dq).astype(BF), flat(dk).astype(BF), flat(dv).astype(BF)


def attend_back(q, k, v, log_total, grad):
    chances = jnp.exp(causal_scores(q, k) - log_total)
    grad = heads(grad)
    dp = jnp.einsum("bqhd,bkhd->bhqk", grad, heads(v), preferred_element_type=F32)
    return probs_back(chances, dp, q, k, grad)


def cross_attend(q, k, v):
    scores = jnp.einsum("bqhd,bkhd->bhqk", heads(q), heads(k), preferred_element_type=F32) * SCALE
    chances = jax.nn.softmax(scores, axis=-1)
    out = jnp.einsum("bhqk,bkhd->bqhd", chances.astype(BF), heads(v), preferred_element_type=F32)
    return flat(out).astype(BF), chances


def cross_attend_back(q, k, v, chances, grad):
    grad = heads(grad)
    dp = jnp.einsum("bqhd,bkhd->bhqk", grad, heads(v), preferred_element_type=F32)
    return probs_back(chances, dp, q, k, grad)


class Whole:
    def __init__(self, dp, tensor):
        self.dp, self.tensor = dp, tensor

    def arrange(self, values):
        return values

    def restore(self, values):
        return values

    def gather_norms(self, packed):
        return lax.all_gather(packed, self.dp, axis=0, tiled=True)

    def gather_first(self, shard):
        return lax.all_gather(shard, self.dp, axis=0, tiled=True)

    gather_middle = gather_first

    def scatter_last(self, make):
        whole = make(slice(None), slice(None)).astype(BF)
        return lax.psum_scatter(whole, self.dp, scatter_dimension=0, tiled=True).astype(F32)

    scatter_middle = scatter_last

    def spread(self, rows, clips):
        local = rows.reshape(clips, -1, rows.shape[-1])
        return lax.all_gather(local, self.tensor, axis=1, tiled=True).reshape(-1, rows.shape[-1])

    def sequence(self, rows, clips):
        return rows.reshape(clips, -1, rows.shape[-1])

    def unsequence(self, rows):
        return rows.reshape(-1, rows.shape[-1])

    def clip_rows(self, rows, clips):
        return rows.reshape(clips, -1, rows.shape[-1])

    unclip_rows = unsequence

    def sum_own(self, left, right, product, clips):
        part = product(left, right).astype(BF).reshape(clips, -1, right_width(product, right))
        own = lax.psum_scatter(part, self.tensor, scatter_dimension=1, tiled=True)
        return own.reshape(-1, part.shape[-1]).astype(F32)

    def sum_all(self, values):
        return lax.psum(values.astype(BF), self.tensor).astype(F32)


def right_width(product, right):
    return right.shape[0] if product is mm_t else right.shape[1]


class Block(Whole):
    def __init__(self, width):
        self.width = width
        self.shard = width // 16
        self.core = lax.axis_index("core")

    def order(self):
        own_y, own_x = lax.axis_index("y"), lax.axis_index("x")
        place = jnp.arange(self.width, dtype=jnp.int32)
        quarter, rest = place // (4 * self.shard), place % (4 * self.shard)
        z, row = rest // self.shard, rest % self.shard
        y, x = (quarter // 2) ^ own_y, (quarter % 2) ^ own_x
        source = ((z * 2 + y) * 2 + x) * self.shard + row
        return (jnp.arange(self.width, dtype=jnp.int32)[:, None] == source[None, :]).astype(BF)

    def arrange(self, values):
        return mm(values, self.order()).astype(BF)

    def restore(self, values):
        if values.dtype == BF:
            return mm_t(values, self.order()).astype(BF)
        high = lax.reduce_precision(values, 8, 7)
        low = (values - high).astype(BF)
        order = self.order()
        return mm_t(high.astype(BF), order) + mm_t(low, order)

    def x(self, v):
        return lax.ppermute(v, "x", SWAP)

    def y(self, v):
        return lax.ppermute(v, "y", SWAP)

    def other(self, v):
        return lax.ppermute(v, "core", SWAP)

    def gather_norms(self, packed):
        pair = jnp.stack([packed, lax.ppermute(packed, "z", [(0, 1), (1, 0), (2, 3), (3, 2)])])
        far = lax.ppermute(pair, "z", [(0, 2), (1, 3), (2, 0), (3, 1)])
        own = lax.axis_index("z")
        four = jnp.concatenate([pair, far])
        four = jnp.stack([lax.dynamic_index_in_dim(four, own ^ p, 0, False) for p in range(4)])
        two = jnp.stack([four, self.x(four)])
        whole = jnp.stack([two, self.y(two)])
        return whole.reshape(self.width, packed.shape[-1])

    def halves(self, shard):
        half = shard.shape[1] // 256 * 128
        return shard[:, :half], shard[:, half:]

    def finish(self, first, second):
        n = first.shape[0] // 2
        far_first, far_second = self.y(first), self.x(second)
        left = jnp.concatenate([first, far_first])
        right = jnp.concatenate([second[:n], far_second[:n], second[n:], far_second[n:]])
        return jnp.concatenate([left, right], axis=1)

    def gather_first(self, shard):
        four = lax.all_gather(shard, "z", axis=0, tiled=True)
        a, b = self.halves(four)
        return self.finish(jnp.concatenate([a, self.x(a)]), jnp.concatenate([b, self.y(b)]))

    def gather_middle(self, shard):
        a, b = self.halves(shard)
        four = jnp.stack([a, self.x(a), b, self.y(b)])
        four = lax.all_gather(four, "z", axis=1, tiled=True)
        return self.finish(
            four[:2].reshape(-1, a.shape[1]), four[2:].reshape(-1, a.shape[1])
        )

    def scatter_open(self, make, columns):
        n = self.width // 4
        half = columns // 256 * 128
        left, right = slice(0, half), slice(half, columns)
        far_left = self.y(make(slice(2 * n, 4 * n), left).astype(BF))
        far_right = self.x(
            jnp.concatenate(
                [make(slice(n, 2 * n), right).astype(BF), make(slice(3 * n, 4 * n), right).astype(BF)]
            )
        )
        a = (make(slice(0, 2 * n), left) + far_left.astype(F32)).astype(BF)
        b = [
            (make(slice(0, n), right) + far_right[:n].astype(F32)).astype(BF),
            (make(slice(2 * n, 3 * n), right) + far_right[n:].astype(F32)).astype(BF),
        ]
        return a[:n], a[n:], b[0], b[1]

    def scatter_middle(self, make, columns):
        four = jnp.stack(self.scatter_open(make, columns))
        four = lax.psum_scatter(four, "z", scatter_dimension=1, tiled=True)
        left = four[0].astype(F32) + self.x(four[1]).astype(F32)
        right = four[2].astype(F32) + self.y(four[3]).astype(F32)
        return jnp.concatenate([left, right], axis=1)

    def scatter_last(self, make, columns):
        a0, a1, b0, b1 = self.scatter_open(make, columns)
        far_a, far_b = self.x(a1), self.y(b1)
        both = jnp.stack(
            [
                (a0.astype(F32) + far_a.astype(F32)).astype(BF),
                (b0.astype(F32) + far_b.astype(F32)).astype(BF),
            ]
        )
        both = lax.psum_scatter(both, "z", scatter_dimension=1, tiled=True).astype(F32)
        return jnp.concatenate([both[0], both[1]], axis=1)

    def spread(self, rows, clips):
        return jnp.concatenate([rows, self.other(rows)])

    def sequence(self, rows, clips):
        parts = rows.reshape(2, clips, -1, rows.shape[-1])
        swapped = jnp.where(self.core == 0, parts, parts[::-1])
        return jnp.swapaxes(swapped, 0, 1).reshape(clips, -1, rows.shape[-1])

    def unsequence(self, rows):
        parts = jnp.swapaxes(rows.reshape(rows.shape[0], 2, -1, rows.shape[-1]), 0, 1)
        return jnp.where(self.core == 0, parts, parts[::-1]).reshape(-1, rows.shape[-1])

    def clip_rows(self, rows, clips):
        parts = rows.reshape(2, clips, -1, rows.shape[-1])
        return jnp.swapaxes(parts, 0, 1).reshape(clips, -1, rows.shape[-1])

    def unclip_rows(self, rows):
        parts = rows.reshape(rows.shape[0], 2, -1, rows.shape[-1])
        return jnp.swapaxes(parts, 0, 1).reshape(-1, rows.shape[-1])

    def sum_own(self, left, right, product, clips):
        n = left.shape[0] // 2
        far = self.other(product(left[n:], right).astype(BF))
        return product(left[:n], right) + far.astype(F32)

    def sum_all(self, values):
        return values + self.other(values.astype(BF)).astype(F32)


def layer(
    comm,
    frames,
    text_states,
    norm_gain,
    norm_shift,
    self_project,
    self_output,
    cross_query,
    cross_memory,
    cross_output,
    feed_input,
    feed_output,
    upstream,
):
    clips, own_frames, width = frames.shape
    texts = text_states.shape[1]
    cols = cross_query.shape[1]
    own_rows = clips * own_frames

    def catenate(parts):
        return jnp.concatenate(parts, axis=1)

    norms = comm.gather_norms(
        jnp.pad(jnp.concatenate([norm_gain, norm_shift]).T, ((0, 0), (0, 122)))
    )
    norms = norms.T.astype(F32)
    gain, shift = norms[0:3], norms[3:6]
    first_set = catenate([self_project[0], self_project[1], self_project[2]])
    second_set = catenate(
        [self_output.T, cross_query, cross_memory[0], cross_memory[1], cross_output.T]
    )
    w_self = comm.gather_first(first_set)
    w_cross = comm.gather_first(second_set)
    w_in = comm.gather_middle(feed_input)
    w_out = comm.gather_middle(feed_output.T)
    w_so, w_cq = w_cross[:, :cols], w_cross[:, cols : 2 * cols]
    w_cm, w_co = w_cross[:, 2 * cols : 4 * cols], w_cross[:, 4 * cols :]

    values0 = comm.arrange(frames.reshape(own_rows, width)).astype(F32)
    up = comm.arrange(upstream.reshape(own_rows, width))
    text = comm.arrange(text_states.reshape(clips * texts, width))
    up_all = comm.spread(up, clips)

    stats0 = norm_stats(values0)
    n1 = comm.spread(norm_apply(values0, stats0, gain[0], shift[0]), clips)
    qkv = comm.sequence(mm(n1, w_self).astype(BF), clips)
    q, k, v = qkv[..., :cols], qkv[..., cols : 2 * cols], qkv[..., 2 * cols :]
    att, log_total = attend(q, k, v)
    att = comm.unsequence(att)
    values1 = values0 + comm.sum_own(att, w_so, mm_t, clips)

    stats1 = norm_stats(values1)
    n2 = comm.spread(norm_apply(values1, stats1, gain[1], shift[1]), clips)
    cq = comm.clip_rows(mm(n2, w_cq).astype(BF), clips)
    memory = mm(text, w_cm).astype(BF).reshape(clips, texts, 2 * cols)
    ck, cv = memory[..., :cols], memory[..., cols:]
    cross, chances = cross_attend(cq, ck, cv)
    cross = comm.unclip_rows(cross)
    values2 = values1 + comm.sum_own(cross, w_co, mm_t, clips)

    stats2 = norm_stats(values2)
    n3 = comm.spread(norm_apply(values2, stats2, gain[2], shift[2]), clips)
    hidden, slope = gelu_pair(mm(n3, w_in))
    layer_out = (values2 + comm.sum_own(hidden, w_out, mm_t, clips)).astype(BF)
    layer_out = comm.restore(layer_out).reshape(clips, own_frames, width)

    def wgrad(left, right):
        return lambda rows, columns: mm_rows(left[:, rows], right[:, columns])

    def scatter(method, left, right):
        if type(comm) is Whole:
            return method(wgrad(left, right))
        return method(wgrad(left, right), right.shape[1])

    grad_out = scatter(comm.scatter_middle, up_all, hidden)
    pre_grad = (mm(up_all, w_out) * slope.astype(F32)).astype(BF)
    grad_in = scatter(comm.scatter_middle, n3, pre_grad)
    e3 = comm.sum_own(pre_grad, w_in, mm_t, clips)
    dv2, gain2, shift2 = norm_back(values2, stats2, gain[2], e3)
    r2 = up.astype(F32) + dv2
    r2_all = comm.spread(r2.astype(BF), clips)
    dco = comm.clip_rows(mm(r2_all, w_co).astype(BF), clips)
    dcq, dck, dcv = cross_attend_back(cq, ck, cv, chances, dco)
    dcq = comm.unclip_rows(dcq)
    dmem = jnp.concatenate([dck, dcv], axis=-1).reshape(clips * texts, 2 * cols)
    text_grad = comm.sum_all(mm_t(dmem, w_cm))
    e2 = comm.sum_own(dcq, w_cq, mm_t, clips)
    dv1, gain1, shift1 = norm_back(values1, stats1, gain[1], e2)
    r1 = r2 + dv1
    r1_all = comm.spread(r1.astype(BF), clips)
    grad_co = scatter(comm.scatter_last, r2_all, cross)
    grad_cq = scatter(comm.scatter_last, n2, dcq)
    grad_cm = scatter(comm.scatter_last, text, dmem)
    grad_so = scatter(comm.scatter_last, r1_all, att)
    datt = comm.sequence(mm(r1_all, w_so).astype(BF), clips)
    dq, dk, dvv = attend_back(q, k, v, log_total, datt)
    dqkv = comm.unsequence(jnp.concatenate([dq, dk, dvv], axis=-1))
    grad_self = scatter(comm.scatter_last, n1, dqkv)
    e1 = comm.sum_own(dqkv, w_self, mm_t, clips)
    dv0, gain0, shift0 = norm_back(values0, stats0, gain[0], e1)
    input_grad = comm.restore(r1 + dv0).reshape(clips, own_frames, width)
    text_grad = comm.restore(text_grad).reshape(clips, texts, width)
    packed = jnp.stack([gain0, gain1, gain2, shift0, shift1, shift2]).T
    packed = jnp.pad(packed, ((0, 0), (0, 250)))

    def norm_sums(rows, columns):
        return packed[rows, columns]

    if type(comm) is Whole:
        norm_grad = comm.scatter_last(norm_sums)
    else:
        norm_grad = comm.scatter_last(norm_sums, packed.shape[1])
    norm_grad = comm.sum_all(norm_grad[:, :8]).T
    return (
        layer_out,
        input_grad,
        text_grad,
        norm_grad[0:3],
        norm_grad[3:6],
        jnp.stack([grad_self[:, i * cols : (i + 1) * cols] for i in range(3)]),
        grad_so.T,
        grad_cq,
        jnp.stack([grad_cm[:, :cols], grad_cm[:, cols:]]),
        grad_co.T,
        grad_in,
        grad_out.T,
    )


def specs(dp, tensor):
    in_specs = (
        P(dp, tensor, None),
        P(dp, None, None),
        P(None, dp),
        P(None, dp),
        P(None, dp, tensor),
        P(tensor, dp),
        P(dp, tensor),
        P(None, dp, tensor),
        P(tensor, dp),
        P(dp, tensor),
        P(tensor, dp),
        P(dp, tensor, None),
    )
    out_specs = (
        P(dp, tensor, None),
        P(dp, tensor, None),
        P(dp, None, None),
        P(None, dp),
        P(None, dp),
        P(None, dp, tensor),
        P(tensor, dp),
        P(dp, tensor),
        P(None, dp, tensor),
        P(tensor, dp),
        P(dp, tensor),
        P(tensor, dp),
    )
    return in_specs, out_specs


def solution(mesh):
    if mesh.shape["dp"] == 16 and mesh.shape["tensor"] == 2:
        mesh = Mesh(mesh.devices.reshape(4, 2, 2, 2), ("z", "y", "x", "core"))
        in_specs, out_specs = specs(("z", "y", "x"), "core")

        def per_device(frames, *rest):
            return layer(Block(frames.shape[-1]), frames, *rest)
    else:
        in_specs, out_specs = specs("dp", "tensor")

        def per_device(frames, *rest):
            return layer(Whole("dp", "tensor"), frames, *rest)

    return jax.shard_map(
        per_device, mesh=mesh, in_specs=in_specs, out_specs=out_specs, check_vma=False
    )
```

```python
import math

import jax
import jax.numpy as jnp
from jax import lax
from jax.experimental import pallas as pl
from jax.experimental.pallas import tpu as pltpu
from jax.sharding import Mesh
from jax.sharding import PartitionSpec as P

HEAD_DIM = 64
EPS = 1e-05
BF = jnp.bfloat16
F32 = jnp.float32
SWAP = [(0, 1), (1, 0)]


def mm(left, right):
    return jnp.dot(left, right, preferred_element_type=F32)


def mm_t(left, right):
    return lax.dot_general(left, right, (((1,), (1,)), ((), ())), preferred_element_type=F32)


def mm_rows(left, right):
    return lax.dot_general(left, right, (((0,), (0,)), ((), ())), preferred_element_type=F32)


def norm_stats(values):
    mean = jnp.mean(values, axis=-1, keepdims=True)
    centred = values - mean
    inv = lax.rsqrt(jnp.mean(centred * centred, axis=-1, keepdims=True) + EPS)
    return mean, inv


def norm_apply(values, stats, gain, shift):
    return ((values - stats[0]) * stats[1] * gain + shift).astype(BF)


def norm_back(values, stats, gain, grad):
    xhat = (values - stats[0]) * stats[1]
    scaled = grad * gain
    part = jnp.mean(scaled, axis=-1, keepdims=True)
    cross = jnp.mean(scaled * xhat, axis=-1, keepdims=True)
    value_grad = (scaled - part - xhat * cross) * stats[1]
    return value_grad, jnp.sum(grad * xhat, axis=0), jnp.sum(grad, axis=0)


def gelu_pair(pre):
    phi = 0.5 * (1.0 + lax.erf(pre * (1.0 / math.sqrt(2.0))))
    dens = jnp.exp(-0.5 * pre * pre) * (1.0 / math.sqrt(2.0 * math.pi))
    return (pre * phi).astype(BF), (phi + pre * dens).astype(BF)


def heads(matrix):
    return matrix.reshape(*matrix.shape[:-1], matrix.shape[-1] // HEAD_DIM, HEAD_DIM)


def flat(matrix):
    return matrix.reshape(*matrix.shape[:-2], -1)


SCALE = 1.0 / math.sqrt(HEAD_DIM)


def causal_scores(q, k):
    scores = jnp.einsum("bqhd,bkhd->bhqk", heads(q), heads(k), preferred_element_type=F32) * SCALE
    n = q.shape[1]
    allowed = jnp.arange(n)[None, :] <= jnp.arange(n)[:, None]
    return jnp.where(allowed, scores, -1e30)


def attend(q, k, v):
    scores = causal_scores(q, k)
    top = jnp.max(scores, axis=-1, keepdims=True)
    terms = jnp.exp(scores - top)
    total = jnp.sum(terms, axis=-1, keepdims=True)
    out = jnp.einsum(
        "bhqk,bkhd->bqhd", (terms / total).astype(BF), heads(v), preferred_element_type=F32
    )
    return flat(out).astype(BF), top + jnp.log(total)


def probs_back(chances, dp, q, k, grad):
    dot = jnp.sum(chances * dp, axis=-1, keepdims=True)
    ds = (chances * (dp - dot)).astype(BF)
    dv = jnp.einsum("bhqk,bqhd->bkhd", chances.astype(BF), grad, preferred_element_type=F32)
    dq = jnp.einsum("bhqk,bkhd->bqhd", ds, heads(k), preferred_element_type=F32) * SCALE
    dk = jnp.einsum("bhqk,bqhd->bkhd", ds, heads(q), preferred_element_type=F32) * SCALE
    return flat(dq).astype(BF), flat(dk).astype(BF), flat(dv).astype(BF)


def attend_back(q, k, v, log_total, grad):
    chances = jnp.exp(causal_scores(q, k) - log_total)
    grad = heads(grad)
    dp = jnp.einsum("bqhd,bkhd->bhqk", grad, heads(v), preferred_element_type=F32)
    return probs_back(chances, dp, q, k, grad)


def cross_attend(q, k, v):
    scores = jnp.einsum("bqhd,bkhd->bhqk", heads(q), heads(k), preferred_element_type=F32) * SCALE
    chances = jax.nn.softmax(scores, axis=-1)
    out = jnp.einsum("bhqk,bkhd->bqhd", chances.astype(BF), heads(v), preferred_element_type=F32)
    return flat(out).astype(BF), chances


def cross_attend_back(q, k, v, chances, grad):
    grad = heads(grad)
    dp = jnp.einsum("bqhd,bkhd->bhqk", grad, heads(v), preferred_element_type=F32)
    return probs_back(chances, dp, q, k, grad)

ANY = pl.BlockSpec(memory_space=pl.ANY)
NEG = -1e30


def place_kernel(*refs, spots):
    sources, out, sems = refs[: len(spots)], refs[len(spots)], refs[len(spots) + 1]
    copies = []
    for i, (source, (row, col)) in enumerate(zip(sources, spots)):
        rows, cols = source.shape
        copies.append(
            pltpu.make_async_copy(
                source, out.at[pl.ds(row, rows), pl.ds(col, cols)], sems.at[i]
            )
        )
    for copy in copies:
        copy.start()
    for copy in copies:
        copy.wait()


def place(pieces, shape):
    spots = tuple((row, col) for _, row, col in pieces)
    return pl.pallas_call(
        lambda *refs: place_kernel(*refs, spots=spots),
        out_shape=jax.ShapeDtypeStruct(shape, pieces[0][0].dtype),
        in_specs=[ANY] * len(pieces),
        out_specs=ANY,
        scratch_shapes=[pltpu.SemaphoreType.DMA((len(pieces),))],
        name="place",
    )(*[piece for piece, _, _ in pieces])


def place_stacked_kernel(four, far_a, far_b, out, sems):
    n, half = four.shape[0] // 4, four.shape[1]
    spots = [
        (four, 0, 2 * n, 0, 0),
        (far_a, 0, 2 * n, 2 * n, 0),
        (four, 2 * n, n, 0, half),
        (far_b, 0, n, n, half),
        (four, 3 * n, n, 2 * n, half),
        (far_b, n, n, 3 * n, half),
    ]
    copies = [
        pltpu.make_async_copy(
            source.at[pl.ds(start, rows)], out.at[pl.ds(row, rows), pl.ds(col, half)], sems.at[i]
        )
        for i, (source, start, rows, row, col) in enumerate(spots)
    ]
    for copy in copies:
        copy.start()
    for copy in copies:
        copy.wait()


def place_stacked(four, far_a, far_b):
    return pl.pallas_call(
        place_stacked_kernel,
        out_shape=jax.ShapeDtypeStruct((four.shape[0], 2 * four.shape[1]), four.dtype),
        in_specs=[ANY] * 3,
        out_specs=ANY,
        scratch_shapes=[pltpu.SemaphoreType.DMA((6,))],
        name="place_stacked",
    )(four, far_a, far_b)


def rows_of(matrix, grad):
    return lax.dot_general(matrix, grad, (((0,), (0,)), ((), ())), preferred_element_type=F32)


def head_of(ref, half, head):
    return ref[half, 0, :, head * HEAD_DIM : (head + 1) * HEAD_DIM]


def masked(scores):
    n = scores.shape[0]
    rows = lax.broadcasted_iota(jnp.int32, (n, n), 0)
    cols = lax.broadcasted_iota(jnp.int32, (n, n), 1)
    return jnp.where(cols <= rows, scores, NEG)


def self_kernel(core_ref, q_ref, k_ref, v_ref, out_ref, log_ref):
    halves = (core_ref[0], 1 - core_ref[0])
    outs, logs = ([], []), ([], [])
    for head in range(2):
        q = [head_of(q_ref, h, head) * BF(SCALE) for h in halves]
        k = [head_of(k_ref, h, head) for h in halves]
        v = [head_of(v_ref, h, head) for h in halves]
        first = masked(mm_t(q[0], k[0]))
        for half, scores in enumerate([[first], [mm_t(q[1], k[0]), masked(mm_t(q[1], k[1]))]]):
            top = jnp.max(scores[0], axis=-1, keepdims=True)
            if half:
                top = jnp.maximum(top, jnp.max(scores[1], axis=-1, keepdims=True))
            terms = [jnp.exp(part - top) for part in scores]
            total = sum(jnp.sum(part, axis=-1, keepdims=True) for part in terms)
            inverse = 1.0 / total
            out = sum(mm((part * inverse).astype(BF), v[i]) for i, part in enumerate(terms))
            outs[half].append(out.astype(BF))
            logs[half].append(jnp.broadcast_to(top + jnp.log(total), out.shape))
    for half, h in enumerate(halves):
        out_ref[h, 0] = jnp.concatenate(outs[half], axis=1)
        log_ref[h, 0] = jnp.concatenate(logs[half], axis=1)


def self_back_kernel(core_ref, q_ref, k_ref, v_ref, log_ref, grad_ref, out_ref):
    halves = (core_ref[0], 1 - core_ref[0])
    found = [[], [], [], [], [], []]
    for head in range(2):
        q = [head_of(q_ref, h, head) * BF(SCALE) for h in halves]
        k = [head_of(k_ref, h, head) for h in halves]
        ks = [part * BF(SCALE) for part in k]
        v = [head_of(v_ref, h, head) for h in halves]
        log = [head_of(log_ref, h, head)[:, :1] for h in halves]
        grad = [head_of(grad_ref, h, head) for h in halves]
        dq, dk, dv = [0.0, 0.0], [0.0, 0.0], [0.0, 0.0]
        for half, parts in enumerate([(0,), (0, 1)]):
            chances, dps = [], []
            for i in parts:
                scores = mm_t(q[half], k[i])
                if i == half:
                    scores = masked(scores)
                chances.append(jnp.exp(scores - log[half]))
                dps.append(mm_t(grad[half], v[i]))
            dot = sum(
                jnp.sum(c * dp, axis=-1, keepdims=True) for c, dp in zip(chances, dps)
            )
            for i, c, dp in zip(parts, chances, dps):
                ds = (c * (dp - dot)).astype(BF)
                dv[i] += rows_of(c.astype(BF), grad[half])
                dk[i] += rows_of(ds, q[half])
                dq[half] += mm(ds, ks[i])
        for i, part in enumerate(dq + dk + dv):
            found[i].append(part.astype(BF))
    width = out_ref.shape[-1] // 3
    for i in range(3):
        col = pl.multiple_of(i * width + pl.program_id(1) * 2 * HEAD_DIM, 2 * HEAD_DIM)
        for half, h in enumerate(halves):
            out_ref[h, 0, :, pl.ds(col, 2 * HEAD_DIM)] = jnp.concatenate(
                found[2 * i + half], axis=1
            )


def cross_parts(q_ref, k_ref, head):
    cs = slice(head * HEAD_DIM, (head + 1) * HEAD_DIM)
    q = jnp.concatenate([q_ref[0, 0, :, cs], q_ref[1, 0, :, cs]]) * BF(SCALE)
    scores = mm_t(q, k_ref[0, :, cs])
    terms = jnp.exp(scores - jnp.max(scores, axis=-1, keepdims=True))
    return q, terms * (1.0 / jnp.sum(terms, axis=-1, keepdims=True)), cs


def cross_kernel(q_ref, k_ref, v_ref, out_ref):
    outs = []
    for head in range(2):
        _, chances, cs = cross_parts(q_ref, k_ref, head)
        outs.append(mm(chances.astype(BF), v_ref[0, :, cs]).astype(BF))
    out = jnp.concatenate(outs, axis=1)
    n = out.shape[0] // 2
    out_ref[0, 0], out_ref[1, 0] = out[:n], out[n:]


def cross_back_kernel(q_ref, k_ref, v_ref, grad_ref, dq_ref, dkv_ref):
    found = [[], [], []]
    for head in range(2):
        q, chances, cs = cross_parts(q_ref, k_ref, head)
        grad = jnp.concatenate([grad_ref[0, 0, :, cs], grad_ref[1, 0, :, cs]])
        dp = mm_t(grad, v_ref[0, :, cs])
        ds = (chances * (dp - jnp.sum(chances * dp, axis=-1, keepdims=True))).astype(BF)
        found[0].append(mm(ds, k_ref[0, :, cs] * BF(SCALE)).astype(BF))
        found[1].append(rows_of(ds, q).astype(BF))
        found[2].append(rows_of(chances.astype(BF), grad).astype(BF))
    dq, dk, dv = [jnp.concatenate(parts, axis=1) for parts in found]
    n = dq.shape[0] // 2
    dq_ref[0, 0], dq_ref[1, 0] = dq[:n], dq[n:]
    width = dkv_ref.shape[-1] // 2
    for i, part in enumerate([dk, dv]):
        col = pl.multiple_of(i * width + pl.program_id(1) * 2 * HEAD_DIM, 2 * HEAD_DIM)
        dkv_ref[0, :, pl.ds(col, 2 * HEAD_DIM)] = part


def feed_kernel(rows_ref, weight_ref, hidden_ref, slope_ref):
    step = 256

    def body(i, carry):
        at = pl.ds(pl.multiple_of(i * step, step), step)
        hidden_ref[at], slope_ref[at] = gelu_pair(mm(rows_ref[at], weight_ref[...]))
        return carry

    lax.fori_loop(0, rows_ref.shape[0] // step, body, 0, unroll=True)


def feed(rows, weight):
    count, depth = rows.shape
    width = weight.shape[1]
    block = 256
    out = jax.ShapeDtypeStruct((count, width), BF)
    return pl.pallas_call(
        feed_kernel,
        grid=(width // block,),
        in_specs=[
            pl.BlockSpec((count, depth), lambda j: (0, 0)),
            pl.BlockSpec((depth, block), lambda j: (0, j)),
        ],
        out_specs=[pl.BlockSpec((count, block), lambda j: (0, j))] * 2,
        out_shape=[out, out],
        cost_estimate=pl.CostEstimate(
            flops=2 * count * depth * width,
            transcendentals=2 * count * width,
            bytes_accessed=2 * (count * depth + depth * width + 2 * count * width),
        ),
        name="feed",
    )(rows, weight)


class Whole:
    def __init__(self, dp, tensor):
        self.dp, self.tensor = dp, tensor

    def arrange(self, values):
        return values

    def restore(self, values):
        return values

    def gather_norms(self, packed):
        return lax.all_gather(packed, self.dp, axis=0, tiled=True)

    def gather_first(self, shard):
        return lax.all_gather(shard, self.dp, axis=0, tiled=True)

    gather_middle = gather_first

    def scatter_last(self, make):
        whole = make(slice(None), slice(None)).astype(BF)
        return lax.psum_scatter(whole, self.dp, scatter_dimension=0, tiled=True).astype(F32)

    scatter_middle = scatter_last

    def spread(self, rows, clips):
        local = rows.reshape(clips, -1, rows.shape[-1])
        return lax.all_gather(local, self.tensor, axis=1, tiled=True).reshape(-1, rows.shape[-1])

    def sequence(self, rows, clips):
        return rows.reshape(clips, -1, rows.shape[-1])

    def unsequence(self, rows):
        return rows.reshape(-1, rows.shape[-1])

    def clip_rows(self, rows, clips):
        return rows.reshape(clips, -1, rows.shape[-1])

    unclip_rows = unsequence

    def self_attend(self, qkv, clips):
        qkv = self.sequence(qkv, clips)
        cols = qkv.shape[-1] // 3
        q, k, v = qkv[..., :cols], qkv[..., cols : 2 * cols], qkv[..., 2 * cols :]
        att, log_total = attend(q, k, v)
        return self.unsequence(att), (q, k, v, log_total)

    def self_back(self, saved, grad, clips):
        dq, dk, dv = attend_back(*saved, self.sequence(grad, clips))
        return self.unsequence(jnp.concatenate([dq, dk, dv], axis=-1))

    def cross_attend(self, q, memory, clips):
        q = self.clip_rows(q, clips)
        memory = memory.reshape(clips, -1, memory.shape[-1])
        cols = q.shape[-1]
        k, v = memory[..., :cols], memory[..., cols:]
        out, chances = cross_attend(q, k, v)
        return self.unclip_rows(out), (q, k, v, chances)

    def cross_back(self, saved, grad, clips):
        dq, dk, dv = cross_attend_back(*saved, self.clip_rows(grad, clips))
        return self.unclip_rows(dq), self.unsequence(jnp.concatenate([dk, dv], axis=-1))

    def feed(self, rows, weight):
        return gelu_pair(mm(rows, weight))

    def sum_own(self, left, right, product, clips):
        part = product(left, right).astype(BF).reshape(clips, -1, right_width(product, right))
        own = lax.psum_scatter(part, self.tensor, scatter_dimension=1, tiled=True)
        return own.reshape(-1, part.shape[-1]).astype(F32)

    def sum_all(self, values):
        return lax.psum(values.astype(BF), self.tensor).astype(F32)


def right_width(product, right):
    return right.shape[0] if product is mm_t else right.shape[1]


class Block(Whole):
    def __init__(self, width):
        self.width = width
        self.shard = width // 16
        self.core = lax.axis_index("core")

    def order(self):
        own_y, own_x = lax.axis_index("y"), lax.axis_index("x")
        place = jnp.arange(self.width, dtype=jnp.int32)
        quarter, rest = place // (4 * self.shard), place % (4 * self.shard)
        z, row = rest // self.shard, rest % self.shard
        y, x = (quarter // 2) ^ own_y, (quarter % 2) ^ own_x
        source = ((z * 2 + y) * 2 + x) * self.shard + row
        return (jnp.arange(self.width, dtype=jnp.int32)[:, None] == source[None, :]).astype(BF)

    def arrange(self, values):
        return mm(values, self.order()).astype(BF)

    def restore(self, values):
        if values.dtype == BF:
            return mm_t(values, self.order()).astype(BF)
        high = lax.reduce_precision(values, 8, 7)
        low = (values - high).astype(BF)
        order = self.order()
        return mm_t(high.astype(BF), order) + mm_t(low, order)

    def x(self, v):
        return lax.ppermute(v, "x", SWAP)

    def y(self, v):
        return lax.ppermute(v, "y", SWAP)

    def other(self, v):
        return lax.ppermute(v, "core", SWAP)

    def gather_norms(self, packed):
        pair = jnp.stack([packed, lax.ppermute(packed, "z", [(0, 1), (1, 0), (2, 3), (3, 2)])])
        far = lax.ppermute(pair, "z", [(0, 2), (1, 3), (2, 0), (3, 1)])
        own = lax.axis_index("z")
        four = jnp.concatenate([pair, far])
        four = jnp.stack([lax.dynamic_index_in_dim(four, own ^ p, 0, False) for p in range(4)])
        two = jnp.stack([four, self.x(four)])
        whole = jnp.stack([two, self.y(two)])
        return whole.reshape(self.width, packed.shape[-1])

    def halves(self, shard):
        half = shard.shape[1] // 256 * 128
        return shard[:, :half], shard[:, half:]

    def gather_first(self, shard):
        four = lax.all_gather(shard, "z", axis=0, tiled=True)
        a, b = self.halves(four)
        n, half = a.shape
        xa, yb, ya, xb = self.x(a), self.y(b), self.y(a), self.x(b)
        far_a, far_b = self.y(xa), self.x(yb)
        return place(
            [
                (four, 0, 0),
                (xa, n, 0),
                (ya, 2 * n, 0),
                (far_a, 3 * n, 0),
                (xb, n, half),
                (yb, 2 * n, half),
                (far_b, 3 * n, half),
            ],
            (4 * n, shard.shape[1]),
        )

    def gather_middle(self, shard):
        a, b = self.halves(shard)
        four = jnp.stack([a, self.x(a), b, self.y(b)])
        four = lax.all_gather(four, "z", axis=1, tiled=True)
        _, n, half = four.shape
        far_a, far_b = self.y(four[:2]), self.x(four[2:])
        four = four.reshape(4 * n, half)
        far_a, far_b = far_a.reshape(2 * n, half), far_b.reshape(2 * n, half)
        return place_stacked(four, far_a, far_b)

    def scatter_open(self, make, columns):
        n = self.width // 4
        half = columns // 256 * 128
        left, right = slice(0, half), slice(half, columns)
        far_left = self.y(make(slice(2 * n, 4 * n), left).astype(BF))
        far_right = self.x(
            jnp.concatenate(
                [make(slice(n, 2 * n), right).astype(BF), make(slice(3 * n, 4 * n), right).astype(BF)]
            )
        )
        a = (make(slice(0, 2 * n), left) + far_left.astype(F32)).astype(BF)
        b = [
            (make(slice(0, n), right) + far_right[:n].astype(F32)).astype(BF),
            (make(slice(2 * n, 3 * n), right) + far_right[n:].astype(F32)).astype(BF),
        ]
        return a[:n], a[n:], b[0], b[1]

    def scatter_middle(self, make, columns):
        four = jnp.stack(self.scatter_open(make, columns))
        four = lax.psum_scatter(four, "z", scatter_dimension=1, tiled=True)
        left = four[0].astype(F32) + self.x(four[1]).astype(F32)
        right = four[2].astype(F32) + self.y(four[3]).astype(F32)
        return jnp.concatenate([left, right], axis=1)

    def scatter_last(self, make, columns):
        a0, a1, b0, b1 = self.scatter_open(make, columns)
        far_a, far_b = self.x(a1), self.y(b1)
        both = jnp.stack(
            [
                (a0.astype(F32) + far_a.astype(F32)).astype(BF),
                (b0.astype(F32) + far_b.astype(F32)).astype(BF),
            ]
        )
        both = lax.psum_scatter(both, "z", scatter_dimension=1, tiled=True).astype(F32)
        return jnp.concatenate([both[0], both[1]], axis=1)

    def spread(self, rows, clips):
        return jnp.concatenate([rows, self.other(rows)])

    def self_attend(self, qkv, clips):
        cols = qkv.shape[-1] // 3
        steps = cols // (2 * HEAD_DIM)
        view = qkv.reshape(2, clips, -1, qkv.shape[-1])
        frames = view.shape[2]

        def block(part):
            return pl.BlockSpec(
                (2, 1, frames, 2 * HEAD_DIM), lambda c, j, _: (0, c, 0, part * steps + j)
            )

        shape = (2, clips, frames, cols)
        core = self.core.reshape(1).astype(jnp.int32)
        scores = clips * steps * 2 * 3 * frames * frames
        out, log_total = pl.pallas_call(
            self_kernel,
            grid_spec=pltpu.PrefetchScalarGridSpec(
                num_scalar_prefetch=1,
                grid=(clips, steps),
                in_specs=[block(0), block(1), block(2)],
                out_specs=[block(0), block(0)],
            ),
            out_shape=[jax.ShapeDtypeStruct(shape, BF), jax.ShapeDtypeStruct(shape, F32)],
            cost_estimate=pl.CostEstimate(
                flops=4 * scores * HEAD_DIM,
                transcendentals=scores,
                bytes_accessed=2 * qkv.size + 6 * qkv.size // 3,
            ),
            name="self_attend",
        )(core, view, view, view)
        return out.reshape(-1, cols), (core, view, log_total)

    def self_back(self, saved, grad, clips):
        core, view, log_total = saved
        cols = view.shape[-1] // 3
        steps = cols // (2 * HEAD_DIM)
        frames = view.shape[2]

        def block(part):
            return pl.BlockSpec(
                (2, 1, frames, 2 * HEAD_DIM), lambda c, j, _: (0, c, 0, part * steps + j)
            )

        scores = clips * steps * 2 * 3 * frames * frames
        out = pl.pallas_call(
            self_back_kernel,
            grid_spec=pltpu.PrefetchScalarGridSpec(
                num_scalar_prefetch=1,
                grid=(clips, steps),
                in_specs=[block(0), block(1), block(2), block(0), block(0)],
                out_specs=pl.BlockSpec((2, 1, frames, 3 * cols), lambda c, j, _: (0, c, 0, 0)),
            ),
            out_shape=jax.ShapeDtypeStruct(view.shape, BF),
            cost_estimate=pl.CostEstimate(
                flops=10 * scores * HEAD_DIM,
                transcendentals=scores,
                bytes_accessed=4 * view.size + 6 * view.size // 3,
            ),
            name="self_back",
        )(core, view, view, view, log_total, grad.reshape(2, clips, frames, cols))
        return out.reshape(-1, 3 * cols)

    def cross_specs(self, q, clips, texts):
        cols = q.shape[-1]
        steps = cols // (2 * HEAD_DIM)
        view = q.reshape(2, clips, -1, cols)
        frames = view.shape[2]
        wide = pl.BlockSpec((2, 1, frames, 2 * HEAD_DIM), lambda c, j: (0, c, 0, j))

        def block(part):
            return pl.BlockSpec((1, texts, 2 * HEAD_DIM), lambda c, j: (c, 0, part * steps + j))

        return view, (clips, steps), wide, block, clips * 2 * frames * cols * texts

    def cross_attend(self, q, memory, clips):
        memory = memory.reshape(clips, -1, memory.shape[-1])
        view, grid, wide, block, work = self.cross_specs(q, clips, memory.shape[1])
        out = pl.pallas_call(
            cross_kernel,
            grid=grid,
            in_specs=[wide, block(0), block(1)],
            out_specs=wide,
            out_shape=jax.ShapeDtypeStruct(view.shape, BF),
            cost_estimate=pl.CostEstimate(
                flops=4 * work, transcendentals=work // HEAD_DIM, bytes_accessed=4 * q.size
            ),
            name="cross_attend",
        )(view, memory, memory)
        return out.reshape(q.shape), (q, memory)

    def cross_back(self, saved, grad, clips):
        q, memory = saved
        texts = memory.shape[1]
        view, grid, wide, block, work = self.cross_specs(q, clips, texts)
        dq, dkv = pl.pallas_call(
            cross_back_kernel,
            grid=grid,
            in_specs=[wide, block(0), block(1), wide],
            out_specs=[
                wide,
                pl.BlockSpec((1, texts, memory.shape[-1]), lambda c, j: (c, 0, 0)),
            ],
            out_shape=[
                jax.ShapeDtypeStruct(view.shape, BF),
                jax.ShapeDtypeStruct(memory.shape, BF),
            ],
            cost_estimate=pl.CostEstimate(
                flops=10 * work, transcendentals=work // HEAD_DIM, bytes_accessed=6 * q.size
            ),
            name="cross_back",
        )(view, memory, memory, grad.reshape(view.shape))
        return dq.reshape(q.shape), dkv.reshape(-1, memory.shape[-1])

    def feed(self, rows, weight):
        return feed(rows, weight)

    def sum_own(self, left, right, product, clips):
        n = left.shape[0] // 2
        far = self.other(product(left[n:], right).astype(BF))
        return product(left[:n], right) + far.astype(F32)

    def sum_all(self, values):
        return values + self.other(values.astype(BF)).astype(F32)


def layer(
    comm,
    frames,
    text_states,
    norm_gain,
    norm_shift,
    self_project,
    self_output,
    cross_query,
    cross_memory,
    cross_output,
    feed_input,
    feed_output,
    upstream,
):
    clips, own_frames, width = frames.shape
    texts = text_states.shape[1]
    cols = cross_query.shape[1]
    own_rows = clips * own_frames

    def catenate(parts):
        return jnp.concatenate(parts, axis=1)

    norms = comm.gather_norms(
        jnp.pad(jnp.concatenate([norm_gain, norm_shift]).T, ((0, 0), (0, 122)))
    )
    norms = norms.T.astype(F32)
    gain, shift = norms[0:3], norms[3:6]
    first_set = catenate([self_project[0], self_project[1], self_project[2]])
    second_set = catenate(
        [self_output.T, cross_query, cross_memory[0], cross_memory[1], cross_output.T]
    )
    w_self = comm.gather_first(first_set)
    w_cross = comm.gather_first(second_set)
    w_in = comm.gather_middle(feed_input)
    w_out = comm.gather_middle(feed_output.T)
    w_so, w_cq = w_cross[:, :cols], w_cross[:, cols : 2 * cols]
    w_cm, w_co = w_cross[:, 2 * cols : 4 * cols], w_cross[:, 4 * cols :]

    values0 = comm.arrange(frames.reshape(own_rows, width)).astype(F32)
    up = comm.arrange(upstream.reshape(own_rows, width))
    text = comm.arrange(text_states.reshape(clips * texts, width))
    up_all = comm.spread(up, clips)

    stats0 = norm_stats(values0)
    n1 = comm.spread(norm_apply(values0, stats0, gain[0], shift[0]), clips)
    att, self_saved = comm.self_attend(mm(n1, w_self).astype(BF), clips)
    values1 = values0 + comm.sum_own(att, w_so, mm_t, clips)

    stats1 = norm_stats(values1)
    n2 = comm.spread(norm_apply(values1, stats1, gain[1], shift[1]), clips)
    cross, cross_saved = comm.cross_attend(
        mm(n2, w_cq).astype(BF), mm(text, w_cm).astype(BF), clips
    )
    values2 = values1 + comm.sum_own(cross, w_co, mm_t, clips)

    stats2 = norm_stats(values2)
    n3 = comm.spread(norm_apply(values2, stats2, gain[2], shift[2]), clips)
    hidden, slope = comm.feed(n3, w_in)
    layer_out = (values2 + comm.sum_own(hidden, w_out, mm_t, clips)).astype(BF)
    layer_out = comm.restore(layer_out).reshape(clips, own_frames, width)

    def wgrad(left, right):
        return lambda rows, columns: mm_rows(left[:, rows], right[:, columns])

    def scatter(method, left, right):
        if type(comm) is Whole:
            return method(wgrad(left, right))
        return method(wgrad(left, right), right.shape[1])

    grad_out = scatter(comm.scatter_middle, up_all, hidden)
    pre_grad = (mm(up_all, w_out) * slope.astype(F32)).astype(BF)
    grad_in = scatter(comm.scatter_middle, n3, pre_grad)
    e3 = comm.sum_own(pre_grad, w_in, mm_t, clips)
    dv2, gain2, shift2 = norm_back(values2, stats2, gain[2], e3)
    r2 = up.astype(F32) + dv2
    r2_all = comm.spread(r2.astype(BF), clips)
    dcq, dmem = comm.cross_back(cross_saved, mm(r2_all, w_co).astype(BF), clips)
    text_grad = comm.sum_all(mm_t(dmem, w_cm))
    e2 = comm.sum_own(dcq, w_cq, mm_t, clips)
    dv1, gain1, shift1 = norm_back(values1, stats1, gain[1], e2)
    r1 = r2 + dv1
    r1_all = comm.spread(r1.astype(BF), clips)
    grad_co = scatter(comm.scatter_last, r2_all, cross)
    grad_cq = scatter(comm.scatter_last, n2, dcq)
    grad_cm = scatter(comm.scatter_last, text, dmem)
    grad_so = scatter(comm.scatter_last, r1_all, att)
    dqkv = comm.self_back(self_saved, mm(r1_all, w_so).astype(BF), clips)
    grad_self = scatter(comm.scatter_last, n1, dqkv)
    e1 = comm.sum_own(dqkv, w_self, mm_t, clips)
    dv0, gain0, shift0 = norm_back(values0, stats0, gain[0], e1)
    input_grad = comm.restore(r1 + dv0).reshape(clips, own_frames, width)
    text_grad = comm.restore(text_grad).reshape(clips, texts, width)
    packed = jnp.stack([gain0, gain1, gain2, shift0, shift1, shift2]).T
    packed = jnp.pad(packed, ((0, 0), (0, 250)))

    def norm_sums(rows, columns):
        return packed[rows, columns]

    if type(comm) is Whole:
        norm_grad = comm.scatter_last(norm_sums)
    else:
        norm_grad = comm.scatter_last(norm_sums, packed.shape[1])
    norm_grad = comm.sum_all(norm_grad[:, :8]).T
    return (
        layer_out,
        input_grad,
        text_grad,
        norm_grad[0:3],
        norm_grad[3:6],
        jnp.stack([grad_self[:, i * cols : (i + 1) * cols] for i in range(3)]),
        grad_so.T,
        grad_cq,
        jnp.stack([grad_cm[:, :cols], grad_cm[:, cols:]]),
        grad_co.T,
        grad_in,
        grad_out.T,
    )


def specs(dp, tensor):
    in_specs = (
        P(dp, tensor, None),
        P(dp, None, None),
        P(None, dp),
        P(None, dp),
        P(None, dp, tensor),
        P(tensor, dp),
        P(dp, tensor),
        P(None, dp, tensor),
        P(tensor, dp),
        P(dp, tensor),
        P(tensor, dp),
        P(dp, tensor, None),
    )
    out_specs = (
        P(dp, tensor, None),
        P(dp, tensor, None),
        P(dp, None, None),
        P(None, dp),
        P(None, dp),
        P(None, dp, tensor),
        P(tensor, dp),
        P(dp, tensor),
        P(None, dp, tensor),
        P(tensor, dp),
        P(dp, tensor),
        P(tensor, dp),
    )
    return in_specs, out_specs


def solution(mesh):
    if mesh.shape["dp"] == 16 and mesh.shape["tensor"] == 2:
        mesh = Mesh(mesh.devices.reshape(4, 2, 2, 2), ("z", "y", "x", "core"))
        in_specs, out_specs = specs(("z", "y", "x"), "core")

        def per_device(frames, *rest):
            return layer(Block(frames.shape[-1]), frames, *rest)
    else:
        in_specs, out_specs = specs("dp", "tensor")

        def per_device(frames, *rest):
            return layer(Whole("dp", "tensor"), frames, *rest)

    return jax.shard_map(
        per_device, mesh=mesh, in_specs=in_specs, out_specs=out_specs, check_vma=False
    )
```

```python
import math

import jax
import jax.numpy as jnp
from jax import lax
from jax.experimental import pallas as pl
from jax.experimental.pallas import tpu as pltpu
from jax.sharding import Mesh
from jax.sharding import PartitionSpec as P

HEAD_DIM = 64
EPS = 1e-05
BF = jnp.bfloat16
F32 = jnp.float32
SWAP = [(0, 1), (1, 0)]


def mm(left, right):
    return jnp.dot(left, right, preferred_element_type=F32)


def mm_t(left, right):
    return lax.dot_general(left, right, (((1,), (1,)), ((), ())), preferred_element_type=F32)


def mm_rows(left, right):
    return lax.dot_general(left, right, (((0,), (0,)), ((), ())), preferred_element_type=F32)


def norm_stats(values):
    mean = jnp.mean(values, axis=-1, keepdims=True)
    centred = values - mean
    inv = lax.rsqrt(jnp.mean(centred * centred, axis=-1, keepdims=True) + EPS)
    return mean, inv


def norm_apply(values, stats, gain, shift):
    return ((values - stats[0]) * stats[1] * gain + shift).astype(BF)


def norm_back(values, stats, gain, grad):
    xhat = (values - stats[0]) * stats[1]
    scaled = grad * gain
    part = jnp.mean(scaled, axis=-1, keepdims=True)
    cross = jnp.mean(scaled * xhat, axis=-1, keepdims=True)
    value_grad = (scaled - part - xhat * cross) * stats[1]
    return value_grad, jnp.sum(grad * xhat, axis=0), jnp.sum(grad, axis=0)


def gelu_pair(pre):
    phi = 0.5 * (1.0 + lax.erf(pre * (1.0 / math.sqrt(2.0))))
    dens = jnp.exp(-0.5 * pre * pre) * (1.0 / math.sqrt(2.0 * math.pi))
    return (pre * phi).astype(BF), (phi + pre * dens).astype(BF)


def heads(matrix):
    return matrix.reshape(*matrix.shape[:-1], matrix.shape[-1] // HEAD_DIM, HEAD_DIM)


def flat(matrix):
    return matrix.reshape(*matrix.shape[:-2], -1)


SCALE = 1.0 / math.sqrt(HEAD_DIM)


def causal_scores(q, k):
    scores = jnp.einsum("bqhd,bkhd->bhqk", heads(q), heads(k), preferred_element_type=F32) * SCALE
    n = q.shape[1]
    allowed = jnp.arange(n)[None, :] <= jnp.arange(n)[:, None]
    return jnp.where(allowed, scores, -1e30)


def attend(q, k, v):
    scores = causal_scores(q, k)
    top = jnp.max(scores, axis=-1, keepdims=True)
    terms = jnp.exp(scores - top)
    total = jnp.sum(terms, axis=-1, keepdims=True)
    out = jnp.einsum(
        "bhqk,bkhd->bqhd", (terms / total).astype(BF), heads(v), preferred_element_type=F32
    )
    return flat(out).astype(BF), top + jnp.log(total)


def probs_back(chances, dp, q, k, grad):
    dot = jnp.sum(chances * dp, axis=-1, keepdims=True)
    ds = (chances * (dp - dot)).astype(BF)
    dv = jnp.einsum("bhqk,bqhd->bkhd", chances.astype(BF), grad, preferred_element_type=F32)
    dq = jnp.einsum("bhqk,bkhd->bqhd", ds, heads(k), preferred_element_type=F32) * SCALE
    dk = jnp.einsum("bhqk,bqhd->bkhd", ds, heads(q), preferred_element_type=F32) * SCALE
    return flat(dq).astype(BF), flat(dk).astype(BF), flat(dv).astype(BF)


def attend_back(q, k, v, log_total, grad):
    chances = jnp.exp(causal_scores(q, k) - log_total)
    grad = heads(grad)
    dp = jnp.einsum("bqhd,bkhd->bhqk", grad, heads(v), preferred_element_type=F32)
    return probs_back(chances, dp, q, k, grad)


def cross_attend(q, k, v):
    scores = jnp.einsum("bqhd,bkhd->bhqk", heads(q), heads(k), preferred_element_type=F32) * SCALE
    chances = jax.nn.softmax(scores, axis=-1)
    out = jnp.einsum("bhqk,bkhd->bqhd", chances.astype(BF), heads(v), preferred_element_type=F32)
    return flat(out).astype(BF), chances


def cross_attend_back(q, k, v, chances, grad):
    grad = heads(grad)
    dp = jnp.einsum("bqhd,bkhd->bhqk", grad, heads(v), preferred_element_type=F32)
    return probs_back(chances, dp, q, k, grad)

ANY = pl.BlockSpec(memory_space=pl.ANY)
NEG = -1e30


def place_kernel(*refs, spots):
    sources, out, sems = refs[: len(spots)], refs[len(spots)], refs[len(spots) + 1]
    copies = []
    for i, (source, (row, col)) in enumerate(zip(sources, spots)):
        rows, cols = source.shape
        copies.append(
            pltpu.make_async_copy(
                source, out.at[pl.ds(row, rows), pl.ds(col, cols)], sems.at[i]
            )
        )
    for copy in copies:
        copy.start()
    for copy in copies:
        copy.wait()


def place(pieces, shape):
    spots = tuple((row, col) for _, row, col in pieces)
    return pl.pallas_call(
        lambda *refs: place_kernel(*refs, spots=spots),
        out_shape=jax.ShapeDtypeStruct(shape, pieces[0][0].dtype),
        in_specs=[ANY] * len(pieces),
        out_specs=pl.BlockSpec(memory_space=pltpu.VMEM),
        scratch_shapes=[pltpu.SemaphoreType.DMA((len(pieces),))],
        name="place",
    )(*[piece for piece, _, _ in pieces])


def place_stacked_kernel(four, far_a, far_b, out, sems):
    n, half = four.shape[0] // 4, four.shape[1]
    spots = [
        (four, 0, 2 * n, 0, 0),
        (far_a, 0, 2 * n, 2 * n, 0),
        (four, 2 * n, n, 0, half),
        (far_b, 0, n, n, half),
        (four, 3 * n, n, 2 * n, half),
        (far_b, n, n, 3 * n, half),
    ]
    copies = [
        pltpu.make_async_copy(
            source.at[pl.ds(start, rows)], out.at[pl.ds(row, rows), pl.ds(col, half)], sems.at[i]
        )
        for i, (source, start, rows, row, col) in enumerate(spots)
    ]
    for copy in copies:
        copy.start()
    for copy in copies:
        copy.wait()


def place_stacked(four, far_a, far_b):
    return pl.pallas_call(
        place_stacked_kernel,
        out_shape=jax.ShapeDtypeStruct((four.shape[0], 2 * four.shape[1]), four.dtype),
        in_specs=[ANY] * 3,
        out_specs=pl.BlockSpec(memory_space=pltpu.VMEM),
        scratch_shapes=[pltpu.SemaphoreType.DMA((6,))],
        name="place_stacked",
    )(four, far_a, far_b)


def rows_of(matrix, grad):
    return lax.dot_general(matrix, grad, (((0,), (0,)), ((), ())), preferred_element_type=F32)


def head_of(ref, half, head):
    return ref[half, 0, :, head * HEAD_DIM : (head + 1) * HEAD_DIM]


def masked(scores):
    n = scores.shape[0]
    rows = lax.broadcasted_iota(jnp.int32, (n, n), 0)
    cols = lax.broadcasted_iota(jnp.int32, (n, n), 1)
    return jnp.where(cols <= rows, scores, NEG)


def self_kernel(core_ref, q_ref, k_ref, v_ref, out_ref, log_ref):
    halves = (core_ref[0], 1 - core_ref[0])
    outs, logs = ([], []), ([], [])
    for head in range(2):
        q = [head_of(q_ref, h, head) * BF(SCALE) for h in halves]
        k = [head_of(k_ref, h, head) for h in halves]
        v = [head_of(v_ref, h, head) for h in halves]
        first = masked(mm_t(q[0], k[0]))
        for half, scores in enumerate([[first], [mm_t(q[1], k[0]), masked(mm_t(q[1], k[1]))]]):
            top = jnp.max(scores[0], axis=-1, keepdims=True)
            if half:
                top = jnp.maximum(top, jnp.max(scores[1], axis=-1, keepdims=True))
            terms = [jnp.exp(part - top) for part in scores]
            total = sum(jnp.sum(part, axis=-1, keepdims=True) for part in terms)
            inverse = 1.0 / total
            out = sum(mm((part * inverse).astype(BF), v[i]) for i, part in enumerate(terms))
            outs[half].append(out.astype(BF))
            logs[half].append(jnp.broadcast_to(top + jnp.log(total), out.shape))
    for half, h in enumerate(halves):
        out_ref[h, 0] = jnp.concatenate(outs[half], axis=1)
        log_ref[h, 0] = jnp.concatenate(logs[half], axis=1)


def self_back_kernel(core_ref, q_ref, k_ref, v_ref, log_ref, grad_ref, out_ref):
    halves = (core_ref[0], 1 - core_ref[0])
    found = [[], [], [], [], [], []]
    for head in range(2):
        q = [head_of(q_ref, h, head) * BF(SCALE) for h in halves]
        k = [head_of(k_ref, h, head) for h in halves]
        ks = [part * BF(SCALE) for part in k]
        v = [head_of(v_ref, h, head) for h in halves]
        log = [head_of(log_ref, h, head)[:, :1] for h in halves]
        grad = [head_of(grad_ref, h, head) for h in halves]
        dq, dk, dv = [0.0, 0.0], [0.0, 0.0], [0.0, 0.0]
        for half, parts in enumerate([(0,), (0, 1)]):
            chances, dps = [], []
            for i in parts:
                scores = mm_t(q[half], k[i])
                if i == half:
                    scores = masked(scores)
                chances.append(jnp.exp(scores - log[half]))
                dps.append(mm_t(grad[half], v[i]))
            dot = sum(
                jnp.sum(c * dp, axis=-1, keepdims=True) for c, dp in zip(chances, dps)
            )
            for i, c, dp in zip(parts, chances, dps):
                ds = (c * (dp - dot)).astype(BF)
                dv[i] += rows_of(c.astype(BF), grad[half])
                dk[i] += rows_of(ds, q[half])
                dq[half] += mm(ds, ks[i])
        for i, part in enumerate(dq + dk + dv):
            found[i].append(part.astype(BF))
    width = out_ref.shape[-1] // 3
    for i in range(3):
        col = pl.multiple_of(i * width + pl.program_id(1) * 2 * HEAD_DIM, 2 * HEAD_DIM)
        for half, h in enumerate(halves):
            out_ref[h, 0, :, pl.ds(col, 2 * HEAD_DIM)] = jnp.concatenate(
                found[2 * i + half], axis=1
            )


def cross_parts(q_ref, k_ref, head):
    cs = slice(head * HEAD_DIM, (head + 1) * HEAD_DIM)
    q = jnp.concatenate([q_ref[0, 0, :, cs], q_ref[1, 0, :, cs]]) * BF(SCALE)
    scores = mm_t(q, k_ref[0, :, cs])
    terms = jnp.exp(scores - jnp.max(scores, axis=-1, keepdims=True))
    return q, terms * (1.0 / jnp.sum(terms, axis=-1, keepdims=True)), cs


def cross_kernel(q_ref, k_ref, v_ref, out_ref):
    outs = []
    for head in range(2):
        _, chances, cs = cross_parts(q_ref, k_ref, head)
        outs.append(mm(chances.astype(BF), v_ref[0, :, cs]).astype(BF))
    out = jnp.concatenate(outs, axis=1)
    n = out.shape[0] // 2
    out_ref[0, 0], out_ref[1, 0] = out[:n], out[n:]


def cross_back_kernel(q_ref, k_ref, v_ref, grad_ref, dq_ref, dkv_ref):
    found = [[], [], []]
    for head in range(2):
        q, chances, cs = cross_parts(q_ref, k_ref, head)
        grad = jnp.concatenate([grad_ref[0, 0, :, cs], grad_ref[1, 0, :, cs]])
        dp = mm_t(grad, v_ref[0, :, cs])
        ds = (chances * (dp - jnp.sum(chances * dp, axis=-1, keepdims=True))).astype(BF)
        found[0].append(mm(ds, k_ref[0, :, cs] * BF(SCALE)).astype(BF))
        found[1].append(rows_of(ds, q).astype(BF))
        found[2].append(rows_of(chances.astype(BF), grad).astype(BF))
    dq, dk, dv = [jnp.concatenate(parts, axis=1) for parts in found]
    n = dq.shape[0] // 2
    dq_ref[0, 0], dq_ref[1, 0] = dq[:n], dq[n:]
    width = dkv_ref.shape[-1] // 2
    for i, part in enumerate([dk, dv]):
        col = pl.multiple_of(i * width + pl.program_id(1) * 2 * HEAD_DIM, 2 * HEAD_DIM)
        dkv_ref[0, :, pl.ds(col, 2 * HEAD_DIM)] = part


def feed_kernel(rows_ref, weight_ref, hidden_ref, slope_ref):
    step = 256

    def body(i, carry):
        at = pl.ds(pl.multiple_of(i * step, step), step)
        hidden_ref[at], slope_ref[at] = gelu_pair(mm(rows_ref[at], weight_ref[...]))
        return carry

    lax.fori_loop(0, rows_ref.shape[0] // step, body, 0, unroll=True)


def feed(rows, weight):
    count, depth = rows.shape
    width = weight.shape[1]
    block = 256
    out = jax.ShapeDtypeStruct((count, width), BF)
    return pl.pallas_call(
        feed_kernel,
        grid=(width // block,),
        in_specs=[
            pl.BlockSpec((count, depth), lambda j: (0, 0)),
            pl.BlockSpec((depth, block), lambda j: (0, j)),
        ],
        out_specs=[pl.BlockSpec((count, block), lambda j: (0, j))] * 2,
        out_shape=[out, out],
        cost_estimate=pl.CostEstimate(
            flops=2 * count * depth * width,
            transcendentals=2 * count * width,
            bytes_accessed=2 * (count * depth + depth * width + 2 * count * width),
        ),
        name="feed",
    )(rows, weight)


class Whole:
    def __init__(self, dp, tensor):
        self.dp, self.tensor = dp, tensor

    def arrange(self, values):
        return values

    def restore(self, values):
        return values

    def gather_norms(self, packed):
        return lax.all_gather(packed, self.dp, axis=0, tiled=True)

    def gather_first(self, shard):
        return lax.all_gather(shard, self.dp, axis=0, tiled=True)

    gather_middle = gather_first

    def scatter_last(self, make):
        whole = make(slice(None), slice(None)).astype(BF)
        return lax.psum_scatter(whole, self.dp, scatter_dimension=0, tiled=True).astype(F32)

    scatter_middle = scatter_last

    def spread(self, rows, clips):
        local = rows.reshape(clips, -1, rows.shape[-1])
        return lax.all_gather(local, self.tensor, axis=1, tiled=True).reshape(-1, rows.shape[-1])

    def sequence(self, rows, clips):
        return rows.reshape(clips, -1, rows.shape[-1])

    def unsequence(self, rows):
        return rows.reshape(-1, rows.shape[-1])

    def clip_rows(self, rows, clips):
        return rows.reshape(clips, -1, rows.shape[-1])

    unclip_rows = unsequence

    def self_attend(self, qkv, clips):
        qkv = self.sequence(qkv, clips)
        cols = qkv.shape[-1] // 3
        q, k, v = qkv[..., :cols], qkv[..., cols : 2 * cols], qkv[..., 2 * cols :]
        att, log_total = attend(q, k, v)
        return self.unsequence(att), (q, k, v, log_total)

    def self_back(self, saved, grad, clips):
        dq, dk, dv = attend_back(*saved, self.sequence(grad, clips))
        return self.unsequence(jnp.concatenate([dq, dk, dv], axis=-1))

    def cross_attend(self, q, memory, clips):
        q = self.clip_rows(q, clips)
        memory = memory.reshape(clips, -1, memory.shape[-1])
        cols = q.shape[-1]
        k, v = memory[..., :cols], memory[..., cols:]
        out, chances = cross_attend(q, k, v)
        return self.unclip_rows(out), (q, k, v, chances)

    def cross_back(self, saved, grad, clips):
        dq, dk, dv = cross_attend_back(*saved, self.clip_rows(grad, clips))
        return self.unclip_rows(dq), self.unsequence(jnp.concatenate([dk, dv], axis=-1))

    def feed(self, rows, weight):
        return gelu_pair(mm(rows, weight))

    def sum_own(self, left, right, product, clips):
        part = product(left, right).astype(BF).reshape(clips, -1, right_width(product, right))
        own = lax.psum_scatter(part, self.tensor, scatter_dimension=1, tiled=True)
        return own.reshape(-1, part.shape[-1]).astype(F32)

    def sum_all(self, values):
        return lax.psum(values.astype(BF), self.tensor).astype(F32)


def right_width(product, right):
    return right.shape[0] if product is mm_t else right.shape[1]


class Block(Whole):
    def __init__(self, width):
        self.width = width
        self.shard = width // 16
        self.core = lax.axis_index("core")

    def order(self):
        own_y, own_x = lax.axis_index("y"), lax.axis_index("x")
        place = jnp.arange(self.width, dtype=jnp.int32)
        quarter, rest = place // (4 * self.shard), place % (4 * self.shard)
        z, row = rest // self.shard, rest % self.shard
        y, x = (quarter // 2) ^ own_y, (quarter % 2) ^ own_x
        source = ((z * 2 + y) * 2 + x) * self.shard + row
        return (jnp.arange(self.width, dtype=jnp.int32)[:, None] == source[None, :]).astype(BF)

    def arrange(self, values):
        return mm(values, self.order()).astype(BF)

    def restore(self, values):
        if values.dtype == BF:
            return mm_t(values, self.order()).astype(BF)
        high = lax.reduce_precision(values, 8, 7)
        low = (values - high).astype(BF)
        order = self.order()
        return mm_t(high.astype(BF), order) + mm_t(low, order)

    def x(self, v):
        return lax.ppermute(v, "x", SWAP)

    def y(self, v):
        return lax.ppermute(v, "y", SWAP)

    def other(self, v):
        return lax.ppermute(v, "core", SWAP)

    def gather_norms(self, packed):
        pair = jnp.stack([packed, lax.ppermute(packed, "z", [(0, 1), (1, 0), (2, 3), (3, 2)])])
        far = lax.ppermute(pair, "z", [(0, 2), (1, 3), (2, 0), (3, 1)])
        own = lax.axis_index("z")
        four = jnp.concatenate([pair, far])
        four = jnp.stack([lax.dynamic_index_in_dim(four, own ^ p, 0, False) for p in range(4)])
        two = jnp.stack([four, self.x(four)])
        whole = jnp.stack([two, self.y(two)])
        return whole.reshape(self.width, packed.shape[-1])

    def halves(self, shard):
        half = shard.shape[1] // 256 * 128
        return shard[:, :half], shard[:, half:]

    def gather_first(self, shard):
        four = lax.all_gather(shard, "z", axis=0, tiled=True)
        a, b = self.halves(four)
        n, half = a.shape
        xa, yb, ya, xb = self.x(a), self.y(b), self.y(a), self.x(b)
        far_a, far_b = self.y(xa), self.x(yb)
        return place(
            [
                (four, 0, 0),
                (xa, n, 0),
                (ya, 2 * n, 0),
                (far_a, 3 * n, 0),
                (xb, n, half),
                (yb, 2 * n, half),
                (far_b, 3 * n, half),
            ],
            (4 * n, shard.shape[1]),
        )

    def gather_middle(self, shard):
        a, b = self.halves(shard)
        four = jnp.stack([a, self.x(a), b, self.y(b)])
        four = lax.all_gather(four, "z", axis=1, tiled=True)
        _, n, half = four.shape
        far_a, far_b = self.y(four[:2]), self.x(four[2:])
        four = four.reshape(4 * n, half)
        far_a, far_b = far_a.reshape(2 * n, half), far_b.reshape(2 * n, half)
        return place_stacked(four, far_a, far_b)

    def scatter_open(self, make, columns):
        n = self.width // 4
        half = columns // 256 * 128
        left, right = slice(0, half), slice(half, columns)
        far_left = self.y(make(slice(2 * n, 4 * n), left).astype(BF))
        far_right = self.x(
            jnp.concatenate(
                [make(slice(n, 2 * n), right).astype(BF), make(slice(3 * n, 4 * n), right).astype(BF)]
            )
        )
        a = (make(slice(0, 2 * n), left) + far_left.astype(F32)).astype(BF)
        b = [
            (make(slice(0, n), right) + far_right[:n].astype(F32)).astype(BF),
            (make(slice(2 * n, 3 * n), right) + far_right[n:].astype(F32)).astype(BF),
        ]
        return a[:n], a[n:], b[0], b[1]

    def scatter_middle(self, make, columns):
        four = jnp.stack(self.scatter_open(make, columns))
        four = lax.psum_scatter(four, "z", scatter_dimension=1, tiled=True)
        left = four[0].astype(F32) + self.x(four[1]).astype(F32)
        right = four[2].astype(F32) + self.y(four[3]).astype(F32)
        return jnp.concatenate([left, right], axis=1)

    def scatter_last(self, make, columns):
        a0, a1, b0, b1 = self.scatter_open(make, columns)
        far_a, far_b = self.x(a1), self.y(b1)
        both = jnp.stack(
            [
                (a0.astype(F32) + far_a.astype(F32)).astype(BF),
                (b0.astype(F32) + far_b.astype(F32)).astype(BF),
            ]
        )
        both = lax.psum_scatter(both, "z", scatter_dimension=1, tiled=True).astype(F32)
        return jnp.concatenate([both[0], both[1]], axis=1)

    def spread(self, rows, clips):
        return jnp.concatenate([rows, self.other(rows)])

    def self_attend(self, qkv, clips):
        cols = qkv.shape[-1] // 3
        steps = cols // (2 * HEAD_DIM)
        view = qkv.reshape(2, clips, -1, qkv.shape[-1])
        frames = view.shape[2]

        def block(part):
            return pl.BlockSpec(
                (2, 1, frames, 2 * HEAD_DIM), lambda c, j, _: (0, c, 0, part * steps + j)
            )

        shape = (2, clips, frames, cols)
        core = self.core.reshape(1).astype(jnp.int32)
        scores = clips * steps * 2 * 3 * frames * frames
        out, log_total = pl.pallas_call(
            self_kernel,
            grid_spec=pltpu.PrefetchScalarGridSpec(
                num_scalar_prefetch=1,
                grid=(clips, steps),
                in_specs=[block(0), block(1), block(2)],
                out_specs=[block(0), block(0)],
            ),
            out_shape=[jax.ShapeDtypeStruct(shape, BF), jax.ShapeDtypeStruct(shape, F32)],
            cost_estimate=pl.CostEstimate(
                flops=4 * scores * HEAD_DIM,
                transcendentals=scores,
                bytes_accessed=2 * qkv.size + 6 * qkv.size // 3,
            ),
            name="self_attend",
        )(core, view, view, view)
        return out.reshape(-1, cols), (core, view, log_total)

    def self_back(self, saved, grad, clips):
        core, view, log_total = saved
        cols = view.shape[-1] // 3
        steps = cols // (2 * HEAD_DIM)
        frames = view.shape[2]

        def block(part):
            return pl.BlockSpec(
                (2, 1, frames, 2 * HEAD_DIM), lambda c, j, _: (0, c, 0, part * steps + j)
            )

        scores = clips * steps * 2 * 3 * frames * frames
        out = pl.pallas_call(
            self_back_kernel,
            grid_spec=pltpu.PrefetchScalarGridSpec(
                num_scalar_prefetch=1,
                grid=(clips, steps),
                in_specs=[block(0), block(1), block(2), block(0), block(0)],
                out_specs=pl.BlockSpec((2, 1, frames, 3 * cols), lambda c, j, _: (0, c, 0, 0)),
            ),
            out_shape=jax.ShapeDtypeStruct(view.shape, BF),
            cost_estimate=pl.CostEstimate(
                flops=10 * scores * HEAD_DIM,
                transcendentals=scores,
                bytes_accessed=4 * view.size + 6 * view.size // 3,
            ),
            name="self_back",
        )(core, view, view, view, log_total, grad.reshape(2, clips, frames, cols))
        return out.reshape(-1, 3 * cols)

    def cross_specs(self, q, clips, texts):
        cols = q.shape[-1]
        steps = cols // (2 * HEAD_DIM)
        view = q.reshape(2, clips, -1, cols)
        frames = view.shape[2]
        wide = pl.BlockSpec((2, 1, frames, 2 * HEAD_DIM), lambda c, j: (0, c, 0, j))

        def block(part):
            return pl.BlockSpec((1, texts, 2 * HEAD_DIM), lambda c, j: (c, 0, part * steps + j))

        return view, (clips, steps), wide, block, clips * 2 * frames * cols * texts

    def cross_attend(self, q, memory, clips):
        memory = memory.reshape(clips, -1, memory.shape[-1])
        view, grid, wide, block, work = self.cross_specs(q, clips, memory.shape[1])
        out = pl.pallas_call(
            cross_kernel,
            grid=grid,
            in_specs=[wide, block(0), block(1)],
            out_specs=wide,
            out_shape=jax.ShapeDtypeStruct(view.shape, BF),
            cost_estimate=pl.CostEstimate(
                flops=4 * work, transcendentals=work // HEAD_DIM, bytes_accessed=4 * q.size
            ),
            name="cross_attend",
        )(view, memory, memory)
        return out.reshape(q.shape), (q, memory)

    def cross_back(self, saved, grad, clips):
        q, memory = saved
        texts = memory.shape[1]
        view, grid, wide, block, work = self.cross_specs(q, clips, texts)
        dq, dkv = pl.pallas_call(
            cross_back_kernel,
            grid=grid,
            in_specs=[wide, block(0), block(1), wide],
            out_specs=[
                wide,
                pl.BlockSpec((1, texts, memory.shape[-1]), lambda c, j: (c, 0, 0)),
            ],
            out_shape=[
                jax.ShapeDtypeStruct(view.shape, BF),
                jax.ShapeDtypeStruct(memory.shape, BF),
            ],
            cost_estimate=pl.CostEstimate(
                flops=10 * work, transcendentals=work // HEAD_DIM, bytes_accessed=6 * q.size
            ),
            name="cross_back",
        )(view, memory, memory, grad.reshape(view.shape))
        return dq.reshape(q.shape), dkv.reshape(-1, memory.shape[-1])

    def feed(self, rows, weight):
        return feed(rows, weight)

    def sum_own(self, left, right, product, clips):
        n = left.shape[0] // 2
        far = self.other(product(left[n:], right).astype(BF))
        return product(left[:n], right) + far.astype(F32)

    def sum_all(self, values):
        return values + self.other(values.astype(BF)).astype(F32)


def layer(
    comm,
    frames,
    text_states,
    norm_gain,
    norm_shift,
    self_project,
    self_output,
    cross_query,
    cross_memory,
    cross_output,
    feed_input,
    feed_output,
    upstream,
):
    clips, own_frames, width = frames.shape
    texts = text_states.shape[1]
    cols = cross_query.shape[1]
    own_rows = clips * own_frames

    def catenate(parts):
        return jnp.concatenate(parts, axis=1)

    norms = comm.gather_norms(
        jnp.pad(jnp.concatenate([norm_gain, norm_shift]).T, ((0, 0), (0, 122)))
    )
    norms = norms.T.astype(F32)
    gain, shift = norms[0:3], norms[3:6]
    first_set = catenate([self_project[0], self_project[1], self_project[2]])
    second_set = catenate(
        [self_output.T, cross_query, cross_memory[0], cross_memory[1], cross_output.T]
    )
    w_self = comm.gather_first(first_set)
    w_cross = comm.gather_first(second_set)
    w_in = comm.gather_middle(feed_input)
    w_out = comm.gather_middle(feed_output.T)
    w_so, w_cq = w_cross[:, :cols], w_cross[:, cols : 2 * cols]
    w_cm, w_co = w_cross[:, 2 * cols : 4 * cols], w_cross[:, 4 * cols :]

    values0 = comm.arrange(frames.reshape(own_rows, width)).astype(F32)
    up = comm.arrange(upstream.reshape(own_rows, width))
    text = comm.arrange(text_states.reshape(clips * texts, width))
    up_all = comm.spread(up, clips)

    stats0 = norm_stats(values0)
    n1 = comm.spread(norm_apply(values0, stats0, gain[0], shift[0]), clips)
    att, self_saved = comm.self_attend(mm(n1, w_self).astype(BF), clips)
    values1 = values0 + comm.sum_own(att, w_so, mm_t, clips)

    stats1 = norm_stats(values1)
    n2 = comm.spread(norm_apply(values1, stats1, gain[1], shift[1]), clips)
    cross, cross_saved = comm.cross_attend(
        mm(n2, w_cq).astype(BF), mm(text, w_cm).astype(BF), clips
    )
    values2 = values1 + comm.sum_own(cross, w_co, mm_t, clips)

    stats2 = norm_stats(values2)
    n3 = comm.spread(norm_apply(values2, stats2, gain[2], shift[2]), clips)
    hidden, slope = comm.feed(n3, w_in)
    layer_out = (values2 + comm.sum_own(hidden, w_out, mm_t, clips)).astype(BF)
    layer_out = comm.restore(layer_out).reshape(clips, own_frames, width)

    def wgrad(left, right):
        return lambda rows, columns: mm_rows(left[:, rows], right[:, columns])

    def scatter(method, left, right):
        if type(comm) is Whole:
            return method(wgrad(left, right))
        return method(wgrad(left, right), right.shape[1])

    grad_out = scatter(comm.scatter_middle, up_all, hidden)
    pre_grad = (mm(up_all, w_out) * slope.astype(F32)).astype(BF)
    grad_in = scatter(comm.scatter_middle, n3, pre_grad)
    e3 = comm.sum_own(pre_grad, w_in, mm_t, clips)
    dv2, gain2, shift2 = norm_back(values2, stats2, gain[2], e3)
    r2 = up.astype(F32) + dv2
    r2_all = comm.spread(r2.astype(BF), clips)
    dcq, dmem = comm.cross_back(cross_saved, mm(r2_all, w_co).astype(BF), clips)
    text_grad = comm.sum_all(mm_t(dmem, w_cm))
    e2 = comm.sum_own(dcq, w_cq, mm_t, clips)
    dv1, gain1, shift1 = norm_back(values1, stats1, gain[1], e2)
    r1 = r2 + dv1
    r1_all = comm.spread(r1.astype(BF), clips)
    grad_co = scatter(comm.scatter_last, r2_all, cross)
    grad_cq = scatter(comm.scatter_last, n2, dcq)
    grad_cm = scatter(comm.scatter_last, text, dmem)
    grad_so = scatter(comm.scatter_last, r1_all, att)
    dqkv = comm.self_back(self_saved, mm(r1_all, w_so).astype(BF), clips)
    grad_self = scatter(comm.scatter_last, n1, dqkv)
    e1 = comm.sum_own(dqkv, w_self, mm_t, clips)
    dv0, gain0, shift0 = norm_back(values0, stats0, gain[0], e1)
    input_grad = comm.restore(r1 + dv0).reshape(clips, own_frames, width)
    text_grad = comm.restore(text_grad).reshape(clips, texts, width)
    packed = jnp.stack([gain0, gain1, gain2, shift0, shift1, shift2]).T
    packed = jnp.pad(packed, ((0, 0), (0, 250)))

    def norm_sums(rows, columns):
        return packed[rows, columns]

    if type(comm) is Whole:
        norm_grad = comm.scatter_last(norm_sums)
    else:
        norm_grad = comm.scatter_last(norm_sums, packed.shape[1])
    norm_grad = comm.sum_all(norm_grad[:, :8]).T
    return (
        layer_out,
        input_grad,
        text_grad,
        norm_grad[0:3],
        norm_grad[3:6],
        jnp.stack([grad_self[:, i * cols : (i + 1) * cols] for i in range(3)]),
        grad_so.T,
        grad_cq,
        jnp.stack([grad_cm[:, :cols], grad_cm[:, cols:]]),
        grad_co.T,
        grad_in,
        grad_out.T,
    )


def specs(dp, tensor):
    in_specs = (
        P(dp, tensor, None),
        P(dp, None, None),
        P(None, dp),
        P(None, dp),
        P(None, dp, tensor),
        P(tensor, dp),
        P(dp, tensor),
        P(None, dp, tensor),
        P(tensor, dp),
        P(dp, tensor),
        P(tensor, dp),
        P(dp, tensor, None),
    )
    out_specs = (
        P(dp, tensor, None),
        P(dp, tensor, None),
        P(dp, None, None),
        P(None, dp),
        P(None, dp),
        P(None, dp, tensor),
        P(tensor, dp),
        P(dp, tensor),
        P(None, dp, tensor),
        P(tensor, dp),
        P(dp, tensor),
        P(tensor, dp),
    )
    return in_specs, out_specs


def solution(mesh):
    if mesh.shape["dp"] == 16 and mesh.shape["tensor"] == 2:
        mesh = Mesh(mesh.devices.reshape(4, 2, 2, 2), ("z", "y", "x", "core"))
        in_specs, out_specs = specs(("z", "y", "x"), "core")

        def per_device(frames, *rest):
            return layer(Block(frames.shape[-1]), frames, *rest)
    else:
        in_specs, out_specs = specs("dp", "tensor")

        def per_device(frames, *rest):
            return layer(Whole("dp", "tensor"), frames, *rest)

    return jax.shard_map(
        per_device, mesh=mesh, in_specs=in_specs, out_specs=out_specs, check_vma=False
    )
```

```python
import math

import jax
import jax.numpy as jnp
from jax import lax
from jax.experimental import pallas as pl
from jax.experimental.pallas import tpu as pltpu
from jax.sharding import Mesh
from jax.sharding import PartitionSpec as P

HEAD_DIM = 64
EPS = 1e-05
BF = jnp.bfloat16
F32 = jnp.float32
SWAP = [(0, 1), (1, 0)]


def mm(left, right):
    return jnp.dot(left, right, preferred_element_type=F32)


def mm_t(left, right):
    return lax.dot_general(left, right, (((1,), (1,)), ((), ())), preferred_element_type=F32)


def mm_rows(left, right):
    return lax.dot_general(left, right, (((0,), (0,)), ((), ())), preferred_element_type=F32)


def tie(value, *others):
    return lax.optimization_barrier((value, others))[0]


def norm_stats(values):
    mean = jnp.mean(values, axis=-1, keepdims=True)
    centred = values - mean
    inv = lax.rsqrt(jnp.mean(centred * centred, axis=-1, keepdims=True) + EPS)
    return mean, inv


def norm_apply(values, stats, gain, shift):
    return ((values - stats[0]) * stats[1] * gain + shift).astype(BF)


def norm_back(values, stats, gain, grad):
    xhat = (values - stats[0]) * stats[1]
    scaled = grad * gain
    part = jnp.mean(scaled, axis=-1, keepdims=True)
    cross = jnp.mean(scaled * xhat, axis=-1, keepdims=True)
    value_grad = (scaled - part - xhat * cross) * stats[1]
    return value_grad, jnp.sum(grad * xhat, axis=0), jnp.sum(grad, axis=0)


def gelu_pair(pre):
    phi = 0.5 * (1.0 + lax.erf(pre * (1.0 / math.sqrt(2.0))))
    dens = jnp.exp(-0.5 * pre * pre) * (1.0 / math.sqrt(2.0 * math.pi))
    return (pre * phi).astype(BF), (phi + pre * dens).astype(BF)


def heads(matrix):
    return matrix.reshape(*matrix.shape[:-1], matrix.shape[-1] // HEAD_DIM, HEAD_DIM)


def flat(matrix):
    return matrix.reshape(*matrix.shape[:-2], -1)


SCALE = 1.0 / math.sqrt(HEAD_DIM)


def causal_scores(q, k):
    scores = jnp.einsum("bqhd,bkhd->bhqk", heads(q), heads(k), preferred_element_type=F32) * SCALE
    n = q.shape[1]
    allowed = jnp.arange(n)[None, :] <= jnp.arange(n)[:, None]
    return jnp.where(allowed, scores, -1e30)


def attend(q, k, v):
    scores = causal_scores(q, k)
    top = jnp.max(scores, axis=-1, keepdims=True)
    terms = jnp.exp(scores - top)
    total = jnp.sum(terms, axis=-1, keepdims=True)
    out = jnp.einsum(
        "bhqk,bkhd->bqhd", (terms / total).astype(BF), heads(v), preferred_element_type=F32
    )
    return flat(out).astype(BF), top + jnp.log(total)


def probs_back(chances, dp, q, k, grad):
    dot = jnp.sum(chances * dp, axis=-1, keepdims=True)
    ds = (chances * (dp - dot)).astype(BF)
    dv = jnp.einsum("bhqk,bqhd->bkhd", chances.astype(BF), grad, preferred_element_type=F32)
    dq = jnp.einsum("bhqk,bkhd->bqhd", ds, heads(k), preferred_element_type=F32) * SCALE
    dk = jnp.einsum("bhqk,bqhd->bkhd", ds, heads(q), preferred_element_type=F32) * SCALE
    return flat(dq).astype(BF), flat(dk).astype(BF), flat(dv).astype(BF)


def attend_back(q, k, v, log_total, grad):
    chances = jnp.exp(causal_scores(q, k) - log_total)
    grad = heads(grad)
    dp = jnp.einsum("bqhd,bkhd->bhqk", grad, heads(v), preferred_element_type=F32)
    return probs_back(chances, dp, q, k, grad)


def cross_attend(q, k, v):
    scores = jnp.einsum("bqhd,bkhd->bhqk", heads(q), heads(k), preferred_element_type=F32) * SCALE
    chances = jax.nn.softmax(scores, axis=-1)
    out = jnp.einsum("bhqk,bkhd->bqhd", chances.astype(BF), heads(v), preferred_element_type=F32)
    return flat(out).astype(BF), chances


def cross_attend_back(q, k, v, chances, grad):
    grad = heads(grad)
    dp = jnp.einsum("bqhd,bkhd->bhqk", grad, heads(v), preferred_element_type=F32)
    return probs_back(chances, dp, q, k, grad)

ANY = pl.BlockSpec(memory_space=pl.ANY)
NEG = -1e30


def place_kernel(*refs, spots):
    sources, out, sems = refs[: len(spots)], refs[len(spots)], refs[len(spots) + 1]
    copies = []
    for i, (source, (row, col)) in enumerate(zip(sources, spots)):
        rows, cols = source.shape
        copies.append(
            pltpu.make_async_copy(
                source, out.at[pl.ds(row, rows), pl.ds(col, cols)], sems.at[i]
            )
        )
    for copy in copies:
        copy.start()
    for copy in copies:
        copy.wait()


def place(pieces, shape):
    spots = tuple((row, col) for _, row, col in pieces)
    return pl.pallas_call(
        lambda *refs: place_kernel(*refs, spots=spots),
        out_shape=jax.ShapeDtypeStruct(shape, pieces[0][0].dtype),
        in_specs=[ANY] * len(pieces),
        out_specs=pl.BlockSpec(memory_space=pltpu.VMEM),
        scratch_shapes=[pltpu.SemaphoreType.DMA((len(pieces),))],
        name="place",
    )(*[piece for piece, _, _ in pieces])


def place_stacked_kernel(four, far_a, far_b, out, sems):
    n, half = four.shape[0] // 4, four.shape[1]
    spots = [
        (four, 0, 2 * n, 0, 0),
        (far_a, 0, 2 * n, 2 * n, 0),
        (four, 2 * n, n, 0, half),
        (far_b, 0, n, n, half),
        (four, 3 * n, n, 2 * n, half),
        (far_b, n, n, 3 * n, half),
    ]
    copies = [
        pltpu.make_async_copy(
            source.at[pl.ds(start, rows)], out.at[pl.ds(row, rows), pl.ds(col, half)], sems.at[i]
        )
        for i, (source, start, rows, row, col) in enumerate(spots)
    ]
    for copy in copies:
        copy.start()
    for copy in copies:
        copy.wait()


def place_stacked(four, far_a, far_b):
    return pl.pallas_call(
        place_stacked_kernel,
        out_shape=jax.ShapeDtypeStruct((four.shape[0], 2 * four.shape[1]), four.dtype),
        in_specs=[ANY] * 3,
        out_specs=pl.BlockSpec(memory_space=pltpu.VMEM),
        scratch_shapes=[pltpu.SemaphoreType.DMA((6,))],
        name="place_stacked",
    )(four, far_a, far_b)


def rows_of(matrix, grad):
    return lax.dot_general(matrix, grad, (((0,), (0,)), ((), ())), preferred_element_type=F32)


def head_of(ref, half, head):
    return ref[half, 0, :, head * HEAD_DIM : (head + 1) * HEAD_DIM]


def masked(scores):
    n = scores.shape[0]
    rows = lax.broadcasted_iota(jnp.int32, (n, n), 0)
    cols = lax.broadcasted_iota(jnp.int32, (n, n), 1)
    return jnp.where(cols <= rows, scores, NEG)


def self_kernel(core_ref, q_ref, k_ref, v_ref, out_ref, log_ref):
    halves = (core_ref[0], 1 - core_ref[0])
    outs, logs = ([], []), ([], [])
    for head in range(2):
        q = [head_of(q_ref, h, head) * BF(SCALE) for h in halves]
        k = [head_of(k_ref, h, head) for h in halves]
        v = [head_of(v_ref, h, head) for h in halves]
        first = masked(mm_t(q[0], k[0]))
        for half, scores in enumerate([[first], [mm_t(q[1], k[0]), masked(mm_t(q[1], k[1]))]]):
            top = jnp.max(scores[0], axis=-1, keepdims=True)
            if half:
                top = jnp.maximum(top, jnp.max(scores[1], axis=-1, keepdims=True))
            terms = [jnp.exp(part - top) for part in scores]
            total = sum(jnp.sum(part, axis=-1, keepdims=True) for part in terms)
            inverse = 1.0 / total
            out = sum(mm((part * inverse).astype(BF), v[i]) for i, part in enumerate(terms))
            outs[half].append(out.astype(BF))
            logs[half].append(jnp.broadcast_to(top + jnp.log(total), out.shape))
    for half, h in enumerate(halves):
        out_ref[h, 0] = jnp.concatenate(outs[half], axis=1)
        log_ref[h, 0] = jnp.concatenate(logs[half], axis=1)


def self_back_kernel(core_ref, q_ref, k_ref, v_ref, log_ref, grad_ref, out_ref):
    halves = (core_ref[0], 1 - core_ref[0])
    found = [[], [], [], [], [], []]
    for head in range(2):
        q = [head_of(q_ref, h, head) * BF(SCALE) for h in halves]
        k = [head_of(k_ref, h, head) for h in halves]
        ks = [part * BF(SCALE) for part in k]
        v = [head_of(v_ref, h, head) for h in halves]
        log = [head_of(log_ref, h, head)[:, :1] for h in halves]
        grad = [head_of(grad_ref, h, head) for h in halves]
        dq, dk, dv = [0.0, 0.0], [0.0, 0.0], [0.0, 0.0]
        for half, parts in enumerate([(0,), (0, 1)]):
            chances, dps = [], []
            for i in parts:
                scores = mm_t(q[half], k[i])
                if i == half:
                    scores = masked(scores)
                chances.append(jnp.exp(scores - log[half]))
                dps.append(mm_t(grad[half], v[i]))
            dot = sum(
                jnp.sum(c * dp, axis=-1, keepdims=True) for c, dp in zip(chances, dps)
            )
            for i, c, dp in zip(parts, chances, dps):
                ds = (c * (dp - dot)).astype(BF)
                dv[i] += rows_of(c.astype(BF), grad[half])
                dk[i] += rows_of(ds, q[half])
                dq[half] += mm(ds, ks[i])
        for i, part in enumerate(dq + dk + dv):
            found[i].append(part.astype(BF))
    width = out_ref.shape[-1] // 3
    for i in range(3):
        col = pl.multiple_of(i * width + pl.program_id(1) * 2 * HEAD_DIM, 2 * HEAD_DIM)
        for half, h in enumerate(halves):
            out_ref[h, 0, :, pl.ds(col, 2 * HEAD_DIM)] = jnp.concatenate(
                found[2 * i + half], axis=1
            )


def cross_parts(q_ref, k_ref, head):
    cs = slice(head * HEAD_DIM, (head + 1) * HEAD_DIM)
    q = jnp.concatenate([q_ref[0, 0, :, cs], q_ref[1, 0, :, cs]]) * BF(SCALE)
    scores = mm_t(q, k_ref[0, :, cs])
    terms = jnp.exp(scores - jnp.max(scores, axis=-1, keepdims=True))
    return q, terms * (1.0 / jnp.sum(terms, axis=-1, keepdims=True)), cs


def cross_kernel(q_ref, k_ref, v_ref, out_ref):
    outs = []
    for head in range(2):
        _, chances, cs = cross_parts(q_ref, k_ref, head)
        outs.append(mm(chances.astype(BF), v_ref[0, :, cs]).astype(BF))
    out = jnp.concatenate(outs, axis=1)
    n = out.shape[0] // 2
    out_ref[0, 0], out_ref[1, 0] = out[:n], out[n:]


def cross_back_kernel(q_ref, k_ref, v_ref, grad_ref, dq_ref, dkv_ref):
    found = [[], [], []]
    for head in range(2):
        q, chances, cs = cross_parts(q_ref, k_ref, head)
        grad = jnp.concatenate([grad_ref[0, 0, :, cs], grad_ref[1, 0, :, cs]])
        dp = mm_t(grad, v_ref[0, :, cs])
        ds = (chances * (dp - jnp.sum(chances * dp, axis=-1, keepdims=True))).astype(BF)
        found[0].append(mm(ds, k_ref[0, :, cs] * BF(SCALE)).astype(BF))
        found[1].append(rows_of(ds, q).astype(BF))
        found[2].append(rows_of(chances.astype(BF), grad).astype(BF))
    dq, dk, dv = [jnp.concatenate(parts, axis=1) for parts in found]
    n = dq.shape[0] // 2
    dq_ref[0, 0], dq_ref[1, 0] = dq[:n], dq[n:]
    width = dkv_ref.shape[-1] // 2
    for i, part in enumerate([dk, dv]):
        col = pl.multiple_of(i * width + pl.program_id(1) * 2 * HEAD_DIM, 2 * HEAD_DIM)
        dkv_ref[0, :, pl.ds(col, 2 * HEAD_DIM)] = part


def feed_kernel(rows_ref, weight_ref, hidden_ref, slope_ref):
    step = 256

    def body(i, carry):
        at = pl.ds(pl.multiple_of(i * step, step), step)
        hidden_ref[at], slope_ref[at] = gelu_pair(mm(rows_ref[at], weight_ref[...]))
        return carry

    lax.fori_loop(0, rows_ref.shape[0] // step, body, 0, unroll=True)


def feed(rows, weight):
    count, depth = rows.shape
    width = weight.shape[1]
    block = 256
    out = jax.ShapeDtypeStruct((count, width), BF)
    return pl.pallas_call(
        feed_kernel,
        grid=(width // block,),
        in_specs=[
            pl.BlockSpec((count, depth), lambda j: (0, 0)),
            pl.BlockSpec((depth, block), lambda j: (0, j)),
        ],
        out_specs=[pl.BlockSpec((count, block), lambda j: (0, j))] * 2,
        out_shape=[out, out],
        cost_estimate=pl.CostEstimate(
            flops=2 * count * depth * width,
            transcendentals=2 * count * width,
            bytes_accessed=2 * (count * depth + depth * width + 2 * count * width),
        ),
        name="feed",
    )(rows, weight)


def slope_kernel(rows_ref, weight_ref, slope_ref, out_ref):
    step = 256

    def body(i, carry):
        at = pl.ds(pl.multiple_of(i * step, step), step)
        grad = mm(rows_ref[at], weight_ref[...])
        out_ref[at] = (grad * slope_ref[at].astype(F32)).astype(BF)
        return carry

    lax.fori_loop(0, rows_ref.shape[0] // step, body, 0, unroll=True)


def slope_product(rows, weight, slope):
    count, depth = rows.shape
    width = weight.shape[1]
    block = 256
    tall = pl.BlockSpec((count, block), lambda j: (0, j))
    return pl.pallas_call(
        slope_kernel,
        grid=(width // block,),
        in_specs=[
            pl.BlockSpec((count, depth), lambda j: (0, 0)),
            pl.BlockSpec((depth, block), lambda j: (0, j)),
            tall,
        ],
        out_specs=tall,
        out_shape=jax.ShapeDtypeStruct((count, width), BF),
        cost_estimate=pl.CostEstimate(
            flops=2 * count * depth * width,
            transcendentals=0,
            bytes_accessed=2 * (count * depth + depth * width + 2 * count * width),
        ),
        name="slope_product",
    )(rows, weight, slope)


class Whole:
    def __init__(self, dp, tensor):
        self.dp, self.tensor = dp, tensor

    def arrange(self, values):
        return values

    def restore(self, values):
        return values

    def gather_norms(self, packed):
        return lax.all_gather(packed, self.dp, axis=0, tiled=True)

    def gather_first(self, shard):
        return lax.all_gather(shard, self.dp, axis=0, tiled=True)

    def gather_weights(self, *sets_and_rows):
        *sets, rows = sets_and_rows
        *first, last = [self.gather_first(shard) for shard in sets]
        return *first, rows, None, None, (last, None)

    def feed_out(self, pieces):
        return pieces[0]

    def after(self, value, *others):
        return value

    def stage(self, work, *values):
        return work(*values)

    def sends(self, left, right):
        return ()

    def exchange(self, sends):
        return ()

    def merged(self, *sends):
        return ()

    def parted(self, far, *widths):
        return [()] * len(widths)

    def adds(self, *products):
        wholes = [mm_rows(left, right).astype(BF) for left, right, _ in products]
        return jnp.concatenate(wholes, axis=1)

    def second(self, whole):
        return ()

    def closing(self, whole, far):
        return whole

    middle = closing

    def scatter_z(self, whole):
        return lax.psum_scatter(whole, self.dp, scatter_dimension=0, tiled=True)

    def close_middle(self, whole):
        return whole.astype(F32)

    def close_last(self, whole, *widths):
        found, at = [], 0
        for columns in widths:
            found.append(whole[:, at : at + columns].astype(F32))
            at += columns
        return found

    def norm_sums(self, sums):
        sums = jnp.pad(sums.T, ((0, 0), (0, 122))).astype(BF)
        sums = lax.psum_scatter(sums, self.dp, scatter_dimension=0, tiled=True)
        return self.sum_all(sums)[:, :6].T

    def spread(self, rows, clips):
        local = rows.reshape(clips, -1, rows.shape[-1])
        return lax.all_gather(local, self.tensor, axis=1, tiled=True).reshape(-1, rows.shape[-1])

    def sequence(self, rows, clips):
        return rows.reshape(clips, -1, rows.shape[-1])

    def unsequence(self, rows):
        return rows.reshape(-1, rows.shape[-1])

    def clip_rows(self, rows, clips):
        return rows.reshape(clips, -1, rows.shape[-1])

    unclip_rows = unsequence

    def self_attend(self, qkv, clips):
        qkv = self.sequence(qkv, clips)
        cols = qkv.shape[-1] // 3
        q, k, v = qkv[..., :cols], qkv[..., cols : 2 * cols], qkv[..., 2 * cols :]
        att, log_total = attend(q, k, v)
        return self.unsequence(att), (q, k, v, log_total)

    def self_back(self, saved, grad, clips):
        dq, dk, dv = attend_back(*saved, self.sequence(grad, clips))
        return self.unsequence(jnp.concatenate([dq, dk, dv], axis=-1))

    def cross_attend(self, q, memory, clips):
        q = self.clip_rows(q, clips)
        memory = memory.reshape(clips, -1, memory.shape[-1])
        cols = q.shape[-1]
        k, v = memory[..., :cols], memory[..., cols:]
        out, chances = cross_attend(q, k, v)
        return self.unclip_rows(out), (q, k, v, chances)

    def cross_back(self, saved, grad, clips):
        dq, dk, dv = cross_attend_back(*saved, self.clip_rows(grad, clips))
        return self.unclip_rows(dq), self.unsequence(jnp.concatenate([dk, dv], axis=-1))

    def feed(self, rows, weight):
        return gelu_pair(mm(rows, weight))

    def slope_product(self, rows, weight, slope):
        return (mm(rows, weight) * slope.astype(F32)).astype(BF)

    def sum_own(self, left, right, product, clips):
        part = product(left, right).astype(BF).reshape(clips, -1, right_width(product, right))
        own = lax.psum_scatter(part, self.tensor, scatter_dimension=1, tiled=True)
        return own.reshape(-1, part.shape[-1]).astype(F32)

    def sum_all(self, values):
        return lax.psum(values.astype(BF), self.tensor).astype(F32)


def right_width(product, right):
    return right.shape[0] if product is mm_t else right.shape[1]


class Block(Whole):
    def __init__(self, width):
        self.width = width
        self.shard = width // 16
        self.core = lax.axis_index("core")

    def after(self, value, *others):
        return tie(value, others)

    def order(self):
        own_y, own_x = lax.axis_index("y"), lax.axis_index("x")
        place = jnp.arange(self.width, dtype=jnp.int32)
        quarter, rest = place // (4 * self.shard), place % (4 * self.shard)
        z, row = rest // self.shard, rest % self.shard
        y, x = (quarter // 2) ^ own_y, (quarter % 2) ^ own_x
        source = ((z * 2 + y) * 2 + x) * self.shard + row
        return (jnp.arange(self.width, dtype=jnp.int32)[:, None] == source[None, :]).astype(BF)

    def arrange(self, values):
        return mm(values, self.order()).astype(BF)

    def restore(self, values):
        if values.dtype == BF:
            return mm_t(values, self.order()).astype(BF)
        high = lax.reduce_precision(values, 8, 7)
        low = (values - high).astype(BF)
        order = self.order()
        return mm_t(high.astype(BF), order) + mm_t(low, order)

    def x(self, v):
        return lax.ppermute(v, "x", SWAP)

    def y(self, v):
        return lax.ppermute(v, "y", SWAP)

    def other(self, v):
        return lax.ppermute(v, "core", SWAP)

    def gather_norms(self, packed):
        pair = jnp.stack([packed, lax.ppermute(packed, "z", [(0, 1), (1, 0), (2, 3), (3, 2)])])
        far = lax.ppermute(pair, "z", [(0, 2), (1, 3), (2, 0), (3, 1)])
        own = lax.axis_index("z")
        four = jnp.concatenate([pair, far])
        four = jnp.stack([lax.dynamic_index_in_dim(four, own ^ p, 0, False) for p in range(4)])
        two = jnp.stack([four, self.x(four)])
        whole = jnp.stack([two, self.y(two)])
        return whole.reshape(self.width, packed.shape[-1])

    def halves(self, shard):
        half = shard.shape[1] // 256 * 128
        return shard[:, :half], shard[:, half:]

    def gather_weights(self, first, second, feed_in, feed_out, rows):
        opened = []
        for shard in (feed_in, feed_out):
            a, b = self.halves(shard)
            opened.append(jnp.stack([a, self.x(a), b, self.y(b)]))
        rows, opened = lax.optimization_barrier((rows, opened))
        sets = [lax.all_gather(shard, "z", axis=0, tiled=True) for shard in (first, second)]
        feeds = [lax.all_gather(four, "z", axis=1, tiled=True) for four in opened]
        whole, last = [], rows
        in_sides = feeds[0][:2], feeds[0][2:]
        for four, ahead in zip(sets, ((), in_sides)):
            a, b = self.halves(tie(four, last))
            n, half = a.shape
            xa, yb, ya, xb = self.x(a), self.y(b), self.y(a), self.x(b)
            far_a, far_b = self.y(xa), self.x(yb)
            last, before = (far_a, far_b, ya, xb), (xa, yb)
            four = tie(four, ahead)
            whole.append(
                place(
                    [
                        (four, 0, 0),
                        (xa, n, 0),
                        (ya, 2 * n, 0),
                        (far_a, 3 * n, 0),
                        (xb, n, half),
                        (yb, 2 * n, half),
                        (far_b, 3 * n, half),
                    ],
                    (4 * n, four.shape[1]),
                )
            )
        a, b = tie(in_sides, before)
        in_far = self.y(a), self.x(b)
        whole.append(self.place_feed(feeds[0], in_far))
        out_sides = feeds[1][:2], feeds[1][2:]
        a, b = tie(out_sides, in_far)
        return *whole, rows, in_far, out_sides, (feeds[1], (self.y(a), self.x(b)))

    def place_feed(self, four, far):
        _, n, half = four.shape
        return place_stacked(
            four.reshape(4 * n, half), far[0].reshape(2 * n, half), far[1].reshape(2 * n, half)
        )

    def feed_out(self, pieces):
        return self.place_feed(*pieces)

    def stage(self, work, *values):
        shapes = jax.eval_shape(work, *values)

        def nothing(*_):
            return jax.tree.map(lambda leaf: jnp.zeros(leaf.shape, leaf.dtype), shapes)

        return lax.cond(self.core < 2, work, nothing, *values)

    def sends(self, left, right):
        n, half = self.width // 4, right.shape[1] // 256 * 128
        far = jnp.concatenate([left[:, n : 2 * n], left[:, 3 * n :]], axis=1)
        return (
            mm_rows(left[:, 2 * n :], right[:, :half]).astype(BF),
            mm_rows(far, right[:, half:]).astype(BF),
        )

    def exchange(self, sends):
        return self.y(sends[0]), self.x(sends[1])

    def merged(self, *sends):
        return [jnp.concatenate(side, axis=1) for side in zip(*sends)]

    def parted(self, far, *widths):
        halves = [width // 256 * 128 for width in widths]
        ends = [sum(halves[: i + 1]) for i in range(len(halves) - 1)]
        lefts = jnp.split(far[0], ends, axis=1)
        halves = [width - half for width, half in zip(widths, halves)]
        ends = [sum(halves[: i + 1]) for i in range(len(halves) - 1)]
        return list(zip(lefts, jnp.split(far[1], ends, axis=1)))

    def adds(self, *products):
        n, parts = self.width // 4, []
        for left, right, (far_y, far_x) in products:
            half = right.shape[1] // 256 * 128
            first = (mm_rows(left[:, : 2 * n], right[:, :half]) + far_y.astype(F32)).astype(BF)
            near = jnp.concatenate([left[:, :n], left[:, 2 * n : 3 * n]], axis=1)
            last = (mm_rows(near, right[:, half:]) + far_x.astype(F32)).astype(BF)
            parts.append((first[:n], first[n:], last[:n], last[n:]))
        return [jnp.concatenate(part, axis=1) for part in zip(*parts)]

    def middle(self, parts, _):
        return jnp.stack(parts)

    def second(self, parts):
        return self.x(parts[1]), self.y(parts[3])

    def closing(self, parts, far):
        pairs = zip((parts[0], parts[2]), far)
        return jnp.stack([(own.astype(F32) + other.astype(F32)).astype(BF) for own, other in pairs])

    def scatter_z(self, parts):
        return lax.psum_scatter(parts, "z", scatter_dimension=1, tiled=True)

    def close_middle(self, four):
        left = four[0].astype(F32) + self.x(four[1]).astype(F32)
        right = four[2].astype(F32) + self.y(four[3]).astype(F32)
        return jnp.concatenate([left, right], axis=1)

    def close_last(self, both, *widths):
        found, left, right = [], 0, 0
        for columns in widths:
            a = columns // 256 * 128
            b = columns - a
            found.append(
                jnp.concatenate([both[0, :, left : left + a], both[1, :, right : right + b]], axis=1)
            )
            left, right = left + a, right + b
        return [part.astype(F32) for part in found]

    def norm_sums(self, sums):
        n = self.width // 4
        sums = self.sum_all(jnp.pad(sums.T, ((0, 0), (0, 122))))
        sums = sums[: 2 * n] + self.y(sums[2 * n :].astype(BF)).astype(F32)
        sums = sums[:n] + self.x(sums[n:].astype(BF)).astype(F32)
        sums = lax.psum_scatter(sums.astype(BF), "z", scatter_dimension=0, tiled=True)
        return sums[:, :6].T.astype(F32)

    def spread(self, rows, clips):
        return jnp.concatenate([rows, self.other(rows)])

    def self_attend(self, qkv, clips):
        cols = qkv.shape[-1] // 3
        steps = cols // (2 * HEAD_DIM)
        view = qkv.reshape(2, clips, -1, qkv.shape[-1])
        frames = view.shape[2]

        def block(part):
            return pl.BlockSpec(
                (2, 1, frames, 2 * HEAD_DIM), lambda c, j, _: (0, c, 0, part * steps + j)
            )

        shape = (2, clips, frames, cols)
        core = self.core.reshape(1).astype(jnp.int32)
        scores = clips * steps * 2 * 3 * frames * frames
        out, log_total = pl.pallas_call(
            self_kernel,
            grid_spec=pltpu.PrefetchScalarGridSpec(
                num_scalar_prefetch=1,
                grid=(clips, steps),
                in_specs=[block(0), block(1), block(2)],
                out_specs=[block(0), block(0)],
            ),
            out_shape=[jax.ShapeDtypeStruct(shape, BF), jax.ShapeDtypeStruct(shape, F32)],
            cost_estimate=pl.CostEstimate(
                flops=4 * scores * HEAD_DIM,
                transcendentals=scores,
                bytes_accessed=2 * qkv.size + 6 * qkv.size // 3,
            ),
            name="self_attend",
        )(core, view, view, view)
        return out.reshape(-1, cols), (core, view, log_total)

    def self_back(self, saved, grad, clips):
        core, view, log_total = saved
        cols = view.shape[-1] // 3
        steps = cols // (2 * HEAD_DIM)
        frames = view.shape[2]

        def block(part):
            return pl.BlockSpec(
                (2, 1, frames, 2 * HEAD_DIM), lambda c, j, _: (0, c, 0, part * steps + j)
            )

        scores = clips * steps * 2 * 3 * frames * frames
        out = pl.pallas_call(
            self_back_kernel,
            grid_spec=pltpu.PrefetchScalarGridSpec(
                num_scalar_prefetch=1,
                grid=(clips, steps),
                in_specs=[block(0), block(1), block(2), block(0), block(0)],
                out_specs=pl.BlockSpec((2, 1, frames, 3 * cols), lambda c, j, _: (0, c, 0, 0)),
            ),
            out_shape=jax.ShapeDtypeStruct(view.shape, BF),
            cost_estimate=pl.CostEstimate(
                flops=10 * scores * HEAD_DIM,
                transcendentals=scores,
                bytes_accessed=4 * view.size + 6 * view.size // 3,
            ),
            name="self_back",
        )(core, view, view, view, log_total, grad.reshape(2, clips, frames, cols))
        return out.reshape(-1, 3 * cols)

    def cross_specs(self, q, clips, texts):
        cols = q.shape[-1]
        steps = cols // (2 * HEAD_DIM)
        view = q.reshape(2, clips, -1, cols)
        frames = view.shape[2]
        wide = pl.BlockSpec((2, 1, frames, 2 * HEAD_DIM), lambda c, j: (0, c, 0, j))

        def block(part):
            return pl.BlockSpec((1, texts, 2 * HEAD_DIM), lambda c, j: (c, 0, part * steps + j))

        return view, (clips, steps), wide, block, clips * 2 * frames * cols * texts

    def cross_attend(self, q, memory, clips):
        memory = memory.reshape(clips, -1, memory.shape[-1])
        view, grid, wide, block, work = self.cross_specs(q, clips, memory.shape[1])
        out = pl.pallas_call(
            cross_kernel,
            grid=grid,
            in_specs=[wide, block(0), block(1)],
            out_specs=wide,
            out_shape=jax.ShapeDtypeStruct(view.shape, BF),
            cost_estimate=pl.CostEstimate(
                flops=4 * work, transcendentals=work // HEAD_DIM, bytes_accessed=4 * q.size
            ),
            name="cross_attend",
        )(view, memory, memory)
        return out.reshape(q.shape), (q, memory)

    def cross_back(self, saved, grad, clips):
        q, memory = saved
        texts = memory.shape[1]
        view, grid, wide, block, work = self.cross_specs(q, clips, texts)
        dq, dkv = pl.pallas_call(
            cross_back_kernel,
            grid=grid,
            in_specs=[wide, block(0), block(1), wide],
            out_specs=[
                wide,
                pl.BlockSpec((1, texts, memory.shape[-1]), lambda c, j: (c, 0, 0)),
            ],
            out_shape=[
                jax.ShapeDtypeStruct(view.shape, BF),
                jax.ShapeDtypeStruct(memory.shape, BF),
            ],
            cost_estimate=pl.CostEstimate(
                flops=10 * work, transcendentals=work // HEAD_DIM, bytes_accessed=6 * q.size
            ),
            name="cross_back",
        )(view, memory, memory, grad.reshape(view.shape))
        return dq.reshape(q.shape), dkv.reshape(-1, memory.shape[-1])

    def feed(self, rows, weight):
        return feed(rows, weight)

    def slope_product(self, rows, weight, slope):
        return slope_product(rows, weight, slope)

    def sum_own(self, left, right, product, clips):
        n = left.shape[0] // 2
        far = self.other(product(left[n:], right).astype(BF))
        return product(left[:n], right) + far.astype(F32)

    def sum_all(self, values):
        return values + self.other(values.astype(BF)).astype(F32)


def layer(
    comm,
    frames,
    text_states,
    norm_gain,
    norm_shift,
    self_project,
    self_output,
    cross_query,
    cross_memory,
    cross_output,
    feed_input,
    feed_output,
    upstream,
):
    clips, own_frames, width = frames.shape
    texts = text_states.shape[1]
    cols = cross_query.shape[1]
    own_rows = clips * own_frames

    def catenate(parts):
        return jnp.concatenate(parts, axis=1)

    norms = comm.gather_norms(
        jnp.pad(jnp.concatenate([norm_gain, norm_shift]).T, ((0, 0), (0, 122)))
    )
    norms = norms.T.astype(F32)
    gain, shift = norms[0:3], norms[3:6]
    first_set = catenate([self_project[0], self_project[1], self_project[2]])
    second_set = catenate(
        [self_output.T, cross_query, cross_memory[0], cross_memory[1], cross_output.T]
    )
    values0 = comm.arrange(frames.reshape(own_rows, width)).astype(F32)
    stats0 = norm_stats(values0)
    own_n1 = norm_apply(values0, stats0, gain[0], shift[0])
    w_self, w_cross, w_in, own_n1, mark_in, mark_out, out_pieces = comm.gather_weights(
        first_set, second_set, feed_input, feed_output.T, own_n1
    )

    def split_cross(weights):
        return jnp.split(weights, [cols, 2 * cols, 4 * cols], axis=1)


    up = comm.arrange(upstream.reshape(own_rows, width))
    text = comm.arrange(text_states.reshape(clips * texts, width))
    up_all = comm.spread(up, clips)

    n1 = comm.spread(own_n1, clips)
    att, self_saved = comm.self_attend(mm(n1, w_self).astype(BF), clips)

    def stage0(values0, att, w_cross, text):
        w_so, w_cq, w_cm, w_co = split_cross(w_cross)
        values1 = values0 + comm.sum_own(att, w_so, mm_t, clips)
        stats1 = norm_stats(values1)
        n2 = comm.spread(norm_apply(values1, stats1, gain[1], shift[1]), clips)
        cross, saved = comm.cross_attend(
            mm(n2, w_cq).astype(BF), mm(text, w_cm).astype(BF), clips
        )
        values2 = values1 + comm.sum_own(cross, w_co, mm_t, clips)
        stats2 = norm_stats(values2)
        n3 = comm.spread(norm_apply(values2, stats2, gain[2], shift[2]), clips)
        return values1, stats1, n2, cross, saved, values2, stats2, n3

    values1, stats1, n2, cross, cross_saved, values2, stats2, n3 = comm.stage(
        stage0, values0, att, w_cross, text
    )
    n3 = comm.after(n3, mark_in, mark_out)
    hidden, slope = comm.feed(n3, w_in)
    send_out = comm.sends(up_all, hidden)
    hidden, slope = comm.after((hidden, slope), out_pieces[1], send_out)
    far_out = comm.exchange(send_out)

    def stage1(pieces, rows, slope, n3, w_in):
        w_out = comm.feed_out(pieces)
        pre_grad = comm.slope_product(rows, w_out, slope)
        sends = [comm.sends(n3, part) for part in jnp.split(pre_grad, 2, axis=1)]
        return w_out, pre_grad, sends, comm.sum_own(pre_grad, w_in, mm_t, clips)

    w_out, pre_grad, send_in, e3 = comm.stage(stage1, out_pieces, up_all, slope, n3, w_in)
    e3, send_in = comm.after((e3, send_in), far_out)
    in_parts = jnp.split(pre_grad, 2, axis=1)
    far_in = [comm.exchange(send_in[0])]

    def stage2(rows, hidden, far, e3, values2, stats2, own):
        sent = comm.middle(comm.adds((rows, hidden, far)), None)
        grads = norm_back(values2, stats2, gain[2], e3)
        r2 = own.astype(F32) + grads[0]
        return sent, r2, r2.astype(BF), grads[1], grads[2]

    sent_out, r2, r2_own, gain2, shift2 = comm.stage(
        stage2, up_all, hidden, far_out, e3, values2, stats2, up
    )
    sent_out, r2_own, send_b = comm.after((sent_out, r2_own, send_in[1:]), far_in[0])
    half_out = comm.scatter_z(sent_out)
    far_in += [comm.exchange(sends) for sends in send_b]

    def stage3(r2_own, saved, w_cross, n2, cross, text):
        w_co = split_cross(w_cross)[3]
        r2_all = comm.spread(r2_own, clips)
        dcq, dmem = comm.cross_back(saved, mm(r2_all, w_co).astype(BF), clips)
        pairs = (n2, dcq), (r2_all, cross), (text, dmem)
        return r2_all, dcq, dmem, comm.merged(*[comm.sends(*pair) for pair in pairs])

    r2_all, dcq, dmem, send_cross = comm.stage(
        stage3, r2_own, cross_saved, w_cross, n2, cross, text
    )
    dcq, send_cross = comm.after((dcq, send_cross), far_in)
    far_cross = comm.exchange(send_cross)
    cross_pairs = (n2, dcq), (r2_all, cross), (text, dmem)

    def stage4(n3, parts, far, dcq, w_cross, values1, stats1, r2):
        w_so, w_cq, *_ = split_cross(w_cross)
        in_sums = comm.adds(*[(n3, part, one) for part, one in zip(parts, far)])
        e2 = comm.sum_own(dcq, w_cq, mm_t, clips)
        grads = norm_back(values1, stats1, gain[1], e2)
        r1 = r2 + grads[0]
        r1_all = comm.spread(r1.astype(BF), clips)
        return in_sums, r1, r1_all, mm(r1_all, w_so).astype(BF), grads[1], grads[2]

    in_sums, r1, r1_all, datt, gain1, shift1 = comm.stage(
        stage4, n3, in_parts, tuple(far_in), dcq, w_cross, values1, stats1, r2
    )
    in_sums, datt = comm.after((in_sums, datt), far_cross, half_out)
    in_second = comm.second(in_sums)

    def stage5(pairs, far, saved, datt, r1_all, att):
        far = comm.parted(far, cols, cols, 2 * cols)
        sums = comm.adds(*[(*pair, one) for pair, one in zip(pairs, far)])
        return sums, comm.self_back(saved, datt, clips), comm.sends(r1_all, att)

    cross_sums, dqkv, send_so = comm.stage(
        stage5, cross_pairs, far_cross, self_saved, datt, r1_all, att
    )
    cross_sums, dqkv, send_so, in_sums = comm.after(
        (cross_sums, dqkv, send_so, in_sums), in_second
    )
    half_in = comm.scatter_z(comm.closing(in_sums, in_second))
    far_so = comm.exchange(send_so)
    cross_second = comm.second(cross_sums)
    send_self = comm.stage(comm.sends, n1, dqkv)
    dmem, hidden, send_self, cross_sums = comm.after(
        (dmem, hidden, send_self, cross_sums), cross_second, far_so
    )
    far_self = comm.exchange(send_self)
    half_cross = comm.scatter_z(comm.closing(cross_sums, cross_second))

    def stage6(dmem, w_cross, values2, hidden, w_out):
        w_cm = split_cross(w_cross)[2]
        text_grad = comm.sum_all(mm_t(dmem, w_cm))
        layer_out = (values2 + comm.sum_own(hidden, w_out, mm_t, clips)).astype(BF)
        return comm.restore(text_grad), comm.restore(layer_out)

    text_grad, layer_out = comm.stage(stage6, dmem, w_cross, values2, hidden, w_out)
    text_grad, layer_out, dqkv = comm.after((text_grad, layer_out, dqkv), far_self, half_in)
    self_sums = comm.adds((r1_all, att, far_so), (n1, dqkv, far_self))
    dqkv = comm.after(dqkv, self_sums)
    self_second = comm.second(self_sums)

    def stage7(dqkv, w_self, values0, stats0, r1):
        e1 = comm.sum_own(dqkv, w_self, mm_t, clips)
        grads = norm_back(values0, stats0, gain[0], e1)
        return comm.restore(r1 + grads[0]), grads[1], grads[2]

    input_grad, gain0, shift0 = comm.stage(stage7, dqkv, w_self, values0, stats0, r1)
    input_grad, gain0 = comm.after((input_grad, gain0), self_second, half_cross)
    half_self = comm.scatter_z(comm.closing(self_sums, self_second))
    norm_grad = comm.norm_sums(jnp.stack([gain0, gain1, gain2, shift0, shift1, shift2]))
    input_grad = input_grad.reshape(clips, own_frames, width)
    text_grad = text_grad.reshape(clips, texts, width)
    layer_out = layer_out.reshape(clips, own_frames, width)
    grad_out = comm.close_middle(half_out)
    grad_in = catenate(comm.close_last(half_in, *[part.shape[1] for part in in_parts]))
    grad_cq, grad_co, grad_cm = comm.close_last(half_cross, cols, cols, 2 * cols)
    grad_so, grad_self = comm.close_last(half_self, cols, 3 * cols)
    return (
        layer_out,
        input_grad,
        text_grad,
        norm_grad[0:3],
        norm_grad[3:6],
        jnp.stack([grad_self[:, i * cols : (i + 1) * cols] for i in range(3)]),
        grad_so.T,
        grad_cq,
        jnp.stack([grad_cm[:, :cols], grad_cm[:, cols:]]),
        grad_co.T,
        grad_in,
        grad_out.T,
    )


def specs(dp, tensor):
    in_specs = (
        P(dp, tensor, None),
        P(dp, None, None),
        P(None, dp),
        P(None, dp),
        P(None, dp, tensor),
        P(tensor, dp),
        P(dp, tensor),
        P(None, dp, tensor),
        P(tensor, dp),
        P(dp, tensor),
        P(tensor, dp),
        P(dp, tensor, None),
    )
    out_specs = (
        P(dp, tensor, None),
        P(dp, tensor, None),
        P(dp, None, None),
        P(None, dp),
        P(None, dp),
        P(None, dp, tensor),
        P(tensor, dp),
        P(dp, tensor),
        P(None, dp, tensor),
        P(tensor, dp),
        P(dp, tensor),
        P(tensor, dp),
    )
    return in_specs, out_specs


def solution(mesh):
    if mesh.shape["dp"] == 16 and mesh.shape["tensor"] == 2:
        mesh = Mesh(mesh.devices.reshape(4, 2, 2, 2), ("z", "y", "x", "core"))
        in_specs, out_specs = specs(("z", "y", "x"), "core")

        def per_device(frames, *rest):
            return layer(Block(frames.shape[-1]), frames, *rest)
    else:
        in_specs, out_specs = specs("dp", "tensor")

        def per_device(frames, *rest):
            return layer(Whole("dp", "tensor"), frames, *rest)

    return jax.shard_map(
        per_device, mesh=mesh, in_specs=in_specs, out_specs=out_specs, check_vma=False
    )
```

```python
import math

import jax
import jax.numpy as jnp
from jax import lax
from jax.experimental import pallas as pl
from jax.experimental.pallas import tpu as pltpu
from jax.sharding import Mesh
from jax.sharding import PartitionSpec as P

HEAD_DIM = 64
EPS = 1e-05
BF = jnp.bfloat16
F32 = jnp.float32
SWAP = [(0, 1), (1, 0)]


def mm(left, right):
    return jnp.dot(left, right, preferred_element_type=F32)


def mm_t(left, right):
    return lax.dot_general(left, right, (((1,), (1,)), ((), ())), preferred_element_type=F32)


def mm_rows(left, right):
    return lax.dot_general(left, right, (((0,), (0,)), ((), ())), preferred_element_type=F32)


def tie(value, *others):
    return lax.optimization_barrier((value, others))[0]


def norm_stats(values):
    mean = jnp.mean(values, axis=-1, keepdims=True)
    centred = values - mean
    inv = lax.rsqrt(jnp.mean(centred * centred, axis=-1, keepdims=True) + EPS)
    return mean, inv


def norm_apply(values, stats, gain, shift):
    return ((values - stats[0]) * stats[1] * gain + shift).astype(BF)


def norm_back(values, stats, gain, grad):
    xhat = (values - stats[0]) * stats[1]
    scaled = grad * gain
    part = jnp.mean(scaled, axis=-1, keepdims=True)
    cross = jnp.mean(scaled * xhat, axis=-1, keepdims=True)
    value_grad = (scaled - part - xhat * cross) * stats[1]
    return value_grad, jnp.sum(grad * xhat, axis=0), jnp.sum(grad, axis=0)


def gelu_pair(pre):
    phi = 0.5 * (1.0 + lax.erf(pre * (1.0 / math.sqrt(2.0))))
    dens = jnp.exp(-0.5 * pre * pre) * (1.0 / math.sqrt(2.0 * math.pi))
    return (pre * phi).astype(BF), (phi + pre * dens).astype(BF)


def heads(matrix):
    return matrix.reshape(*matrix.shape[:-1], matrix.shape[-1] // HEAD_DIM, HEAD_DIM)


def flat(matrix):
    return matrix.reshape(*matrix.shape[:-2], -1)


SCALE = 1.0 / math.sqrt(HEAD_DIM)


def causal_scores(q, k):
    scores = jnp.einsum("bqhd,bkhd->bhqk", heads(q), heads(k), preferred_element_type=F32) * SCALE
    n = q.shape[1]
    allowed = jnp.arange(n)[None, :] <= jnp.arange(n)[:, None]
    return jnp.where(allowed, scores, -1e30)


def attend(q, k, v):
    scores = causal_scores(q, k)
    top = jnp.max(scores, axis=-1, keepdims=True)
    terms = jnp.exp(scores - top)
    total = jnp.sum(terms, axis=-1, keepdims=True)
    out = jnp.einsum(
        "bhqk,bkhd->bqhd", (terms / total).astype(BF), heads(v), preferred_element_type=F32
    )
    return flat(out).astype(BF), top + jnp.log(total)


def probs_back(chances, dp, q, k, grad):
    dot = jnp.sum(chances * dp, axis=-1, keepdims=True)
    ds = (chances * (dp - dot)).astype(BF)
    dv = jnp.einsum("bhqk,bqhd->bkhd", chances.astype(BF), grad, preferred_element_type=F32)
    dq = jnp.einsum("bhqk,bkhd->bqhd", ds, heads(k), preferred_element_type=F32) * SCALE
    dk = jnp.einsum("bhqk,bqhd->bkhd", ds, heads(q), preferred_element_type=F32) * SCALE
    return flat(dq).astype(BF), flat(dk).astype(BF), flat(dv).astype(BF)


def attend_back(q, k, v, log_total, grad):
    chances = jnp.exp(causal_scores(q, k) - log_total)
    grad = heads(grad)
    dp = jnp.einsum("bqhd,bkhd->bhqk", grad, heads(v), preferred_element_type=F32)
    return probs_back(chances, dp, q, k, grad)


def cross_attend(q, k, v):
    scores = jnp.einsum("bqhd,bkhd->bhqk", heads(q), heads(k), preferred_element_type=F32) * SCALE
    chances = jax.nn.softmax(scores, axis=-1)
    out = jnp.einsum("bhqk,bkhd->bqhd", chances.astype(BF), heads(v), preferred_element_type=F32)
    return flat(out).astype(BF), chances


def cross_attend_back(q, k, v, chances, grad):
    grad = heads(grad)
    dp = jnp.einsum("bqhd,bkhd->bhqk", grad, heads(v), preferred_element_type=F32)
    return probs_back(chances, dp, q, k, grad)

ANY = pl.BlockSpec(memory_space=pl.ANY)
NEG = -1e30


def place_kernel(*refs, spots):
    sources, out, sems = refs[: len(spots)], refs[len(spots)], refs[len(spots) + 1]
    copies = []
    for i, (source, (row, col)) in enumerate(zip(sources, spots)):
        rows, cols = source.shape
        copies.append(
            pltpu.make_async_copy(
                source, out.at[pl.ds(row, rows), pl.ds(col, cols)], sems.at[i]
            )
        )
    for copy in copies:
        copy.start()
    for copy in copies:
        copy.wait()


def place(pieces, shape):
    spots = tuple((row, col) for _, row, col in pieces)
    return pl.pallas_call(
        lambda *refs: place_kernel(*refs, spots=spots),
        out_shape=jax.ShapeDtypeStruct(shape, pieces[0][0].dtype),
        in_specs=[ANY] * len(pieces),
        out_specs=pl.BlockSpec(memory_space=pltpu.VMEM),
        scratch_shapes=[pltpu.SemaphoreType.DMA((len(pieces),))],
        name="place",
    )(*[piece for piece, _, _ in pieces])


def place_stacked_kernel(four, far_a, far_b, out, sems):
    n, half = four.shape[0] // 4, four.shape[1]
    spots = [
        (four, 0, 2 * n, 0, 0),
        (far_a, 0, 2 * n, 2 * n, 0),
        (four, 2 * n, n, 0, half),
        (far_b, 0, n, n, half),
        (four, 3 * n, n, 2 * n, half),
        (far_b, n, n, 3 * n, half),
    ]
    copies = [
        pltpu.make_async_copy(
            source.at[pl.ds(start, rows)], out.at[pl.ds(row, rows), pl.ds(col, half)], sems.at[i]
        )
        for i, (source, start, rows, row, col) in enumerate(spots)
    ]
    for copy in copies:
        copy.start()
    for copy in copies:
        copy.wait()


def place_stacked(four, far_a, far_b):
    return pl.pallas_call(
        place_stacked_kernel,
        out_shape=jax.ShapeDtypeStruct((four.shape[0], 2 * four.shape[1]), four.dtype),
        in_specs=[ANY] * 3,
        out_specs=pl.BlockSpec(memory_space=pltpu.VMEM),
        scratch_shapes=[pltpu.SemaphoreType.DMA((6,))],
        name="place_stacked",
    )(four, far_a, far_b)


def rows_of(matrix, grad):
    return lax.dot_general(matrix, grad, (((0,), (0,)), ((), ())), preferred_element_type=F32)


def head_of(ref, half, head):
    return ref[half, 0, :, head * HEAD_DIM : (head + 1) * HEAD_DIM]


def masked(scores):
    n = scores.shape[0]
    rows = lax.broadcasted_iota(jnp.int32, (n, n), 0)
    cols = lax.broadcasted_iota(jnp.int32, (n, n), 1)
    return jnp.where(cols <= rows, scores, NEG)


def self_kernel(core_ref, q_ref, k_ref, v_ref, out_ref, log_ref):
    halves = (core_ref[0], 1 - core_ref[0])
    outs, logs = ([], []), ([], [])
    for head in range(2):
        q = [head_of(q_ref, h, head) * BF(SCALE) for h in halves]
        k = [head_of(k_ref, h, head) for h in halves]
        v = [head_of(v_ref, h, head) for h in halves]
        first = masked(mm_t(q[0], k[0]))
        for half, scores in enumerate([[first], [mm_t(q[1], k[0]), masked(mm_t(q[1], k[1]))]]):
            top = jnp.max(scores[0], axis=-1, keepdims=True)
            if half:
                top = jnp.maximum(top, jnp.max(scores[1], axis=-1, keepdims=True))
            terms = [jnp.exp(part - top) for part in scores]
            total = sum(jnp.sum(part, axis=-1, keepdims=True) for part in terms)
            inverse = 1.0 / total
            out = sum(mm((part * inverse).astype(BF), v[i]) for i, part in enumerate(terms))
            outs[half].append(out.astype(BF))
            logs[half].append(jnp.broadcast_to(top + jnp.log(total), out.shape))
    for half, h in enumerate(halves):
        out_ref[h, 0] = jnp.concatenate(outs[half], axis=1)
        log_ref[h, 0] = jnp.concatenate(logs[half], axis=1)


def self_back_kernel(core_ref, q_ref, k_ref, v_ref, log_ref, grad_ref, out_ref):
    halves = (core_ref[0], 1 - core_ref[0])
    found = [[], [], [], [], [], []]
    for head in range(2):
        q = [head_of(q_ref, h, head) * BF(SCALE) for h in halves]
        k = [head_of(k_ref, h, head) for h in halves]
        ks = [part * BF(SCALE) for part in k]
        v = [head_of(v_ref, h, head) for h in halves]
        log = [head_of(log_ref, h, head)[:, :1] for h in halves]
        grad = [head_of(grad_ref, h, head) for h in halves]
        dq, dk, dv = [0.0, 0.0], [0.0, 0.0], [0.0, 0.0]
        for half, parts in enumerate([(0,), (0, 1)]):
            chances, dps = [], []
            for i in parts:
                scores = mm_t(q[half], k[i])
                if i == half:
                    scores = masked(scores)
                chances.append(jnp.exp(scores - log[half]))
                dps.append(mm_t(grad[half], v[i]))
            dot = sum(
                jnp.sum(c * dp, axis=-1, keepdims=True) for c, dp in zip(chances, dps)
            )
            for i, c, dp in zip(parts, chances, dps):
                ds = (c * (dp - dot)).astype(BF)
                dv[i] += rows_of(c.astype(BF), grad[half])
                dk[i] += rows_of(ds, q[half])
                dq[half] += mm(ds, ks[i])
        for i, part in enumerate(dq + dk + dv):
            found[i].append(part.astype(BF))
    width = out_ref.shape[-1] // 3
    for i in range(3):
        col = pl.multiple_of(i * width + pl.program_id(1) * 2 * HEAD_DIM, 2 * HEAD_DIM)
        for half, h in enumerate(halves):
            out_ref[h, 0, :, pl.ds(col, 2 * HEAD_DIM)] = jnp.concatenate(
                found[2 * i + half], axis=1
            )


def cross_parts(q_ref, k_ref, head):
    cs = slice(head * HEAD_DIM, (head + 1) * HEAD_DIM)
    q = jnp.concatenate([q_ref[0, 0, :, cs], q_ref[1, 0, :, cs]]) * BF(SCALE)
    scores = mm_t(q, k_ref[0, :, cs])
    terms = jnp.exp(scores - jnp.max(scores, axis=-1, keepdims=True))
    return q, terms * (1.0 / jnp.sum(terms, axis=-1, keepdims=True)), cs


def cross_kernel(q_ref, k_ref, v_ref, out_ref):
    outs = []
    for head in range(2):
        _, chances, cs = cross_parts(q_ref, k_ref, head)
        outs.append(mm(chances.astype(BF), v_ref[0, :, cs]).astype(BF))
    out = jnp.concatenate(outs, axis=1)
    n = out.shape[0] // 2
    out_ref[0, 0], out_ref[1, 0] = out[:n], out[n:]


def cross_back_kernel(q_ref, k_ref, v_ref, grad_ref, dq_ref, dkv_ref):
    found = [[], [], []]
    for head in range(2):
        q, chances, cs = cross_parts(q_ref, k_ref, head)
        grad = jnp.concatenate([grad_ref[0, 0, :, cs], grad_ref[1, 0, :, cs]])
        dp = mm_t(grad, v_ref[0, :, cs])
        ds = (chances * (dp - jnp.sum(chances * dp, axis=-1, keepdims=True))).astype(BF)
        found[0].append(mm(ds, k_ref[0, :, cs] * BF(SCALE)).astype(BF))
        found[1].append(rows_of(ds, q).astype(BF))
        found[2].append(rows_of(chances.astype(BF), grad).astype(BF))
    dq, dk, dv = [jnp.concatenate(parts, axis=1) for parts in found]
    n = dq.shape[0] // 2
    dq_ref[0, 0], dq_ref[1, 0] = dq[:n], dq[n:]
    width = dkv_ref.shape[-1] // 2
    for i, part in enumerate([dk, dv]):
        col = pl.multiple_of(i * width + pl.program_id(1) * 2 * HEAD_DIM, 2 * HEAD_DIM)
        dkv_ref[0, :, pl.ds(col, 2 * HEAD_DIM)] = part


def feed_kernel(rows_ref, weight_ref, hidden_ref, slope_ref):
    step = 256

    def body(i, carry):
        at = pl.ds(pl.multiple_of(i * step, step), step)
        hidden_ref[at], slope_ref[at] = gelu_pair(mm(rows_ref[at], weight_ref[...]))
        return carry

    lax.fori_loop(0, rows_ref.shape[0] // step, body, 0, unroll=True)


def feed(rows, weight):
    count, depth = rows.shape
    width = weight.shape[1]
    block = 256
    out = jax.ShapeDtypeStruct((count, width), BF)
    return pl.pallas_call(
        feed_kernel,
        grid=(width // block,),
        in_specs=[
            pl.BlockSpec((count, depth), lambda j: (0, 0)),
            pl.BlockSpec((depth, block), lambda j: (0, j)),
        ],
        out_specs=[pl.BlockSpec((count, block), lambda j: (0, j))] * 2,
        out_shape=[out, out],
        cost_estimate=pl.CostEstimate(
            flops=2 * count * depth * width,
            transcendentals=2 * count * width,
            bytes_accessed=2 * (count * depth + depth * width + 2 * count * width),
        ),
        name="feed",
    )(rows, weight)


def slope_kernel(rows_ref, weight_ref, slope_ref, out_ref):
    step = 256

    def body(i, carry):
        at = pl.ds(pl.multiple_of(i * step, step), step)
        grad = mm(rows_ref[at], weight_ref[...])
        out_ref[at] = (grad * slope_ref[at].astype(F32)).astype(BF)
        return carry

    lax.fori_loop(0, rows_ref.shape[0] // step, body, 0, unroll=True)


def slope_product(rows, weight, slope):
    count, depth = rows.shape
    width = weight.shape[1]
    block = 256
    tall = pl.BlockSpec((count, block), lambda j: (0, j))
    return pl.pallas_call(
        slope_kernel,
        grid=(width // block,),
        in_specs=[
            pl.BlockSpec((count, depth), lambda j: (0, 0)),
            pl.BlockSpec((depth, block), lambda j: (0, j)),
            tall,
        ],
        out_specs=tall,
        out_shape=jax.ShapeDtypeStruct((count, width), BF),
        cost_estimate=pl.CostEstimate(
            flops=2 * count * depth * width,
            transcendentals=0,
            bytes_accessed=2 * (count * depth + depth * width + 2 * count * width),
        ),
        name="slope_product",
    )(rows, weight, slope)


class Whole:
    def __init__(self, dp, tensor):
        self.dp, self.tensor = dp, tensor

    def arrange(self, values):
        return values

    def restore(self, values):
        return values

    def gather_norms(self, packed):
        return lax.all_gather(packed, self.dp, axis=0, tiled=True)

    def gather_first(self, shard):
        return lax.all_gather(shard, self.dp, axis=0, tiled=True)

    def gather_first_set(self, first, second, feed_in, feed_out, rows):
        return first, rows, (second, feed_in, feed_out)

    def place_pieces(self, first):
        return self.gather_first(first)

    def gather_rest(self, rest, value):
        second, feed_in, feed_out = [self.gather_first(shard) for shard in rest]
        return second, feed_in, None, None, (feed_out, None)

    def feed_out(self, pieces):
        return pieces[0]

    def after(self, value, *others):
        return value

    def stage(self, work, *values):
        return work(*values)

    def sends(self, left, right):
        return ()

    def exchange(self, sends):
        return ()

    def merged(self, *sends):
        return ()

    def parted(self, far, *widths):
        return [()] * len(widths)

    def adds(self, *products):
        wholes = [mm_rows(left, right).astype(BF) for left, right, _ in products]
        return jnp.concatenate(wholes, axis=1)

    def second(self, whole):
        return ()

    def closing(self, whole, far):
        return whole

    middle = closing

    def scatter_z(self, whole):
        return lax.psum_scatter(whole, self.dp, scatter_dimension=0, tiled=True)

    def close_middle(self, whole):
        return whole.astype(F32)

    def close_last(self, whole, *widths):
        found, at = [], 0
        for columns in widths:
            found.append(whole[:, at : at + columns].astype(F32))
            at += columns
        return found

    def norm_sums(self, sums):
        sums = jnp.pad(sums.T, ((0, 0), (0, 122))).astype(BF)
        sums = lax.psum_scatter(sums, self.dp, scatter_dimension=0, tiled=True)
        return self.sum_all(sums)[:, :6].T

    def spread(self, rows, clips):
        local = rows.reshape(clips, -1, rows.shape[-1])
        return lax.all_gather(local, self.tensor, axis=1, tiled=True).reshape(-1, rows.shape[-1])

    def sequence(self, rows, clips):
        return rows.reshape(clips, -1, rows.shape[-1])

    def unsequence(self, rows):
        return rows.reshape(-1, rows.shape[-1])

    def clip_rows(self, rows, clips):
        return rows.reshape(clips, -1, rows.shape[-1])

    unclip_rows = unsequence

    def self_attend(self, qkv, clips):
        qkv = self.sequence(qkv, clips)
        cols = qkv.shape[-1] // 3
        q, k, v = qkv[..., :cols], qkv[..., cols : 2 * cols], qkv[..., 2 * cols :]
        att, log_total = attend(q, k, v)
        return self.unsequence(att), (q, k, v, log_total)

    def self_back(self, saved, grad, clips):
        dq, dk, dv = attend_back(*saved, self.sequence(grad, clips))
        return self.unsequence(jnp.concatenate([dq, dk, dv], axis=-1))

    def cross_attend(self, q, memory, clips):
        q = self.clip_rows(q, clips)
        memory = memory.reshape(clips, -1, memory.shape[-1])
        cols = q.shape[-1]
        k, v = memory[..., :cols], memory[..., cols:]
        out, chances = cross_attend(q, k, v)
        return self.unclip_rows(out), (q, k, v, chances)

    def cross_back(self, saved, grad, clips):
        dq, dk, dv = cross_attend_back(*saved, self.clip_rows(grad, clips))
        return self.unclip_rows(dq), self.unsequence(jnp.concatenate([dk, dv], axis=-1))

    def feed(self, rows, weight):
        return gelu_pair(mm(rows, weight))

    def slope_product(self, rows, weight, slope):
        return (mm(rows, weight) * slope.astype(F32)).astype(BF)

    def sum_own(self, left, right, product, clips):
        part = product(left, right).astype(BF).reshape(clips, -1, right_width(product, right))
        own = lax.psum_scatter(part, self.tensor, scatter_dimension=1, tiled=True)
        return own.reshape(-1, part.shape[-1]).astype(F32)

    def sum_all(self, values):
        return lax.psum(values.astype(BF), self.tensor).astype(F32)


def right_width(product, right):
    return right.shape[0] if product is mm_t else right.shape[1]


class Block(Whole):
    def __init__(self, width):
        self.width = width
        self.shard = width // 16
        self.core = lax.axis_index("core")

    def after(self, value, *others):
        return tie(value, others)

    def order(self):
        own_y, own_x = lax.axis_index("y"), lax.axis_index("x")
        place = jnp.arange(self.width, dtype=jnp.int32)
        quarter, rest = place // (4 * self.shard), place % (4 * self.shard)
        z, row = rest // self.shard, rest % self.shard
        y, x = (quarter // 2) ^ own_y, (quarter % 2) ^ own_x
        source = ((z * 2 + y) * 2 + x) * self.shard + row
        return (jnp.arange(self.width, dtype=jnp.int32)[:, None] == source[None, :]).astype(BF)

    def arrange(self, values):
        return mm(values, self.order()).astype(BF)

    def restore(self, values):
        if values.dtype == BF:
            return mm_t(values, self.order()).astype(BF)
        high = lax.reduce_precision(values, 8, 7)
        low = (values - high).astype(BF)
        order = self.order()
        return mm_t(high.astype(BF), order) + mm_t(low, order)

    def x(self, v):
        return lax.ppermute(v, "x", SWAP)

    def y(self, v):
        return lax.ppermute(v, "y", SWAP)

    def other(self, v):
        return lax.ppermute(v, "core", SWAP)

    def gather_norms(self, packed):
        pair = jnp.stack([packed, lax.ppermute(packed, "z", [(0, 1), (1, 0), (2, 3), (3, 2)])])
        far = lax.ppermute(pair, "z", [(0, 2), (1, 3), (2, 0), (3, 1)])
        own = lax.axis_index("z")
        four = jnp.concatenate([pair, far])
        four = jnp.stack([lax.dynamic_index_in_dim(four, own ^ p, 0, False) for p in range(4)])
        two = jnp.stack([four, self.x(four)])
        whole = jnp.stack([two, self.y(two)])
        return whole.reshape(self.width, packed.shape[-1])

    def halves(self, shard):
        half = shard.shape[1] // 256 * 128
        return shard[:, :half], shard[:, half:]

    def gather_first_set(self, first, second, feed_in, feed_out, rows):
        opened = []
        for shard in (feed_in, feed_out):
            a, b = self.halves(shard)
            opened.append(jnp.stack([a, self.x(a), b, self.y(b)]))
        rows, opened = lax.optimization_barrier((rows, opened))
        sets = [lax.all_gather(shard, "z", axis=0, tiled=True) for shard in (first, second)]
        feeds = [lax.all_gather(four, "z", axis=1, tiled=True) for four in opened]
        pieces, last, _ = self.gather_pieces(sets[0], rows)
        pieces_next = self.gather_pieces(sets[1], last)
        return pieces, rows, (pieces_next, feeds)

    def gather_pieces(self, four, last):
        a, b = self.halves(tie(four, last))
        xa, yb, ya, xb = self.x(a), self.y(b), self.y(a), self.x(b)
        far_a, far_b = self.y(xa), self.x(yb)
        return (four, xa, ya, far_a, xb, yb, far_b), (far_a, far_b, ya, xb), (xa, yb)

    def place_pieces(self, pieces):
        four, xa, ya, far_a, xb, yb, far_b = pieces
        n, half = xa.shape
        return place(
            [
                (four, 0, 0),
                (xa, n, 0),
                (ya, 2 * n, 0),
                (far_a, 3 * n, 0),
                (xb, n, half),
                (yb, 2 * n, half),
                (far_b, 3 * n, half),
            ],
            (4 * n, four.shape[1]),
        )

    def gather_rest(self, rest, value):
        (pieces, last, _), feeds = rest
        feeds[0] = tie(feeds[0], value)
        in_sides = feeds[0][:2], feeds[0][2:]
        a, b = tie(in_sides, last)
        in_far = self.y(a), self.x(b)
        w_cross = self.place_pieces(pieces)
        w_in = self.place_feed(feeds[0], in_far)
        out_sides = feeds[1][:2], feeds[1][2:]
        a, b = tie(out_sides, in_far)
        return w_cross, w_in, in_far, out_sides, (feeds[1], (self.y(a), self.x(b)))

    def place_feed(self, four, far):
        _, n, half = four.shape
        return place_stacked(
            four.reshape(4 * n, half), far[0].reshape(2 * n, half), far[1].reshape(2 * n, half)
        )

    def feed_out(self, pieces):
        return self.place_feed(*pieces)

    def stage(self, work, *values):
        shapes = jax.eval_shape(work, *values)

        def nothing(*_):
            return jax.tree.map(lambda leaf: jnp.zeros(leaf.shape, leaf.dtype), shapes)

        return lax.cond(self.core < 2, work, nothing, *values)

    def sends(self, left, right):
        n, half = self.width // 4, right.shape[1] // 256 * 128
        far = jnp.concatenate([left[:, n : 2 * n], left[:, 3 * n :]], axis=1)
        return (
            mm_rows(left[:, 2 * n :], right[:, :half]).astype(BF),
            mm_rows(far, right[:, half:]).astype(BF),
        )

    def exchange(self, sends):
        return self.y(sends[0]), self.x(sends[1])

    def merged(self, *sends):
        return [jnp.concatenate(side, axis=1) for side in zip(*sends)]

    def parted(self, far, *widths):
        halves = [width // 256 * 128 for width in widths]
        ends = [sum(halves[: i + 1]) for i in range(len(halves) - 1)]
        lefts = jnp.split(far[0], ends, axis=1)
        halves = [width - half for width, half in zip(widths, halves)]
        ends = [sum(halves[: i + 1]) for i in range(len(halves) - 1)]
        return list(zip(lefts, jnp.split(far[1], ends, axis=1)))

    def adds(self, *products):
        n, parts = self.width // 4, []
        for left, right, (far_y, far_x) in products:
            half = right.shape[1] // 256 * 128
            first = (mm_rows(left[:, : 2 * n], right[:, :half]) + far_y.astype(F32)).astype(BF)
            near = jnp.concatenate([left[:, :n], left[:, 2 * n : 3 * n]], axis=1)
            last = (mm_rows(near, right[:, half:]) + far_x.astype(F32)).astype(BF)
            parts.append((first[:n], first[n:], last[:n], last[n:]))
        return [jnp.concatenate(part, axis=1) for part in zip(*parts)]

    def middle(self, parts, _):
        return jnp.stack(parts)

    def second(self, parts):
        return self.x(parts[1]), self.y(parts[3])

    def closing(self, parts, far):
        pairs = zip((parts[0], parts[2]), far)
        return jnp.stack([(own.astype(F32) + other.astype(F32)).astype(BF) for own, other in pairs])

    def scatter_z(self, parts):
        return lax.psum_scatter(parts, "z", scatter_dimension=1, tiled=True)

    def close_middle(self, four):
        left = four[0].astype(F32) + self.x(four[1]).astype(F32)
        right = four[2].astype(F32) + self.y(four[3]).astype(F32)
        return jnp.concatenate([left, right], axis=1)

    def close_last(self, both, *widths):
        found, left, right = [], 0, 0
        for columns in widths:
            a = columns // 256 * 128
            b = columns - a
            found.append(
                jnp.concatenate([both[0, :, left : left + a], both[1, :, right : right + b]], axis=1)
            )
            left, right = left + a, right + b
        return [part.astype(F32) for part in found]

    def norm_sums(self, sums):
        n = self.width // 4
        sums = self.sum_all(jnp.pad(sums.T, ((0, 0), (0, 122))))
        sums = sums[: 2 * n] + self.y(sums[2 * n :].astype(BF)).astype(F32)
        sums = sums[:n] + self.x(sums[n:].astype(BF)).astype(F32)
        own = lax.axis_index("z")
        for step, pairs, side in (
            (n // 2, [(0, 2), (1, 3), (2, 0), (3, 1)], own // 2),
            (n // 4, [(0, 1), (1, 0), (2, 3), (3, 2)], own % 2),
        ):
            near = lax.dynamic_slice_in_dim(sums, side * step, step)
            away = lax.dynamic_slice_in_dim(sums, (1 - side) * step, step)
            sums = near + lax.ppermute(away.astype(BF), "z", pairs).astype(F32)
        return sums[:, :6].T

    def spread(self, rows, clips):
        return jnp.concatenate([rows, self.other(rows)])

    def self_attend(self, qkv, clips):
        cols = qkv.shape[-1] // 3
        steps = cols // (2 * HEAD_DIM)
        view = qkv.reshape(2, clips, -1, qkv.shape[-1])
        frames = view.shape[2]

        def block(part):
            return pl.BlockSpec(
                (2, 1, frames, 2 * HEAD_DIM), lambda c, j, _: (0, c, 0, part * steps + j)
            )

        shape = (2, clips, frames, cols)
        core = self.core.reshape(1).astype(jnp.int32)
        scores = clips * steps * 2 * 3 * frames * frames
        out, log_total = pl.pallas_call(
            self_kernel,
            grid_spec=pltpu.PrefetchScalarGridSpec(
                num_scalar_prefetch=1,
                grid=(clips, steps),
                in_specs=[block(0), block(1), block(2)],
                out_specs=[block(0), block(0)],
            ),
            out_shape=[jax.ShapeDtypeStruct(shape, BF), jax.ShapeDtypeStruct(shape, F32)],
            cost_estimate=pl.CostEstimate(
                flops=4 * scores * HEAD_DIM,
                transcendentals=scores,
                bytes_accessed=2 * qkv.size + 6 * qkv.size // 3,
            ),
            name="self_attend",
        )(core, view, view, view)
        return out.reshape(-1, cols), (core, view, log_total)

    def self_back(self, saved, grad, clips):
        core, view, log_total = saved
        cols = view.shape[-1] // 3
        steps = cols // (2 * HEAD_DIM)
        frames = view.shape[2]

        def block(part):
            return pl.BlockSpec(
                (2, 1, frames, 2 * HEAD_DIM), lambda c, j, _: (0, c, 0, part * steps + j)
            )

        scores = clips * steps * 2 * 3 * frames * frames
        out = pl.pallas_call(
            self_back_kernel,
            grid_spec=pltpu.PrefetchScalarGridSpec(
                num_scalar_prefetch=1,
                grid=(clips, steps),
                in_specs=[block(0), block(1), block(2), block(0), block(0)],
                out_specs=pl.BlockSpec((2, 1, frames, 3 * cols), lambda c, j, _: (0, c, 0, 0)),
            ),
            out_shape=jax.ShapeDtypeStruct(view.shape, BF),
            cost_estimate=pl.CostEstimate(
                flops=10 * scores * HEAD_DIM,
                transcendentals=scores,
                bytes_accessed=4 * view.size + 6 * view.size // 3,
            ),
            name="self_back",
        )(core, view, view, view, log_total, grad.reshape(2, clips, frames, cols))
        return out.reshape(-1, 3 * cols)

    def cross_specs(self, q, clips, texts):
        cols = q.shape[-1]
        steps = cols // (2 * HEAD_DIM)
        view = q.reshape(2, clips, -1, cols)
        frames = view.shape[2]
        wide = pl.BlockSpec((2, 1, frames, 2 * HEAD_DIM), lambda c, j: (0, c, 0, j))

        def block(part):
            return pl.BlockSpec((1, texts, 2 * HEAD_DIM), lambda c, j: (c, 0, part * steps + j))

        return view, (clips, steps), wide, block, clips * 2 * frames * cols * texts

    def cross_attend(self, q, memory, clips):
        memory = memory.reshape(clips, -1, memory.shape[-1])
        view, grid, wide, block, work = self.cross_specs(q, clips, memory.shape[1])
        out = pl.pallas_call(
            cross_kernel,
            grid=grid,
            in_specs=[wide, block(0), block(1)],
            out_specs=wide,
            out_shape=jax.ShapeDtypeStruct(view.shape, BF),
            cost_estimate=pl.CostEstimate(
                flops=4 * work, transcendentals=work // HEAD_DIM, bytes_accessed=4 * q.size
            ),
            name="cross_attend",
        )(view, memory, memory)
        return out.reshape(q.shape), (q, memory)

    def cross_back(self, saved, grad, clips):
        q, memory = saved
        texts = memory.shape[1]
        view, grid, wide, block, work = self.cross_specs(q, clips, texts)
        dq, dkv = pl.pallas_call(
            cross_back_kernel,
            grid=grid,
            in_specs=[wide, block(0), block(1), wide],
            out_specs=[
                wide,
                pl.BlockSpec((1, texts, memory.shape[-1]), lambda c, j: (c, 0, 0)),
            ],
            out_shape=[
                jax.ShapeDtypeStruct(view.shape, BF),
                jax.ShapeDtypeStruct(memory.shape, BF),
            ],
            cost_estimate=pl.CostEstimate(
                flops=10 * work, transcendentals=work // HEAD_DIM, bytes_accessed=6 * q.size
            ),
            name="cross_back",
        )(view, memory, memory, grad.reshape(view.shape))
        return dq.reshape(q.shape), dkv.reshape(-1, memory.shape[-1])

    def feed(self, rows, weight):
        return feed(rows, weight)

    def slope_product(self, rows, weight, slope):
        return slope_product(rows, weight, slope)

    def sum_own(self, left, right, product, clips):
        n = left.shape[0] // 2
        far = self.other(product(left[n:], right).astype(BF))
        return product(left[:n], right) + far.astype(F32)

    def sum_all(self, values):
        return values + self.other(values.astype(BF)).astype(F32)


def layer(
    comm,
    frames,
    text_states,
    norm_gain,
    norm_shift,
    self_project,
    self_output,
    cross_query,
    cross_memory,
    cross_output,
    feed_input,
    feed_output,
    upstream,
):
    clips, own_frames, width = frames.shape
    texts = text_states.shape[1]
    cols = cross_query.shape[1]
    own_rows = clips * own_frames

    def catenate(parts):
        return jnp.concatenate(parts, axis=1)

    norms = comm.gather_norms(
        jnp.pad(jnp.concatenate([norm_gain, norm_shift]).T, ((0, 0), (0, 122)))
    )
    norms = norms.T.astype(F32)
    gain, shift = norms[0:3], norms[3:6]
    first_set = catenate([self_project[0], self_project[1], self_project[2]])
    second_set = catenate(
        [self_output.T, cross_query, cross_memory[0], cross_memory[1], cross_output.T]
    )
    values0 = comm.arrange(frames.reshape(own_rows, width)).astype(F32)
    stats0 = norm_stats(values0)
    own_n1 = norm_apply(values0, stats0, gain[0], shift[0])
    pieces, own_n1, rest = comm.gather_first_set(
        first_set, second_set, feed_input, feed_output.T, own_n1
    )
    up = comm.arrange(upstream.reshape(own_rows, width))
    text = comm.arrange(text_states.reshape(clips * texts, width))
    up_all = comm.spread(up, clips)

    n1 = comm.spread(own_n1, clips)

    def split_cross(weights):
        return jnp.split(weights, [cols, 2 * cols, 4 * cols], axis=1)

    def stage_self(pieces, n1):
        w_self = comm.place_pieces(pieces)
        return w_self, comm.self_attend(mm(n1, w_self).astype(BF), clips)

    w_self, (att, self_saved) = comm.stage(stage_self, pieces, n1)
    w_cross, w_in, mark_in, mark_out, out_pieces = comm.gather_rest(rest, att)

    def stage0(values0, att, w_cross, text):
        w_so, w_cq, w_cm, w_co = split_cross(w_cross)
        values1 = values0 + comm.sum_own(att, w_so, mm_t, clips)
        stats1 = norm_stats(values1)
        n2 = comm.spread(norm_apply(values1, stats1, gain[1], shift[1]), clips)
        cross, saved = comm.cross_attend(
            mm(n2, w_cq).astype(BF), mm(text, w_cm).astype(BF), clips
        )
        values2 = values1 + comm.sum_own(cross, w_co, mm_t, clips)
        stats2 = norm_stats(values2)
        n3 = comm.spread(norm_apply(values2, stats2, gain[2], shift[2]), clips)
        return values1, stats1, n2, cross, saved, values2, stats2, n3

    values1, stats1, n2, cross, cross_saved, values2, stats2, n3 = comm.stage(
        stage0, values0, att, w_cross, text
    )
    n3 = comm.after(n3, mark_in, mark_out)
    hidden, slope = comm.feed(n3, w_in)
    send_out = comm.sends(up_all, hidden)
    hidden, slope = comm.after((hidden, slope), out_pieces[1], send_out)
    far_out = comm.exchange(send_out)

    def stage1(pieces, rows, slope, n3, w_in):
        w_out = comm.feed_out(pieces)
        pre_grad = comm.slope_product(rows, w_out, slope)
        sends = [comm.sends(n3, part) for part in jnp.split(pre_grad, 2, axis=1)]
        return w_out, pre_grad, sends, comm.sum_own(pre_grad, w_in, mm_t, clips)

    w_out, pre_grad, send_in, e3 = comm.stage(stage1, out_pieces, up_all, slope, n3, w_in)
    e3, send_in = comm.after((e3, send_in), far_out)
    in_parts = jnp.split(pre_grad, 2, axis=1)
    far_in = [comm.exchange(send_in[0])]

    def stage2(rows, hidden, far, e3, values2, stats2, own):
        sent = comm.middle(comm.adds((rows, hidden, far)), None)
        grads = norm_back(values2, stats2, gain[2], e3)
        r2 = own.astype(F32) + grads[0]
        return sent, r2, r2.astype(BF), grads[1], grads[2]

    sent_out, r2, r2_own, gain2, shift2 = comm.stage(
        stage2, up_all, hidden, far_out, e3, values2, stats2, up
    )
    sent_out, r2_own, send_b = comm.after((sent_out, r2_own, send_in[1:]), far_in[0])
    half_out = comm.scatter_z(sent_out)
    far_in += [comm.exchange(sends) for sends in send_b]

    def stage3(r2_own, saved, w_cross, n2, cross, text):
        w_co = split_cross(w_cross)[3]
        r2_all = comm.spread(r2_own, clips)
        dcq, dmem = comm.cross_back(saved, mm(r2_all, w_co).astype(BF), clips)
        pairs = (n2, dcq), (r2_all, cross), (text, dmem)
        return r2_all, dcq, dmem, comm.merged(*[comm.sends(*pair) for pair in pairs])

    r2_all, dcq, dmem, send_cross = comm.stage(
        stage3, r2_own, cross_saved, w_cross, n2, cross, text
    )
    dcq, send_cross = comm.after((dcq, send_cross), far_in)
    far_cross = comm.exchange(send_cross)
    cross_pairs = (n2, dcq), (r2_all, cross), (text, dmem)

    def stage4(n3, parts, far, dcq, w_cross, values1, stats1, r2):
        w_so, w_cq, *_ = split_cross(w_cross)
        in_sums = comm.adds(*[(n3, part, one) for part, one in zip(parts, far)])
        e2 = comm.sum_own(dcq, w_cq, mm_t, clips)
        grads = norm_back(values1, stats1, gain[1], e2)
        r1 = r2 + grads[0]
        r1_all = comm.spread(r1.astype(BF), clips)
        return in_sums, r1, r1_all, mm(r1_all, w_so).astype(BF), grads[1], grads[2]

    in_sums, r1, r1_all, datt, gain1, shift1 = comm.stage(
        stage4, n3, in_parts, tuple(far_in), dcq, w_cross, values1, stats1, r2
    )
    in_sums, datt = comm.after((in_sums, datt), far_cross, half_out)
    in_second = comm.second(in_sums)

    def stage5(pairs, far, r1_all, att):
        far = comm.parted(far, cols, cols, 2 * cols)
        sums = comm.adds(*[(*pair, one) for pair, one in zip(pairs, far)])
        return sums, comm.sends(r1_all, att)

    cross_sums, send_so = comm.stage(stage5, cross_pairs, far_cross, r1_all, att)
    cross_sums, send_so, datt, in_sums = comm.after(
        (cross_sums, send_so, datt, in_sums), in_second
    )
    cross_second = comm.second(cross_sums)
    far_so = comm.exchange(send_so)
    half_in = comm.scatter_z(comm.closing(in_sums, in_second))

    def stage_back(saved, datt, n1):
        dqkv = comm.self_back(saved, datt, clips)
        return dqkv, comm.sends(n1, dqkv)

    dqkv, send_self = comm.stage(stage_back, self_saved, datt, n1)
    dmem, hidden, send_self, cross_sums, dqkv = comm.after(
        (dmem, hidden, send_self, cross_sums, dqkv), cross_second, far_so
    )
    far_self = comm.exchange(send_self)
    half_cross = comm.scatter_z(comm.closing(cross_sums, cross_second))

    def stage6(dmem, w_cross, values2, hidden, w_out):
        w_cm = split_cross(w_cross)[2]
        text_grad = comm.sum_all(mm_t(dmem, w_cm))
        layer_out = (values2 + comm.sum_own(hidden, w_out, mm_t, clips)).astype(BF)
        return comm.restore(text_grad), comm.restore(layer_out)

    text_grad, layer_out = comm.stage(stage6, dmem, w_cross, values2, hidden, w_out)
    text_grad, layer_out, dqkv = comm.after((text_grad, layer_out, dqkv), far_self, half_in)
    self_sums = comm.adds((r1_all, att, far_so), (n1, dqkv, far_self))
    dqkv = comm.after(dqkv, self_sums)
    self_second = comm.second(self_sums)

    def stage7(dqkv, w_self, values0, stats0, r1):
        e1 = comm.sum_own(dqkv, w_self, mm_t, clips)
        grads = norm_back(values0, stats0, gain[0], e1)
        return comm.restore(r1 + grads[0]), grads[1], grads[2]

    input_grad, gain0, shift0 = comm.stage(stage7, dqkv, w_self, values0, stats0, r1)
    input_grad, gain0 = comm.after((input_grad, gain0), self_second, half_cross)
    half_self = comm.scatter_z(comm.closing(self_sums, self_second))
    norm_grad = comm.norm_sums(jnp.stack([gain0, gain1, gain2, shift0, shift1, shift2]))
    input_grad = input_grad.reshape(clips, own_frames, width)
    text_grad = text_grad.reshape(clips, texts, width)
    layer_out = layer_out.reshape(clips, own_frames, width)
    grad_out = comm.close_middle(half_out)
    grad_in = catenate(comm.close_last(half_in, *[part.shape[1] for part in in_parts]))
    grad_cq, grad_co, grad_cm = comm.close_last(half_cross, cols, cols, 2 * cols)
    grad_so, grad_self = comm.close_last(half_self, cols, 3 * cols)
    return (
        layer_out,
        input_grad,
        text_grad,
        norm_grad[0:3],
        norm_grad[3:6],
        jnp.stack([grad_self[:, i * cols : (i + 1) * cols] for i in range(3)]),
        grad_so.T,
        grad_cq,
        jnp.stack([grad_cm[:, :cols], grad_cm[:, cols:]]),
        grad_co.T,
        grad_in,
        grad_out.T,
    )


def specs(dp, tensor):
    in_specs = (
        P(dp, tensor, None),
        P(dp, None, None),
        P(None, dp),
        P(None, dp),
        P(None, dp, tensor),
        P(tensor, dp),
        P(dp, tensor),
        P(None, dp, tensor),
        P(tensor, dp),
        P(dp, tensor),
        P(tensor, dp),
        P(dp, tensor, None),
    )
    out_specs = (
        P(dp, tensor, None),
        P(dp, tensor, None),
        P(dp, None, None),
        P(None, dp),
        P(None, dp),
        P(None, dp, tensor),
        P(tensor, dp),
        P(dp, tensor),
        P(None, dp, tensor),
        P(tensor, dp),
        P(dp, tensor),
        P(tensor, dp),
    )
    return in_specs, out_specs


def solution(mesh):
    if mesh.shape["dp"] == 16 and mesh.shape["tensor"] == 2:
        mesh = Mesh(mesh.devices.reshape(4, 2, 2, 2), ("z", "y", "x", "core"))
        in_specs, out_specs = specs(("z", "y", "x"), "core")

        def per_device(frames, *rest):
            return layer(Block(frames.shape[-1]), frames, *rest)
    else:
        in_specs, out_specs = specs("dp", "tensor")

        def per_device(frames, *rest):
            return layer(Whole("dp", "tensor"), frames, *rest)

    return jax.shard_map(
        per_device, mesh=mesh, in_specs=in_specs, out_specs=out_specs, check_vma=False
    )
```

```python
import math

import jax
import jax.numpy as jnp
from jax import lax
from jax.experimental import pallas as pl
from jax.experimental.pallas import tpu as pltpu
from jax.sharding import Mesh
from jax.sharding import PartitionSpec as P

HEAD_DIM = 64
EPS = 1e-05
BF = jnp.bfloat16
F32 = jnp.float32
SWAP = [(0, 1), (1, 0)]


def mm(left, right):
    return jnp.dot(left, right, preferred_element_type=F32)


def mm_t(left, right):
    return lax.dot_general(left, right, (((1,), (1,)), ((), ())), preferred_element_type=F32)


def mm_rows(left, right):
    return lax.dot_general(left, right, (((0,), (0,)), ((), ())), preferred_element_type=F32)


def tie(value, *others):
    return lax.optimization_barrier((value, others))[0]


def norm_stats(values):
    mean = jnp.mean(values, axis=-1, keepdims=True)
    centred = values - mean
    inv = lax.rsqrt(jnp.mean(centred * centred, axis=-1, keepdims=True) + EPS)
    return mean, inv


def norm_apply(values, stats, gain, shift):
    return ((values - stats[0]) * stats[1] * gain + shift).astype(BF)


def norm_back(values, stats, gain, grad):
    xhat = (values - stats[0]) * stats[1]
    scaled = grad * gain
    part = jnp.mean(scaled, axis=-1, keepdims=True)
    cross = jnp.mean(scaled * xhat, axis=-1, keepdims=True)
    value_grad = (scaled - part - xhat * cross) * stats[1]
    return value_grad, jnp.sum(grad * xhat, axis=0), jnp.sum(grad, axis=0)


def gelu_pair(pre):
    phi = 0.5 * (1.0 + lax.erf(pre * (1.0 / math.sqrt(2.0))))
    dens = jnp.exp(-0.5 * pre * pre) * (1.0 / math.sqrt(2.0 * math.pi))
    return (pre * phi).astype(BF), (phi + pre * dens).astype(BF)


def heads(matrix):
    return matrix.reshape(*matrix.shape[:-1], matrix.shape[-1] // HEAD_DIM, HEAD_DIM)


def flat(matrix):
    return matrix.reshape(*matrix.shape[:-2], -1)


SCALE = 1.0 / math.sqrt(HEAD_DIM)


def causal_scores(q, k):
    scores = jnp.einsum("bqhd,bkhd->bhqk", heads(q), heads(k), preferred_element_type=F32) * SCALE
    n = q.shape[1]
    allowed = jnp.arange(n)[None, :] <= jnp.arange(n)[:, None]
    return jnp.where(allowed, scores, -1e30)


def attend(q, k, v):
    scores = causal_scores(q, k)
    top = jnp.max(scores, axis=-1, keepdims=True)
    terms = jnp.exp(scores - top)
    total = jnp.sum(terms, axis=-1, keepdims=True)
    out = jnp.einsum(
        "bhqk,bkhd->bqhd", (terms / total).astype(BF), heads(v), preferred_element_type=F32
    )
    return flat(out).astype(BF), top + jnp.log(total)


def probs_back(chances, dp, q, k, grad):
    dot = jnp.sum(chances * dp, axis=-1, keepdims=True)
    ds = (chances * (dp - dot)).astype(BF)
    dv = jnp.einsum("bhqk,bqhd->bkhd", chances.astype(BF), grad, preferred_element_type=F32)
    dq = jnp.einsum("bhqk,bkhd->bqhd", ds, heads(k), preferred_element_type=F32) * SCALE
    dk = jnp.einsum("bhqk,bqhd->bkhd", ds, heads(q), preferred_element_type=F32) * SCALE
    return flat(dq).astype(BF), flat(dk).astype(BF), flat(dv).astype(BF)


def attend_back(q, k, v, log_total, grad):
    chances = jnp.exp(causal_scores(q, k) - log_total)
    grad = heads(grad)
    dp = jnp.einsum("bqhd,bkhd->bhqk", grad, heads(v), preferred_element_type=F32)
    return probs_back(chances, dp, q, k, grad)


def cross_attend(q, k, v):
    scores = jnp.einsum("bqhd,bkhd->bhqk", heads(q), heads(k), preferred_element_type=F32) * SCALE
    chances = jax.nn.softmax(scores, axis=-1)
    out = jnp.einsum("bhqk,bkhd->bqhd", chances.astype(BF), heads(v), preferred_element_type=F32)
    return flat(out).astype(BF), chances


def cross_attend_back(q, k, v, chances, grad):
    grad = heads(grad)
    dp = jnp.einsum("bqhd,bkhd->bhqk", grad, heads(v), preferred_element_type=F32)
    return probs_back(chances, dp, q, k, grad)

ANY = pl.BlockSpec(memory_space=pl.ANY)
NEG = -1e30


def place_kernel(*refs, spots):
    sources, out, sems = refs[: len(spots)], refs[len(spots)], refs[len(spots) + 1]
    copies = []
    for i, (source, (row, col)) in enumerate(zip(sources, spots)):
        rows, cols = source.shape
        copies.append(
            pltpu.make_async_copy(
                source, out.at[pl.ds(row, rows), pl.ds(col, cols)], sems.at[i]
            )
        )
    for copy in copies:
        copy.start()
    for copy in copies:
        copy.wait()


def place(pieces, shape):
    spots = tuple((row, col) for _, row, col in pieces)
    return pl.pallas_call(
        lambda *refs: place_kernel(*refs, spots=spots),
        out_shape=jax.ShapeDtypeStruct(shape, pieces[0][0].dtype),
        in_specs=[ANY] * len(pieces),
        out_specs=pl.BlockSpec(memory_space=pltpu.VMEM),
        scratch_shapes=[pltpu.SemaphoreType.DMA((len(pieces),))],
        name="place",
    )(*[piece for piece, _, _ in pieces])


def place_stacked_kernel(four, far_a, far_b, out, sems):
    n, half = four.shape[0] // 4, four.shape[1]
    spots = [
        (four, 0, 2 * n, 0, 0),
        (far_a, n, n, 2 * n, 0),
        (far_a, 0, n, 3 * n, 0),
        (four, 2 * n, n, 0, half),
        (far_b, 0, 2 * n, n, half),
        (four, 3 * n, n, 3 * n, half),
    ]
    copies = [
        pltpu.make_async_copy(
            source.at[pl.ds(start, rows)], out.at[pl.ds(row, rows), pl.ds(col, half)], sems.at[i]
        )
        for i, (source, start, rows, row, col) in enumerate(spots)
    ]
    for copy in copies:
        copy.start()
    for copy in copies:
        copy.wait()


def place_stacked(four, far_a, far_b):
    return pl.pallas_call(
        place_stacked_kernel,
        out_shape=jax.ShapeDtypeStruct((four.shape[0], 2 * four.shape[1]), four.dtype),
        in_specs=[ANY] * 3,
        out_specs=pl.BlockSpec(memory_space=pltpu.VMEM),
        scratch_shapes=[pltpu.SemaphoreType.DMA((6,))],
        name="place_stacked",
    )(four, far_a, far_b)


def rows_of(matrix, grad):
    return lax.dot_general(matrix, grad, (((0,), (0,)), ((), ())), preferred_element_type=F32)


def head_of(ref, half, head):
    return ref[half, 0, :, head * HEAD_DIM : (head + 1) * HEAD_DIM]


def masked(scores):
    n = scores.shape[0]
    rows = lax.broadcasted_iota(jnp.int32, (n, n), 0)
    cols = lax.broadcasted_iota(jnp.int32, (n, n), 1)
    return jnp.where(cols <= rows, scores, NEG)


def self_kernel(core_ref, q_ref, k_ref, v_ref, out_ref, log_ref):
    halves = (core_ref[0], 1 - core_ref[0])
    outs, logs = ([], []), ([], [])
    for head in range(2):
        q = [head_of(q_ref, h, head) * BF(SCALE) for h in halves]
        k = [head_of(k_ref, h, head) for h in halves]
        v = [head_of(v_ref, h, head) for h in halves]
        first = masked(mm_t(q[0], k[0]))
        for half, scores in enumerate([[first], [mm_t(q[1], k[0]), masked(mm_t(q[1], k[1]))]]):
            top = jnp.max(scores[0], axis=-1, keepdims=True)
            if half:
                top = jnp.maximum(top, jnp.max(scores[1], axis=-1, keepdims=True))
            terms = [jnp.exp(part - top) for part in scores]
            total = sum(jnp.sum(part, axis=-1, keepdims=True) for part in terms)
            inverse = 1.0 / total
            out = sum(mm((part * inverse).astype(BF), v[i]) for i, part in enumerate(terms))
            outs[half].append(out.astype(BF))
            logs[half].append(jnp.broadcast_to(top + jnp.log(total), out.shape))
    for half, h in enumerate(halves):
        out_ref[h, 0] = jnp.concatenate(outs[half], axis=1)
        log_ref[h, 0] = jnp.concatenate(logs[half], axis=1)


def self_back_kernel(core_ref, q_ref, k_ref, v_ref, log_ref, grad_ref, out_ref):
    halves = (core_ref[0], 1 - core_ref[0])
    found = [[], [], [], [], [], []]
    for head in range(2):
        q = [head_of(q_ref, h, head) * BF(SCALE) for h in halves]
        k = [head_of(k_ref, h, head) for h in halves]
        ks = [part * BF(SCALE) for part in k]
        v = [head_of(v_ref, h, head) for h in halves]
        log = [head_of(log_ref, h, head)[:, :1] for h in halves]
        grad = [head_of(grad_ref, h, head) for h in halves]
        dq, dk, dv = [0.0, 0.0], [0.0, 0.0], [0.0, 0.0]
        for half, parts in enumerate([(0,), (0, 1)]):
            chances, dps = [], []
            for i in parts:
                scores = mm_t(q[half], k[i])
                if i == half:
                    scores = masked(scores)
                chances.append(jnp.exp(scores - log[half]))
                dps.append(mm_t(grad[half], v[i]))
            dot = sum(
                jnp.sum(c * dp, axis=-1, keepdims=True) for c, dp in zip(chances, dps)
            )
            for i, c, dp in zip(parts, chances, dps):
                ds = (c * (dp - dot)).astype(BF)
                dv[i] += rows_of(c.astype(BF), grad[half])
                dk[i] += rows_of(ds, q[half])
                dq[half] += mm(ds, ks[i])
        for i, part in enumerate(dq + dk + dv):
            found[i].append(part.astype(BF))
    width = out_ref.shape[-1] // 3
    for i in range(3):
        col = pl.multiple_of(i * width + pl.program_id(1) * 2 * HEAD_DIM, 2 * HEAD_DIM)
        for half, h in enumerate(halves):
            out_ref[h, 0, :, pl.ds(col, 2 * HEAD_DIM)] = jnp.concatenate(
                found[2 * i + half], axis=1
            )


def cross_parts(q_ref, k_ref, head):
    cs = slice(head * HEAD_DIM, (head + 1) * HEAD_DIM)
    q = jnp.concatenate([q_ref[0, 0, :, cs], q_ref[1, 0, :, cs]]) * BF(SCALE)
    scores = mm_t(q, k_ref[0, :, cs])
    terms = jnp.exp(scores - jnp.max(scores, axis=-1, keepdims=True))
    return q, terms * (1.0 / jnp.sum(terms, axis=-1, keepdims=True)), cs


def cross_kernel(q_ref, k_ref, v_ref, out_ref):
    outs = []
    for head in range(2):
        _, chances, cs = cross_parts(q_ref, k_ref, head)
        outs.append(mm(chances.astype(BF), v_ref[0, :, cs]).astype(BF))
    out = jnp.concatenate(outs, axis=1)
    n = out.shape[0] // 2
    out_ref[0, 0], out_ref[1, 0] = out[:n], out[n:]


def cross_back_kernel(q_ref, k_ref, v_ref, grad_ref, dq_ref, dkv_ref):
    found = [[], [], []]
    for head in range(2):
        q, chances, cs = cross_parts(q_ref, k_ref, head)
        grad = jnp.concatenate([grad_ref[0, 0, :, cs], grad_ref[1, 0, :, cs]])
        dp = mm_t(grad, v_ref[0, :, cs])
        ds = (chances * (dp - jnp.sum(chances * dp, axis=-1, keepdims=True))).astype(BF)
        found[0].append(mm(ds, k_ref[0, :, cs] * BF(SCALE)).astype(BF))
        found[1].append(rows_of(ds, q).astype(BF))
        found[2].append(rows_of(chances.astype(BF), grad).astype(BF))
    dq, dk, dv = [jnp.concatenate(parts, axis=1) for parts in found]
    n = dq.shape[0] // 2
    dq_ref[0, 0], dq_ref[1, 0] = dq[:n], dq[n:]
    width = dkv_ref.shape[-1] // 2
    for i, part in enumerate([dk, dv]):
        col = pl.multiple_of(i * width + pl.program_id(1) * 2 * HEAD_DIM, 2 * HEAD_DIM)
        dkv_ref[0, :, pl.ds(col, 2 * HEAD_DIM)] = part


def feed_kernel(rows_ref, weight_ref, hidden_ref, slope_ref):
    step = 256

    def body(i, carry):
        at = pl.ds(pl.multiple_of(i * step, step), step)
        hidden_ref[at], slope_ref[at] = gelu_pair(mm(rows_ref[at], weight_ref[...]))
        return carry

    lax.fori_loop(0, rows_ref.shape[0] // step, body, 0, unroll=True)


def feed(rows, weight):
    count, depth = rows.shape
    width = weight.shape[1]
    block = 256
    out = jax.ShapeDtypeStruct((count, width), BF)
    return pl.pallas_call(
        feed_kernel,
        grid=(width // block,),
        in_specs=[
            pl.BlockSpec((count, depth), lambda j: (0, 0)),
            pl.BlockSpec((depth, block), lambda j: (0, j)),
        ],
        out_specs=[pl.BlockSpec((count, block), lambda j: (0, j))] * 2,
        out_shape=[out, out],
        cost_estimate=pl.CostEstimate(
            flops=2 * count * depth * width,
            transcendentals=2 * count * width,
            bytes_accessed=2 * (count * depth + depth * width + 2 * count * width),
        ),
        name="feed",
    )(rows, weight)


def slope_kernel(rows_ref, weight_ref, slope_ref, out_ref):
    step = 256

    def body(i, carry):
        at = pl.ds(pl.multiple_of(i * step, step), step)
        grad = mm(rows_ref[at], weight_ref[...])
        out_ref[at] = (grad * slope_ref[at].astype(F32)).astype(BF)
        return carry

    lax.fori_loop(0, rows_ref.shape[0] // step, body, 0, unroll=True)


def slope_product(rows, weight, slope):
    count, depth = rows.shape
    width = weight.shape[1]
    block = 256
    tall = pl.BlockSpec((count, block), lambda j: (0, j))
    return pl.pallas_call(
        slope_kernel,
        grid=(width // block,),
        in_specs=[
            pl.BlockSpec((count, depth), lambda j: (0, 0)),
            pl.BlockSpec((depth, block), lambda j: (0, j)),
            tall,
        ],
        out_specs=tall,
        out_shape=jax.ShapeDtypeStruct((count, width), BF),
        cost_estimate=pl.CostEstimate(
            flops=2 * count * depth * width,
            transcendentals=0,
            bytes_accessed=2 * (count * depth + depth * width + 2 * count * width),
        ),
        name="slope_product",
    )(rows, weight, slope)


class Whole:
    def __init__(self, dp, tensor):
        self.dp, self.tensor = dp, tensor

    def arrange(self, values):
        return values

    def restore(self, values):
        return values

    def gather_norms(self, packed):
        return lax.all_gather(packed, self.dp, axis=0, tiled=True)

    def gather_first(self, shard):
        return lax.all_gather(shard, self.dp, axis=0, tiled=True)

    def gather_first_set(self, first, second, feed_in, feed_out, rows):
        return first, rows, (second, feed_in, feed_out)

    def place_pieces(self, first):
        return self.gather_first(first)

    def gather_rest(self, rest, value):
        second, feed_in, feed_out = [self.gather_first(shard) for shard in rest]
        return second, feed_in, None, None, (feed_out, None)

    def feed_out(self, pieces):
        return pieces[0]

    def after(self, value, *others):
        return value

    def stage(self, work, *values):
        return work(*values)

    def sends(self, left, right):
        return ()

    def exchange(self, sends):
        return ()

    def merged(self, *sends):
        return ()

    def parted(self, far, *widths):
        return [()] * len(widths)

    def adds(self, *products):
        wholes = [mm_rows(left, right).astype(BF) for left, right, _ in products]
        return jnp.concatenate(wholes, axis=1)

    def second(self, whole):
        return ()

    def closing(self, whole, far):
        return whole

    middle = closing

    def scatter_z(self, whole):
        return lax.psum_scatter(whole, self.dp, scatter_dimension=0, tiled=True)

    def close_middle(self, whole):
        return whole.astype(F32)

    def close_last(self, whole, *widths):
        found, at = [], 0
        for columns in widths:
            found.append(whole[:, at : at + columns].astype(F32))
            at += columns
        return found

    def norm_sums(self, sums):
        sums = jnp.pad(sums.T, ((0, 0), (0, 122))).astype(BF)
        sums = lax.psum_scatter(sums, self.dp, scatter_dimension=0, tiled=True)
        return self.sum_all(sums)[:, :6].T

    def spread(self, rows, clips):
        local = rows.reshape(clips, -1, rows.shape[-1])
        return lax.all_gather(local, self.tensor, axis=1, tiled=True).reshape(-1, rows.shape[-1])

    def sequence(self, rows, clips):
        return rows.reshape(clips, -1, rows.shape[-1])

    def unsequence(self, rows):
        return rows.reshape(-1, rows.shape[-1])

    def clip_rows(self, rows, clips):
        return rows.reshape(clips, -1, rows.shape[-1])

    unclip_rows = unsequence

    def self_attend(self, qkv, clips):
        qkv = self.sequence(qkv, clips)
        cols = qkv.shape[-1] // 3
        q, k, v = qkv[..., :cols], qkv[..., cols : 2 * cols], qkv[..., 2 * cols :]
        att, log_total = attend(q, k, v)
        return self.unsequence(att), (q, k, v, log_total)

    def self_back(self, saved, grad, clips):
        dq, dk, dv = attend_back(*saved, self.sequence(grad, clips))
        return self.unsequence(jnp.concatenate([dq, dk, dv], axis=-1))

    def cross_attend(self, q, memory, clips):
        q = self.clip_rows(q, clips)
        memory = memory.reshape(clips, -1, memory.shape[-1])
        cols = q.shape[-1]
        k, v = memory[..., :cols], memory[..., cols:]
        out, chances = cross_attend(q, k, v)
        return self.unclip_rows(out), (q, k, v, chances)

    def cross_back(self, saved, grad, clips):
        dq, dk, dv = cross_attend_back(*saved, self.clip_rows(grad, clips))
        return self.unclip_rows(dq), self.unsequence(jnp.concatenate([dk, dv], axis=-1))

    def feed(self, rows, weight):
        return gelu_pair(mm(rows, weight))

    def slope_product(self, rows, weight, slope):
        return (mm(rows, weight) * slope.astype(F32)).astype(BF)

    def sum_own(self, left, right, product, clips):
        part = product(left, right).astype(BF).reshape(clips, -1, right_width(product, right))
        own = lax.psum_scatter(part, self.tensor, scatter_dimension=1, tiled=True)
        return own.reshape(-1, part.shape[-1]).astype(F32)

    def sum_all(self, values):
        return lax.psum(values.astype(BF), self.tensor).astype(F32)


def right_width(product, right):
    return right.shape[0] if product is mm_t else right.shape[1]


class Block(Whole):
    def __init__(self, width):
        self.width = width
        self.shard = width // 16
        self.core = lax.axis_index("core")

    def after(self, value, *others):
        return tie(value, others)

    def order(self):
        own_y, own_x = lax.axis_index("y"), lax.axis_index("x")
        place = jnp.arange(self.width, dtype=jnp.int32)
        quarter, rest = place // (4 * self.shard), place % (4 * self.shard)
        z, row = rest // self.shard, rest % self.shard
        y, x = (quarter // 2) ^ own_y, (quarter // 2) ^ (quarter % 2) ^ own_x
        source = ((z * 2 + y) * 2 + x) * self.shard + row
        return (jnp.arange(self.width, dtype=jnp.int32)[:, None] == source[None, :]).astype(BF)

    def arrange(self, values):
        return mm(values, self.order()).astype(BF)

    def restore(self, values):
        if values.dtype == BF:
            return mm_t(values, self.order()).astype(BF)
        high = lax.reduce_precision(values, 8, 7)
        low = (values - high).astype(BF)
        order = self.order()
        return mm_t(high.astype(BF), order) + mm_t(low, order)

    def x(self, v):
        return lax.ppermute(v, "x", SWAP)

    def y(self, v):
        return lax.ppermute(v, "y", SWAP)

    def other(self, v):
        return lax.ppermute(v, "core", SWAP)

    def gather_norms(self, packed):
        pair = jnp.stack([packed, lax.ppermute(packed, "z", [(0, 1), (1, 0), (2, 3), (3, 2)])])
        far = lax.ppermute(pair, "z", [(0, 2), (1, 3), (2, 0), (3, 1)])
        own = lax.axis_index("z")
        four = jnp.concatenate([pair, far])
        four = jnp.stack([lax.dynamic_index_in_dim(four, own ^ p, 0, False) for p in range(4)])
        two = jnp.stack([four, self.x(four)])
        far = self.y(two)
        whole = jnp.stack([two[0], two[1], far[1], far[0]])
        return whole.reshape(self.width, packed.shape[-1])

    def halves(self, shard):
        half = shard.shape[1] // 256 * 128
        return shard[:, :half], shard[:, half:]

    def gather_first_set(self, first, second, feed_in, feed_out, rows):
        opened = []
        for shard in (feed_in, feed_out):
            a, b = self.halves(shard)
            opened.append(jnp.stack([a, self.x(a), b, self.y(b)]))
        rows, opened = lax.optimization_barrier((rows, opened))
        sets = [lax.all_gather(shard, "z", axis=0, tiled=True) for shard in (first, second)]
        feeds = [lax.all_gather(four, "z", axis=1, tiled=True) for four in opened]
        pieces, last, _ = self.gather_pieces(sets[0], rows)
        pieces_next = self.gather_pieces(sets[1], last)
        return pieces, rows, (pieces_next, feeds)

    def gather_pieces(self, four, last):
        a, b = self.halves(tie(four, last))
        xa, yb, ya, xb = self.x(a), self.y(b), self.y(a), self.x(b)
        far_a, far_b = self.y(xa), self.x(yb)
        return (four, xa, ya, far_a, xb, yb, far_b), (far_a, far_b, ya, xb), (xa, yb)

    def place_pieces(self, pieces):
        four, xa, ya, far_a, xb, yb, far_b = pieces
        n, half = xa.shape
        return place(
            [
                (four, 0, 0),
                (xa, n, 0),
                (far_a, 2 * n, 0),
                (ya, 3 * n, 0),
                (xb, n, half),
                (far_b, 2 * n, half),
                (yb, 3 * n, half),
            ],
            (4 * n, four.shape[1]),
        )

    def gather_rest(self, rest, value):
        (pieces, last, _), feeds = rest
        feeds[0] = tie(feeds[0], value)
        in_sides = feeds[0][:2], feeds[0][2:]
        a, b = tie(in_sides, last)
        in_far = self.y(a), self.x(b)
        w_cross = self.place_pieces(pieces)
        w_in = self.place_feed(feeds[0], in_far)
        out_sides = feeds[1][:2], feeds[1][2:]
        a, b = tie(out_sides, in_far)
        return w_cross, w_in, in_far, out_sides, (feeds[1], (self.y(a), self.x(b)))

    def place_feed(self, four, far):
        _, n, half = four.shape
        return place_stacked(
            four.reshape(4 * n, half), far[0].reshape(2 * n, half), far[1].reshape(2 * n, half)
        )

    def feed_out(self, pieces):
        return self.place_feed(*pieces)

    def stage(self, work, *values):
        shapes = jax.eval_shape(work, *values)

        def nothing(*_):
            return jax.tree.map(lambda leaf: jnp.zeros(leaf.shape, leaf.dtype), shapes)

        return lax.cond(self.core < 2, work, nothing, *values)

    def sends(self, left, right):
        n, half = self.width // 4, right.shape[1] // 256 * 128
        return (
            mm_rows(left[:, 2 * n :], right[:, :half]).astype(BF),
            mm_rows(left[:, n : 3 * n], right[:, half:]).astype(BF),
        )

    def exchange(self, sends):
        return self.y(sends[0]), self.x(sends[1])

    def merged(self, *sends):
        return [jnp.concatenate(side, axis=1) for side in zip(*sends)]

    def parted(self, far, *widths):
        halves = [width // 256 * 128 for width in widths]
        ends = [sum(halves[: i + 1]) for i in range(len(halves) - 1)]
        lefts = jnp.split(far[0], ends, axis=1)
        halves = [width - half for width, half in zip(widths, halves)]
        ends = [sum(halves[: i + 1]) for i in range(len(halves) - 1)]
        return list(zip(lefts, jnp.split(far[1], ends, axis=1)))

    def adds(self, *products):
        n, parts = self.width // 4, []
        for left, right, (far_y, far_x) in products:
            half = right.shape[1] // 256 * 128
            first, last = right[:, :half], right[:, half:]
            parts.append(
                [
                    (mm_rows(own, side) + far.astype(F32)).astype(BF)
                    for own, side, far in (
                        (left[:, :n], first, far_y[n:]),
                        (left[:, n : 2 * n], first, far_y[:n]),
                        (left[:, :n], last, far_x[:n]),
                        (left[:, 3 * n :], last, far_x[n:]),
                    )
                ]
            )
        return [jnp.concatenate(part, axis=1) for part in zip(*parts)]

    def middle(self, parts, _):
        return jnp.stack(parts)

    def second(self, parts):
        return self.x(parts[1]), self.y(parts[3])

    def closing(self, parts, far):
        pairs = zip((parts[0], parts[2]), far)
        return jnp.stack([(own.astype(F32) + other.astype(F32)).astype(BF) for own, other in pairs])

    def scatter_z(self, parts):
        return lax.psum_scatter(parts, "z", scatter_dimension=1, tiled=True)

    def close_middle(self, four):
        left = four[0].astype(F32) + self.x(four[1]).astype(F32)
        right = four[2].astype(F32) + self.y(four[3]).astype(F32)
        return jnp.concatenate([left, right], axis=1)

    def close_last(self, both, *widths):
        found, left, right = [], 0, 0
        for columns in widths:
            a = columns // 256 * 128
            b = columns - a
            found.append(
                jnp.concatenate([both[0, :, left : left + a], both[1, :, right : right + b]], axis=1)
            )
            left, right = left + a, right + b
        return [part.astype(F32) for part in found]

    def norm_sums(self, sums):
        n = self.width // 4
        sums = self.sum_all(jnp.pad(sums.T, ((0, 0), (0, 122))))
        far = self.y(sums[2 * n :].astype(BF)).astype(F32)
        away = (sums[n : 2 * n] + far[:n]).astype(BF)
        sums = sums[:n] + far[n:] + self.x(away).astype(F32)
        own = lax.axis_index("z")
        for step, pairs, side in (
            (n // 2, [(0, 2), (1, 3), (2, 0), (3, 1)], own // 2),
            (n // 4, [(0, 1), (1, 0), (2, 3), (3, 2)], own % 2),
        ):
            near = lax.dynamic_slice_in_dim(sums, side * step, step)
            away = lax.dynamic_slice_in_dim(sums, (1 - side) * step, step)
            sums = near + lax.ppermute(away.astype(BF), "z", pairs).astype(F32)
        return sums[:, :6].T

    def spread(self, rows, clips):
        return jnp.concatenate([rows, self.other(rows)])

    def self_attend(self, qkv, clips):
        cols = qkv.shape[-1] // 3
        steps = cols // (2 * HEAD_DIM)
        view = qkv.reshape(2, clips, -1, qkv.shape[-1])
        frames = view.shape[2]

        def block(part):
            return pl.BlockSpec(
                (2, 1, frames, 2 * HEAD_DIM), lambda c, j, _: (0, c, 0, part * steps + j)
            )

        shape = (2, clips, frames, cols)
        core = self.core.reshape(1).astype(jnp.int32)
        scores = clips * steps * 2 * 3 * frames * frames
        out, log_total = pl.pallas_call(
            self_kernel,
            grid_spec=pltpu.PrefetchScalarGridSpec(
                num_scalar_prefetch=1,
                grid=(clips, steps),
                in_specs=[block(0), block(1), block(2)],
                out_specs=[block(0), block(0)],
            ),
            out_shape=[jax.ShapeDtypeStruct(shape, BF), jax.ShapeDtypeStruct(shape, F32)],
            cost_estimate=pl.CostEstimate(
                flops=4 * scores * HEAD_DIM,
                transcendentals=scores,
                bytes_accessed=2 * qkv.size + 6 * qkv.size // 3,
            ),
            name="self_attend",
        )(core, view, view, view)
        return out.reshape(-1, cols), (core, view, log_total)

    def self_back(self, saved, grad, clips):
        core, view, log_total = saved
        cols = view.shape[-1] // 3
        steps = cols // (2 * HEAD_DIM)
        frames = view.shape[2]

        def block(part):
            return pl.BlockSpec(
                (2, 1, frames, 2 * HEAD_DIM), lambda c, j, _: (0, c, 0, part * steps + j)
            )

        scores = clips * steps * 2 * 3 * frames * frames
        out = pl.pallas_call(
            self_back_kernel,
            grid_spec=pltpu.PrefetchScalarGridSpec(
                num_scalar_prefetch=1,
                grid=(clips, steps),
                in_specs=[block(0), block(1), block(2), block(0), block(0)],
                out_specs=pl.BlockSpec((2, 1, frames, 3 * cols), lambda c, j, _: (0, c, 0, 0)),
            ),
            out_shape=jax.ShapeDtypeStruct(view.shape, BF),
            cost_estimate=pl.CostEstimate(
                flops=10 * scores * HEAD_DIM,
                transcendentals=scores,
                bytes_accessed=4 * view.size + 6 * view.size // 3,
            ),
            name="self_back",
        )(core, view, view, view, log_total, grad.reshape(2, clips, frames, cols))
        return out.reshape(-1, 3 * cols)

    def cross_specs(self, q, clips, texts):
        cols = q.shape[-1]
        steps = cols // (2 * HEAD_DIM)
        view = q.reshape(2, clips, -1, cols)
        frames = view.shape[2]
        wide = pl.BlockSpec((2, 1, frames, 2 * HEAD_DIM), lambda c, j: (0, c, 0, j))

        def block(part):
            return pl.BlockSpec((1, texts, 2 * HEAD_DIM), lambda c, j: (c, 0, part * steps + j))

        return view, (clips, steps), wide, block, clips * 2 * frames * cols * texts

    def cross_attend(self, q, memory, clips):
        memory = memory.reshape(clips, -1, memory.shape[-1])
        view, grid, wide, block, work = self.cross_specs(q, clips, memory.shape[1])
        out = pl.pallas_call(
            cross_kernel,
            grid=grid,
            in_specs=[wide, block(0), block(1)],
            out_specs=wide,
            out_shape=jax.ShapeDtypeStruct(view.shape, BF),
            cost_estimate=pl.CostEstimate(
                flops=4 * work, transcendentals=work // HEAD_DIM, bytes_accessed=4 * q.size
            ),
            name="cross_attend",
        )(view, memory, memory)
        return out.reshape(q.shape), (q, memory)

    def cross_back(self, saved, grad, clips):
        q, memory = saved
        texts = memory.shape[1]
        view, grid, wide, block, work = self.cross_specs(q, clips, texts)
        dq, dkv = pl.pallas_call(
            cross_back_kernel,
            grid=grid,
            in_specs=[wide, block(0), block(1), wide],
            out_specs=[
                wide,
                pl.BlockSpec((1, texts, memory.shape[-1]), lambda c, j: (c, 0, 0)),
            ],
            out_shape=[
                jax.ShapeDtypeStruct(view.shape, BF),
                jax.ShapeDtypeStruct(memory.shape, BF),
            ],
            cost_estimate=pl.CostEstimate(
                flops=10 * work, transcendentals=work // HEAD_DIM, bytes_accessed=6 * q.size
            ),
            name="cross_back",
        )(view, memory, memory, grad.reshape(view.shape))
        return dq.reshape(q.shape), dkv.reshape(-1, memory.shape[-1])

    def feed(self, rows, weight):
        return feed(rows, weight)

    def slope_product(self, rows, weight, slope):
        return slope_product(rows, weight, slope)

    def sum_own(self, left, right, product, clips):
        n = left.shape[0] // 2
        far = self.other(product(left[n:], right).astype(BF))
        return product(left[:n], right) + far.astype(F32)

    def sum_all(self, values):
        return values + self.other(values.astype(BF)).astype(F32)


def layer(
    comm,
    frames,
    text_states,
    norm_gain,
    norm_shift,
    self_project,
    self_output,
    cross_query,
    cross_memory,
    cross_output,
    feed_input,
    feed_output,
    upstream,
):
    clips, own_frames, width = frames.shape
    texts = text_states.shape[1]
    cols = cross_query.shape[1]
    own_rows = clips * own_frames

    def catenate(parts):
        return jnp.concatenate(parts, axis=1)

    norms = comm.gather_norms(
        jnp.pad(jnp.concatenate([norm_gain, norm_shift]).T, ((0, 0), (0, 122)))
    )
    norms = norms.T.astype(F32)
    gain, shift = norms[0:3], norms[3:6]
    first_set = catenate([self_project[0], self_project[1], self_project[2]])
    second_set = catenate(
        [self_output.T, cross_query, cross_memory[0], cross_memory[1], cross_output.T]
    )
    values0 = comm.arrange(frames.reshape(own_rows, width)).astype(F32)
    stats0 = norm_stats(values0)
    own_n1 = norm_apply(values0, stats0, gain[0], shift[0])
    pieces, own_n1, rest = comm.gather_first_set(
        first_set, second_set, feed_input, feed_output.T, own_n1
    )
    up = comm.arrange(upstream.reshape(own_rows, width))
    text = comm.arrange(text_states.reshape(clips * texts, width))
    up_all = comm.spread(up, clips)

    n1 = comm.spread(own_n1, clips)

    def split_cross(weights):
        return jnp.split(weights, [cols, 2 * cols, 4 * cols], axis=1)

    def stage_self(pieces, n1):
        w_self = comm.place_pieces(pieces)
        return w_self, comm.self_attend(mm(n1, w_self).astype(BF), clips)

    w_self, (att, self_saved) = comm.stage(stage_self, pieces, n1)
    w_cross, w_in, mark_in, mark_out, out_pieces = comm.gather_rest(rest, att)

    def stage0(values0, att, w_cross, text):
        w_so, w_cq, w_cm, w_co = split_cross(w_cross)
        values1 = values0 + comm.sum_own(att, w_so, mm_t, clips)
        stats1 = norm_stats(values1)
        n2 = comm.spread(norm_apply(values1, stats1, gain[1], shift[1]), clips)
        cross, saved = comm.cross_attend(
            mm(n2, w_cq).astype(BF), mm(text, w_cm).astype(BF), clips
        )
        values2 = values1 + comm.sum_own(cross, w_co, mm_t, clips)
        stats2 = norm_stats(values2)
        n3 = comm.spread(norm_apply(values2, stats2, gain[2], shift[2]), clips)
        return values1, stats1, n2, cross, saved, values2, stats2, n3

    values1, stats1, n2, cross, cross_saved, values2, stats2, n3 = comm.stage(
        stage0, values0, att, w_cross, text
    )
    n3 = comm.after(n3, mark_in, mark_out)
    hidden, slope = comm.feed(n3, w_in)
    send_out = comm.sends(up_all, hidden)
    hidden, slope = comm.after((hidden, slope), out_pieces[1], send_out)
    far_out = comm.exchange(send_out)

    def stage1(pieces, rows, slope, n3, w_in):
        w_out = comm.feed_out(pieces)
        pre_grad = comm.slope_product(rows, w_out, slope)
        return w_out, pre_grad, comm.sends(n3, pre_grad), comm.sum_own(pre_grad, w_in, mm_t, clips)

    w_out, pre_grad, send_in, e3 = comm.stage(stage1, out_pieces, up_all, slope, n3, w_in)
    e3, send_in = comm.after((e3, send_in), far_out)
    far_in = comm.exchange(send_in)

    def stage2(rows, hidden, far, e3, values2, stats2, own):
        sent = comm.middle(comm.adds((rows, hidden, far)), None)
        grads = norm_back(values2, stats2, gain[2], e3)
        r2 = own.astype(F32) + grads[0]
        return sent, r2, r2.astype(BF), grads[1], grads[2]

    sent_out, r2, r2_own, gain2, shift2 = comm.stage(
        stage2, up_all, hidden, far_out, e3, values2, stats2, up
    )
    half_out = comm.scatter_z(sent_out)

    def stage3(r2_own, saved, w_cross, n2, cross, text):
        w_co = split_cross(w_cross)[3]
        r2_all = comm.spread(r2_own, clips)
        dcq, dmem = comm.cross_back(saved, mm(r2_all, w_co).astype(BF), clips)
        pairs = (n2, dcq), (r2_all, cross), (text, dmem)
        return r2_all, dcq, dmem, comm.merged(*[comm.sends(*pair) for pair in pairs])

    r2_all, dcq, dmem, send_cross = comm.stage(
        stage3, r2_own, cross_saved, w_cross, n2, cross, text
    )
    dcq, send_cross = comm.after((dcq, send_cross), far_in)
    far_cross = comm.exchange(send_cross)
    cross_pairs = (n2, dcq), (r2_all, cross), (text, dmem)

    def stage4(n3, pre_grad, far, dcq, w_cross, values1, stats1, r2):
        w_so, w_cq, *_ = split_cross(w_cross)
        in_sums = comm.adds((n3, pre_grad, far))
        e2 = comm.sum_own(dcq, w_cq, mm_t, clips)
        grads = norm_back(values1, stats1, gain[1], e2)
        r1 = r2 + grads[0]
        r1_all = comm.spread(r1.astype(BF), clips)
        return in_sums, r1, r1_all, mm(r1_all, w_so).astype(BF), grads[1], grads[2]

    in_sums, r1, r1_all, datt, gain1, shift1 = comm.stage(
        stage4, n3, pre_grad, far_in, dcq, w_cross, values1, stats1, r2
    )
    in_sums, datt = comm.after((in_sums, datt), far_cross, half_out)
    in_second = comm.second(in_sums)

    def stage5(pairs, far, r1_all, att):
        far = comm.parted(far, cols, cols, 2 * cols)
        sums = comm.adds(*[(*pair, one) for pair, one in zip(pairs, far)])
        return sums, comm.sends(r1_all, att)

    cross_sums, send_so = comm.stage(stage5, cross_pairs, far_cross, r1_all, att)
    cross_sums, send_so, datt, in_sums = comm.after(
        (cross_sums, send_so, datt, in_sums), in_second
    )
    cross_second = comm.second(cross_sums)
    far_so = comm.exchange(send_so)
    half_in = comm.scatter_z(comm.closing(in_sums, in_second))

    def stage_back(saved, datt, n1):
        dqkv = comm.self_back(saved, datt, clips)
        return dqkv, comm.sends(n1, dqkv)

    dqkv, send_self = comm.stage(stage_back, self_saved, datt, n1)
    dmem, hidden, send_self, cross_sums, dqkv = comm.after(
        (dmem, hidden, send_self, cross_sums, dqkv), cross_second, far_so
    )
    far_self = comm.exchange(send_self)
    half_cross = comm.scatter_z(comm.closing(cross_sums, cross_second))

    def stage6(dmem, w_cross, values2, hidden, w_out):
        w_cm = split_cross(w_cross)[2]
        text_grad = comm.sum_all(mm_t(dmem, w_cm))
        layer_out = (values2 + comm.sum_own(hidden, w_out, mm_t, clips)).astype(BF)
        return comm.restore(text_grad), comm.restore(layer_out)

    text_grad, layer_out = comm.stage(stage6, dmem, w_cross, values2, hidden, w_out)
    text_grad, layer_out, dqkv = comm.after((text_grad, layer_out, dqkv), far_self, half_in)
    self_sums = comm.adds((r1_all, att, far_so), (n1, dqkv, far_self))
    dqkv = comm.after(dqkv, self_sums)
    self_second = comm.second(self_sums)

    def stage7(dqkv, w_self, values0, stats0, r1):
        e1 = comm.sum_own(dqkv, w_self, mm_t, clips)
        grads = norm_back(values0, stats0, gain[0], e1)
        return comm.restore(r1 + grads[0]), grads[1], grads[2]

    input_grad, gain0, shift0 = comm.stage(stage7, dqkv, w_self, values0, stats0, r1)
    input_grad, gain0, self_sums = comm.after(
        (input_grad, gain0, self_sums), self_second, half_cross
    )
    half_self = comm.scatter_z(comm.closing(self_sums, self_second))
    norm_grad = comm.norm_sums(jnp.stack([gain0, gain1, gain2, shift0, shift1, shift2]))
    input_grad = input_grad.reshape(clips, own_frames, width)
    text_grad = text_grad.reshape(clips, texts, width)
    layer_out = layer_out.reshape(clips, own_frames, width)
    grad_out = comm.close_middle(half_out)
    (grad_in,) = comm.close_last(half_in, pre_grad.shape[1])
    grad_cq, grad_co, grad_cm = comm.close_last(half_cross, cols, cols, 2 * cols)
    grad_so, grad_self = comm.close_last(half_self, cols, 3 * cols)
    return (
        layer_out,
        input_grad,
        text_grad,
        norm_grad[0:3],
        norm_grad[3:6],
        jnp.stack([grad_self[:, i * cols : (i + 1) * cols] for i in range(3)]),
        grad_so.T,
        grad_cq,
        jnp.stack([grad_cm[:, :cols], grad_cm[:, cols:]]),
        grad_co.T,
        grad_in,
        grad_out.T,
    )


def specs(dp, tensor):
    in_specs = (
        P(dp, tensor, None),
        P(dp, None, None),
        P(None, dp),
        P(None, dp),
        P(None, dp, tensor),
        P(tensor, dp),
        P(dp, tensor),
        P(None, dp, tensor),
        P(tensor, dp),
        P(dp, tensor),
        P(tensor, dp),
        P(dp, tensor, None),
    )
    out_specs = (
        P(dp, tensor, None),
        P(dp, tensor, None),
        P(dp, None, None),
        P(None, dp),
        P(None, dp),
        P(None, dp, tensor),
        P(tensor, dp),
        P(dp, tensor),
        P(None, dp, tensor),
        P(tensor, dp),
        P(dp, tensor),
        P(tensor, dp),
    )
    return in_specs, out_specs


def solution(mesh):
    if mesh.shape["dp"] == 16 and mesh.shape["tensor"] == 2:
        mesh = Mesh(mesh.devices.reshape(4, 2, 2, 2), ("z", "y", "x", "core"))
        in_specs, out_specs = specs(("z", "y", "x"), "core")

        def per_device(frames, *rest):
            return layer(Block(frames.shape[-1]), frames, *rest)
    else:
        in_specs, out_specs = specs("dp", "tensor")

        def per_device(frames, *rest):
            return layer(Whole("dp", "tensor"), frames, *rest)

    return jax.shard_map(
        per_device, mesh=mesh, in_specs=in_specs, out_specs=out_specs, check_vma=False
    )
```

```python
import math

import jax
import jax.numpy as jnp
from jax import lax
from jax.experimental import pallas as pl
from jax.experimental.pallas import tpu as pltpu
from jax.sharding import Mesh
from jax.sharding import PartitionSpec as P

HEAD_DIM = 64
EPS = 1e-05
BF = jnp.bfloat16
F32 = jnp.float32
SWAP = [(0, 1), (1, 0)]


def mm(left, right):
    return jnp.dot(left, right, preferred_element_type=F32)


def mm_t(left, right):
    return lax.dot_general(left, right, (((1,), (1,)), ((), ())), preferred_element_type=F32)


def mm_rows(left, right):
    return lax.dot_general(left, right, (((0,), (0,)), ((), ())), preferred_element_type=F32)


def tie(value, *others):
    return lax.optimization_barrier((value, others))[0]


def norm_stats(values):
    mean = jnp.mean(values, axis=-1, keepdims=True)
    centred = values - mean
    inv = lax.rsqrt(jnp.mean(centred * centred, axis=-1, keepdims=True) + EPS)
    return mean, inv


def norm_apply(values, stats, gain, shift):
    return ((values - stats[0]) * stats[1] * gain + shift).astype(BF)


def norm_back(values, stats, gain, grad):
    xhat = (values - stats[0]) * stats[1]
    scaled = grad * gain
    part = jnp.mean(scaled, axis=-1, keepdims=True)
    cross = jnp.mean(scaled * xhat, axis=-1, keepdims=True)
    value_grad = (scaled - part - xhat * cross) * stats[1]
    return value_grad, jnp.sum(grad * xhat, axis=0), jnp.sum(grad, axis=0)


def gelu_pair(pre):
    phi = 0.5 * (1.0 + lax.erf(pre * (1.0 / math.sqrt(2.0))))
    dens = jnp.exp(-0.5 * pre * pre) * (1.0 / math.sqrt(2.0 * math.pi))
    return (pre * phi).astype(BF), (phi + pre * dens).astype(BF)


def heads(matrix):
    return matrix.reshape(*matrix.shape[:-1], matrix.shape[-1] // HEAD_DIM, HEAD_DIM)


def flat(matrix):
    return matrix.reshape(*matrix.shape[:-2], -1)


SCALE = 1.0 / math.sqrt(HEAD_DIM)


def causal_scores(q, k):
    scores = jnp.einsum("bqhd,bkhd->bhqk", heads(q), heads(k), preferred_element_type=F32) * SCALE
    n = q.shape[1]
    allowed = jnp.arange(n)[None, :] <= jnp.arange(n)[:, None]
    return jnp.where(allowed, scores, -1e30)


def attend(q, k, v):
    scores = causal_scores(q, k)
    top = jnp.max(scores, axis=-1, keepdims=True)
    terms = jnp.exp(scores - top)
    total = jnp.sum(terms, axis=-1, keepdims=True)
    out = jnp.einsum(
        "bhqk,bkhd->bqhd", (terms / total).astype(BF), heads(v), preferred_element_type=F32
    )
    return flat(out).astype(BF), top + jnp.log(total)


def probs_back(chances, dp, q, k, grad):
    dot = jnp.sum(chances * dp, axis=-1, keepdims=True)
    ds = (chances * (dp - dot)).astype(BF)
    dv = jnp.einsum("bhqk,bqhd->bkhd", chances.astype(BF), grad, preferred_element_type=F32)
    dq = jnp.einsum("bhqk,bkhd->bqhd", ds, heads(k), preferred_element_type=F32) * SCALE
    dk = jnp.einsum("bhqk,bqhd->bkhd", ds, heads(q), preferred_element_type=F32) * SCALE
    return flat(dq).astype(BF), flat(dk).astype(BF), flat(dv).astype(BF)


def attend_back(q, k, v, log_total, grad):
    chances = jnp.exp(causal_scores(q, k) - log_total)
    grad = heads(grad)
    dp = jnp.einsum("bqhd,bkhd->bhqk", grad, heads(v), preferred_element_type=F32)
    return probs_back(chances, dp, q, k, grad)


def cross_attend(q, k, v):
    scores = jnp.einsum("bqhd,bkhd->bhqk", heads(q), heads(k), preferred_element_type=F32) * SCALE
    chances = jax.nn.softmax(scores, axis=-1)
    out = jnp.einsum("bhqk,bkhd->bqhd", chances.astype(BF), heads(v), preferred_element_type=F32)
    return flat(out).astype(BF), chances


def cross_attend_back(q, k, v, chances, grad):
    grad = heads(grad)
    dp = jnp.einsum("bqhd,bkhd->bhqk", grad, heads(v), preferred_element_type=F32)
    return probs_back(chances, dp, q, k, grad)

ANY = pl.BlockSpec(memory_space=pl.ANY)
NEG = -1e30


def place_kernel(*refs, spots):
    sources, out, sems = refs[: len(spots)], refs[len(spots)], refs[len(spots) + 1]
    copies = []
    for i, (source, (row, col)) in enumerate(zip(sources, spots)):
        rows, cols = source.shape
        copies.append(
            pltpu.make_async_copy(
                source, out.at[pl.ds(row, rows), pl.ds(col, cols)], sems.at[i]
            )
        )
    for copy in copies:
        copy.start()
    for copy in copies:
        copy.wait()


def place(pieces, shape):
    spots = tuple((row, col) for _, row, col in pieces)
    return pl.pallas_call(
        lambda *refs: place_kernel(*refs, spots=spots),
        out_shape=jax.ShapeDtypeStruct(shape, pieces[0][0].dtype),
        in_specs=[ANY] * len(pieces),
        out_specs=pl.BlockSpec(memory_space=pltpu.VMEM),
        scratch_shapes=[pltpu.SemaphoreType.DMA((len(pieces),))],
        name="place",
    )(*[piece for piece, _, _ in pieces])


def place_stacked_kernel(four, far_a, far_b, out, sems):
    n, half = four.shape[0] // 4, four.shape[1]
    spots = [
        (four, 0, 2 * n, 0, 0),
        (far_a, 0, 2 * n, 2 * n, 0),
        (four, 2 * n, n, 0, half),
        (far_b, 0, n, n, half),
        (four, 3 * n, n, 2 * n, half),
        (far_b, n, n, 3 * n, half),
    ]
    copies = [
        pltpu.make_async_copy(
            source.at[pl.ds(start, rows)], out.at[pl.ds(row, rows), pl.ds(col, half)], sems.at[i]
        )
        for i, (source, start, rows, row, col) in enumerate(spots)
    ]
    for copy in copies:
        copy.start()
    for copy in copies:
        copy.wait()


def place_stacked(four, far_a, far_b):
    return pl.pallas_call(
        place_stacked_kernel,
        out_shape=jax.ShapeDtypeStruct((four.shape[0], 2 * four.shape[1]), four.dtype),
        in_specs=[ANY] * 3,
        out_specs=pl.BlockSpec(memory_space=pltpu.VMEM),
        scratch_shapes=[pltpu.SemaphoreType.DMA((6,))],
        name="place_stacked",
    )(four, far_a, far_b)


def rows_of(matrix, grad):
    return lax.dot_general(matrix, grad, (((0,), (0,)), ((), ())), preferred_element_type=F32)


def head_of(ref, half, head):
    return ref[half, 0, :, head * HEAD_DIM : (head + 1) * HEAD_DIM]


def masked(scores):
    n = scores.shape[0]
    rows = lax.broadcasted_iota(jnp.int32, (n, n), 0)
    cols = lax.broadcasted_iota(jnp.int32, (n, n), 1)
    return jnp.where(cols <= rows, scores, NEG)


def self_kernel(core_ref, q_ref, k_ref, v_ref, out_ref, log_ref):
    halves = (core_ref[0], 1 - core_ref[0])
    outs, logs = ([], []), ([], [])
    for head in range(2):
        q = [head_of(q_ref, h, head) * BF(SCALE) for h in halves]
        k = [head_of(k_ref, h, head) for h in halves]
        v = [head_of(v_ref, h, head) for h in halves]
        first = masked(mm_t(q[0], k[0]))
        for half, scores in enumerate([[first], [mm_t(q[1], k[0]), masked(mm_t(q[1], k[1]))]]):
            top = jnp.max(scores[0], axis=-1, keepdims=True)
            if half:
                top = jnp.maximum(top, jnp.max(scores[1], axis=-1, keepdims=True))
            terms = [jnp.exp(part - top) for part in scores]
            total = sum(jnp.sum(part, axis=-1, keepdims=True) for part in terms)
            inverse = 1.0 / total
            out = sum(mm((part * inverse).astype(BF), v[i]) for i, part in enumerate(terms))
            outs[half].append(out.astype(BF))
            logs[half].append(jnp.broadcast_to(top + jnp.log(total), out.shape))
    for half, h in enumerate(halves):
        out_ref[h, 0] = jnp.concatenate(outs[half], axis=1)
        log_ref[h, 0] = jnp.concatenate(logs[half], axis=1)


def self_back_kernel(core_ref, q_ref, k_ref, v_ref, log_ref, grad_ref, out_ref):
    halves = (core_ref[0], 1 - core_ref[0])
    found = [[], [], [], [], [], []]
    for head in range(2):
        q = [head_of(q_ref, h, head) * BF(SCALE) for h in halves]
        k = [head_of(k_ref, h, head) for h in halves]
        ks = [part * BF(SCALE) for part in k]
        v = [head_of(v_ref, h, head) for h in halves]
        log = [head_of(log_ref, h, head)[:, :1] for h in halves]
        grad = [head_of(grad_ref, h, head) for h in halves]
        dq, dk, dv = [0.0, 0.0], [0.0, 0.0], [0.0, 0.0]
        for half, parts in enumerate([(0,), (0, 1)]):
            chances, dps = [], []
            for i in parts:
                scores = mm_t(q[half], k[i])
                if i == half:
                    scores = masked(scores)
                chances.append(jnp.exp(scores - log[half]))
                dps.append(mm_t(grad[half], v[i]))
            dot = sum(
                jnp.sum(c * dp, axis=-1, keepdims=True) for c, dp in zip(chances, dps)
            )
            for i, c, dp in zip(parts, chances, dps):
                ds = (c * (dp - dot)).astype(BF)
                dv[i] += rows_of(c.astype(BF), grad[half])
                dk[i] += rows_of(ds, q[half])
                dq[half] += mm(ds, ks[i])
        for i, part in enumerate(dq + dk + dv):
            found[i].append(part.astype(BF))
    width = out_ref.shape[-1] // 3
    for i in range(3):
        col = pl.multiple_of(i * width + pl.program_id(1) * 2 * HEAD_DIM, 2 * HEAD_DIM)
        for half, h in enumerate(halves):
            out_ref[h, 0, :, pl.ds(col, 2 * HEAD_DIM)] = jnp.concatenate(
                found[2 * i + half], axis=1
            )


def cross_parts(q_ref, k_ref, head):
    cs = slice(head * HEAD_DIM, (head + 1) * HEAD_DIM)
    q = jnp.concatenate([q_ref[0, 0, :, cs], q_ref[1, 0, :, cs]]) * BF(SCALE)
    scores = mm_t(q, k_ref[0, :, cs])
    terms = jnp.exp(scores - jnp.max(scores, axis=-1, keepdims=True))
    return q, terms * (1.0 / jnp.sum(terms, axis=-1, keepdims=True)), cs


def cross_kernel(q_ref, k_ref, v_ref, out_ref):
    outs = []
    for head in range(2):
        _, chances, cs = cross_parts(q_ref, k_ref, head)
        outs.append(mm(chances.astype(BF), v_ref[0, :, cs]).astype(BF))
    out = jnp.concatenate(outs, axis=1)
    n = out.shape[0] // 2
    out_ref[0, 0], out_ref[1, 0] = out[:n], out[n:]


def cross_back_kernel(q_ref, k_ref, v_ref, grad_ref, dq_ref, dkv_ref):
    found = [[], [], []]
    for head in range(2):
        q, chances, cs = cross_parts(q_ref, k_ref, head)
        grad = jnp.concatenate([grad_ref[0, 0, :, cs], grad_ref[1, 0, :, cs]])
        dp = mm_t(grad, v_ref[0, :, cs])
        ds = (chances * (dp - jnp.sum(chances * dp, axis=-1, keepdims=True))).astype(BF)
        found[0].append(mm(ds, k_ref[0, :, cs] * BF(SCALE)).astype(BF))
        found[1].append(rows_of(ds, q).astype(BF))
        found[2].append(rows_of(chances.astype(BF), grad).astype(BF))
    dq, dk, dv = [jnp.concatenate(parts, axis=1) for parts in found]
    n = dq.shape[0] // 2
    dq_ref[0, 0], dq_ref[1, 0] = dq[:n], dq[n:]
    width = dkv_ref.shape[-1] // 2
    for i, part in enumerate([dk, dv]):
        col = pl.multiple_of(i * width + pl.program_id(1) * 2 * HEAD_DIM, 2 * HEAD_DIM)
        dkv_ref[0, :, pl.ds(col, 2 * HEAD_DIM)] = part


def feed_kernel(rows_ref, weight_ref, hidden_ref, slope_ref):
    step = 256

    def body(i, carry):
        at = pl.ds(pl.multiple_of(i * step, step), step)
        hidden_ref[at], slope_ref[at] = gelu_pair(mm(rows_ref[at], weight_ref[...]))
        return carry

    lax.fori_loop(0, rows_ref.shape[0] // step, body, 0, unroll=True)


def feed(rows, weight):
    count, depth = rows.shape
    width = weight.shape[1]
    block = 256
    out = jax.ShapeDtypeStruct((count, width), BF)
    return pl.pallas_call(
        feed_kernel,
        grid=(width // block,),
        in_specs=[
            pl.BlockSpec((count, depth), lambda j: (0, 0)),
            pl.BlockSpec((depth, block), lambda j: (0, j)),
        ],
        out_specs=[pl.BlockSpec((count, block), lambda j: (0, j))] * 2,
        out_shape=[out, out],
        cost_estimate=pl.CostEstimate(
            flops=2 * count * depth * width,
            transcendentals=2 * count * width,
            bytes_accessed=2 * (count * depth + depth * width + 2 * count * width),
        ),
        name="feed",
    )(rows, weight)


def slope_kernel(rows_ref, weight_ref, slope_ref, out_ref):
    step = 256

    def body(i, carry):
        at = pl.ds(pl.multiple_of(i * step, step), step)
        grad = mm(rows_ref[at], weight_ref[...])
        out_ref[at] = (grad * slope_ref[at].astype(F32)).astype(BF)
        return carry

    lax.fori_loop(0, rows_ref.shape[0] // step, body, 0, unroll=True)


def slope_product(rows, weight, slope):
    count, depth = rows.shape
    width = weight.shape[1]
    block = 256
    tall = pl.BlockSpec((count, block), lambda j: (0, j))
    return pl.pallas_call(
        slope_kernel,
        grid=(width // block,),
        in_specs=[
            pl.BlockSpec((count, depth), lambda j: (0, 0)),
            pl.BlockSpec((depth, block), lambda j: (0, j)),
            tall,
        ],
        out_specs=tall,
        out_shape=jax.ShapeDtypeStruct((count, width), BF),
        cost_estimate=pl.CostEstimate(
            flops=2 * count * depth * width,
            transcendentals=0,
            bytes_accessed=2 * (count * depth + depth * width + 2 * count * width),
        ),
        name="slope_product",
    )(rows, weight, slope)


class Whole:
    def __init__(self, dp, tensor):
        self.dp, self.tensor = dp, tensor

    def arrange(self, values):
        return values

    def restore(self, values):
        return values

    def gather_norms(self, packed):
        return lax.all_gather(packed, self.dp, axis=0, tiled=True)

    def gather_first(self, shard):
        return lax.all_gather(shard, self.dp, axis=0, tiled=True)

    def gather_first_set(self, first, second, feed_in, feed_out, rows):
        return first, rows, (second, feed_in, feed_out)

    def place_pieces(self, first):
        return self.gather_first(first)

    def gather_rest(self, rest, value):
        second, feed_in, feed_out = [self.gather_first(shard) for shard in rest]
        return second, feed_in, None, None, (feed_out, None)

    def feed_out(self, pieces):
        return pieces[0]

    def after(self, value, *others):
        return value

    def stage(self, work, *values):
        return work(*values)

    def sends(self, left, right):
        return ()

    def exchange(self, sends):
        return ()

    def merged(self, *sends):
        return ()

    def parted(self, far, *widths):
        return [()] * len(widths)

    def adds(self, *products):
        wholes = [mm_rows(left, right).astype(BF) for left, right, _ in products]
        return jnp.concatenate(wholes, axis=1)

    def second(self, whole):
        return ()

    def closing(self, whole, far):
        return whole

    middle = closing

    def scatter_z(self, whole):
        return lax.psum_scatter(whole, self.dp, scatter_dimension=0, tiled=True)

    def close_middle(self, whole):
        return whole.astype(F32)

    def close_last(self, whole, *widths):
        found, at = [], 0
        for columns in widths:
            found.append(whole[:, at : at + columns].astype(F32))
            at += columns
        return found

    def norm_sums(self, sums):
        sums = jnp.pad(sums.T, ((0, 0), (0, 122))).astype(BF)
        sums = lax.psum_scatter(sums, self.dp, scatter_dimension=0, tiled=True)
        return self.sum_all(sums)[:, :6].T

    def spread(self, rows, clips):
        local = rows.reshape(clips, -1, rows.shape[-1])
        return lax.all_gather(local, self.tensor, axis=1, tiled=True).reshape(-1, rows.shape[-1])

    def sequence(self, rows, clips):
        return rows.reshape(clips, -1, rows.shape[-1])

    def unsequence(self, rows):
        return rows.reshape(-1, rows.shape[-1])

    def clip_rows(self, rows, clips):
        return rows.reshape(clips, -1, rows.shape[-1])

    unclip_rows = unsequence

    def self_attend(self, qkv, clips):
        qkv = self.sequence(qkv, clips)
        cols = qkv.shape[-1] // 3
        q, k, v = qkv[..., :cols], qkv[..., cols : 2 * cols], qkv[..., 2 * cols :]
        att, log_total = attend(q, k, v)
        return self.unsequence(att), (q, k, v, log_total)

    def self_back(self, saved, grad, clips):
        dq, dk, dv = attend_back(*saved, self.sequence(grad, clips))
        return self.unsequence(jnp.concatenate([dq, dk, dv], axis=-1))

    def cross_attend(self, q, memory, clips):
        q = self.clip_rows(q, clips)
        memory = memory.reshape(clips, -1, memory.shape[-1])
        cols = q.shape[-1]
        k, v = memory[..., :cols], memory[..., cols:]
        out, chances = cross_attend(q, k, v)
        return self.unclip_rows(out), (q, k, v, chances)

    def cross_back(self, saved, grad, clips):
        dq, dk, dv = cross_attend_back(*saved, self.clip_rows(grad, clips))
        return self.unclip_rows(dq), self.unsequence(jnp.concatenate([dk, dv], axis=-1))

    def feed(self, rows, weight):
        return gelu_pair(mm(rows, weight))

    def slope_product(self, rows, weight, slope):
        return (mm(rows, weight) * slope.astype(F32)).astype(BF)

    def sum_own(self, left, right, product, clips):
        part = product(left, right).astype(BF).reshape(clips, -1, right_width(product, right))
        own = lax.psum_scatter(part, self.tensor, scatter_dimension=1, tiled=True)
        return own.reshape(-1, part.shape[-1]).astype(F32)

    def sum_all(self, values):
        return lax.psum(values.astype(BF), self.tensor).astype(F32)


def right_width(product, right):
    return right.shape[0] if product is mm_t else right.shape[1]


class Block(Whole):
    def __init__(self, width):
        self.width = width
        self.shard = width // 16
        self.core = lax.axis_index("core")

    def after(self, value, *others):
        return tie(value, others)

    def order(self):
        own_y, own_x = lax.axis_index("y"), lax.axis_index("x")
        place = jnp.arange(self.width, dtype=jnp.int32)
        quarter, rest = place // (4 * self.shard), place % (4 * self.shard)
        z, row = rest // self.shard, rest % self.shard
        y, x = (quarter // 2) ^ own_y, (quarter % 2) ^ own_x
        source = ((z * 2 + y) * 2 + x) * self.shard + row
        return (jnp.arange(self.width, dtype=jnp.int32)[:, None] == source[None, :]).astype(BF)

    def arrange(self, values):
        return mm(values, self.order()).astype(BF)

    def restore(self, values):
        if values.dtype == BF:
            return mm_t(values, self.order()).astype(BF)
        high = lax.reduce_precision(values, 8, 7)
        low = (values - high).astype(BF)
        order = self.order()
        return mm_t(high.astype(BF), order) + mm_t(low, order)

    def x(self, v):
        return lax.ppermute(v, "x", SWAP)

    def y(self, v):
        return lax.ppermute(v, "y", SWAP)

    def other(self, v):
        return lax.ppermute(v, "core", SWAP)

    def gather_norms(self, packed):
        pair = jnp.stack([packed, lax.ppermute(packed, "z", [(0, 1), (1, 0), (2, 3), (3, 2)])])
        far = lax.ppermute(pair, "z", [(0, 2), (1, 3), (2, 0), (3, 1)])
        own = lax.axis_index("z")
        four = jnp.concatenate([pair, far])
        four = jnp.stack([lax.dynamic_index_in_dim(four, own ^ p, 0, False) for p in range(4)])
        two = jnp.stack([four, self.x(four)])
        whole = jnp.stack([two, self.y(two)])
        return whole.reshape(self.width, packed.shape[-1])

    def halves(self, shard):
        half = shard.shape[1] // 256 * 128
        return shard[:, :half], shard[:, half:]

    def gather_first_set(self, first, second, feed_in, feed_out, rows):
        opened = []
        for shard in (feed_in, feed_out):
            a, b = self.halves(shard)
            opened.append(jnp.stack([a, self.x(a), b, self.y(b)]))
        rows, opened = lax.optimization_barrier((rows, opened))
        sets = [lax.all_gather(shard, "z", axis=0, tiled=True) for shard in (first, second)]
        feeds = [lax.all_gather(four, "z", axis=1, tiled=True) for four in opened]
        pieces, last, _ = self.gather_pieces(sets[0], rows)
        pieces_next = self.gather_pieces(sets[1], last)
        return pieces, rows, (pieces_next, feeds)

    def gather_pieces(self, four, last):
        a, b = self.halves(tie(four, last))
        xa, yb, ya, xb = self.x(a), self.y(b), self.y(a), self.x(b)
        far_a, far_b = self.y(xa), self.x(yb)
        return (four, xa, ya, far_a, xb, yb, far_b), (far_a, far_b, ya, xb), (xa, yb)

    def place_pieces(self, pieces):
        four, xa, ya, far_a, xb, yb, far_b = pieces
        n, half = xa.shape
        return place(
            [
                (four, 0, 0),
                (xa, n, 0),
                (ya, 2 * n, 0),
                (far_a, 3 * n, 0),
                (xb, n, half),
                (yb, 2 * n, half),
                (far_b, 3 * n, half),
            ],
            (4 * n, four.shape[1]),
        )

    def gather_rest(self, rest, value):
        (pieces, last, _), feeds = rest
        feeds[0] = tie(feeds[0], value)
        in_sides = feeds[0][:2], feeds[0][2:]
        a, b = tie(in_sides, last)
        in_far = self.y(a), self.x(b)
        w_cross = self.place_pieces(pieces)
        w_in = self.place_feed(feeds[0], in_far)
        out_sides = feeds[1][:2], feeds[1][2:]
        a, b = tie(out_sides, in_far)
        return w_cross, w_in, in_far, out_sides, (feeds[1], (self.y(a), self.x(b)))

    def place_feed(self, four, far):
        _, n, half = four.shape
        return place_stacked(
            four.reshape(4 * n, half), far[0].reshape(2 * n, half), far[1].reshape(2 * n, half)
        )

    def feed_out(self, pieces):
        return self.place_feed(*pieces)

    def stage(self, work, *values):
        shapes = jax.eval_shape(work, *values)

        def nothing(*_):
            return jax.tree.map(lambda leaf: jnp.zeros(leaf.shape, leaf.dtype), shapes)

        return lax.cond(self.core < 2, work, nothing, *values)

    def sends(self, left, right):
        n, half = self.width // 4, right.shape[1] // 256 * 128
        far = jnp.concatenate([left[:, n : 2 * n], left[:, 3 * n :]], axis=1)
        return (
            mm_rows(left[:, 2 * n :], right[:, :half]).astype(BF),
            mm_rows(far, right[:, half:]).astype(BF),
        )

    def exchange(self, sends):
        return self.y(sends[0]), self.x(sends[1])

    def merged(self, *sends):
        return [jnp.concatenate(side, axis=1) for side in zip(*sends)]

    def parted(self, far, *widths):
        halves = [width // 256 * 128 for width in widths]
        ends = [sum(halves[: i + 1]) for i in range(len(halves) - 1)]
        lefts = jnp.split(far[0], ends, axis=1)
        halves = [width - half for width, half in zip(widths, halves)]
        ends = [sum(halves[: i + 1]) for i in range(len(halves) - 1)]
        return list(zip(lefts, jnp.split(far[1], ends, axis=1)))

    def adds(self, *products):
        n, parts = self.width // 4, []
        for left, right, (far_y, far_x) in products:
            half = right.shape[1] // 256 * 128
            first = (mm_rows(left[:, : 2 * n], right[:, :half]) + far_y.astype(F32)).astype(BF)
            near = jnp.concatenate([left[:, :n], left[:, 2 * n : 3 * n]], axis=1)
            last = (mm_rows(near, right[:, half:]) + far_x.astype(F32)).astype(BF)
            parts.append((first[:n], first[n:], last[:n], last[n:]))
        return [jnp.concatenate(part, axis=1) for part in zip(*parts)]

    def middle(self, parts, _):
        return jnp.stack(parts)

    def second(self, parts):
        return self.x(parts[1]), self.y(parts[3])

    def closing(self, parts, far):
        pairs = zip((parts[0], parts[2]), far)
        return jnp.stack([(own.astype(F32) + other.astype(F32)).astype(BF) for own, other in pairs])

    def scatter_z(self, parts):
        return lax.psum_scatter(parts, "z", scatter_dimension=1, tiled=True)

    def close_middle(self, four):
        left = four[0].astype(F32) + self.x(four[1]).astype(F32)
        right = four[2].astype(F32) + self.y(four[3]).astype(F32)
        return jnp.concatenate([left, right], axis=1)

    def close_last(self, both, *widths):
        found, left, right = [], 0, 0
        for columns in widths:
            a = columns // 256 * 128
            b = columns - a
            found.append(
                jnp.concatenate([both[0, :, left : left + a], both[1, :, right : right + b]], axis=1)
            )
            left, right = left + a, right + b
        return [part.astype(F32) for part in found]

    def norm_sums(self, sums):
        n = self.width // 4
        sums = self.sum_all(jnp.pad(sums.T, ((0, 0), (0, 122))))
        sums = sums[: 2 * n] + self.y(sums[2 * n :].astype(BF)).astype(F32)
        sums = sums[:n] + self.x(sums[n:].astype(BF)).astype(F32)
        own = lax.axis_index("z")
        for step, pairs, side in (
            (n // 2, [(0, 2), (1, 3), (2, 0), (3, 1)], own // 2),
            (n // 4, [(0, 1), (1, 0), (2, 3), (3, 2)], own % 2),
        ):
            near = lax.dynamic_slice_in_dim(sums, side * step, step)
            away = lax.dynamic_slice_in_dim(sums, (1 - side) * step, step)
            sums = near + lax.ppermute(away.astype(BF), "z", pairs).astype(F32)
        return sums[:, :6].T

    def spread(self, rows, clips):
        return jnp.concatenate([rows, self.other(rows)])

    def self_attend(self, qkv, clips):
        cols = qkv.shape[-1] // 3
        steps = cols // (2 * HEAD_DIM)
        view = qkv.reshape(2, clips, -1, qkv.shape[-1])
        frames = view.shape[2]

        def block(part):
            return pl.BlockSpec(
                (2, 1, frames, 2 * HEAD_DIM), lambda c, j, _: (0, c, 0, part * steps + j)
            )

        shape = (2, clips, frames, cols)
        core = self.core.reshape(1).astype(jnp.int32)
        scores = clips * steps * 2 * 3 * frames * frames
        out, log_total = pl.pallas_call(
            self_kernel,
            grid_spec=pltpu.PrefetchScalarGridSpec(
                num_scalar_prefetch=1,
                grid=(clips, steps),
                in_specs=[block(0), block(1), block(2)],
                out_specs=[block(0), block(0)],
            ),
            out_shape=[jax.ShapeDtypeStruct(shape, BF), jax.ShapeDtypeStruct(shape, F32)],
            cost_estimate=pl.CostEstimate(
                flops=4 * scores * HEAD_DIM,
                transcendentals=scores,
                bytes_accessed=2 * qkv.size + 6 * qkv.size // 3,
            ),
            name="self_attend",
        )(core, view, view, view)
        return out.reshape(-1, cols), (core, view, log_total)

    def self_back(self, saved, grad, clips):
        core, view, log_total = saved
        cols = view.shape[-1] // 3
        steps = cols // (2 * HEAD_DIM)
        frames = view.shape[2]

        def block(part):
            return pl.BlockSpec(
                (2, 1, frames, 2 * HEAD_DIM), lambda c, j, _: (0, c, 0, part * steps + j)
            )

        scores = clips * steps * 2 * 3 * frames * frames
        out = pl.pallas_call(
            self_back_kernel,
            grid_spec=pltpu.PrefetchScalarGridSpec(
                num_scalar_prefetch=1,
                grid=(clips, steps),
                in_specs=[block(0), block(1), block(2), block(0), block(0)],
                out_specs=pl.BlockSpec((2, 1, frames, 3 * cols), lambda c, j, _: (0, c, 0, 0)),
            ),
            out_shape=jax.ShapeDtypeStruct(view.shape, BF),
            cost_estimate=pl.CostEstimate(
                flops=10 * scores * HEAD_DIM,
                transcendentals=scores,
                bytes_accessed=4 * view.size + 6 * view.size // 3,
            ),
            name="self_back",
        )(core, view, view, view, log_total, grad.reshape(2, clips, frames, cols))
        return out.reshape(-1, 3 * cols)

    def cross_specs(self, q, clips, texts):
        cols = q.shape[-1]
        steps = cols // (2 * HEAD_DIM)
        view = q.reshape(2, clips, -1, cols)
        frames = view.shape[2]
        wide = pl.BlockSpec((2, 1, frames, 2 * HEAD_DIM), lambda c, j: (0, c, 0, j))

        def block(part):
            return pl.BlockSpec((1, texts, 2 * HEAD_DIM), lambda c, j: (c, 0, part * steps + j))

        return view, (clips, steps), wide, block, clips * 2 * frames * cols * texts

    def cross_attend(self, q, memory, clips):
        memory = memory.reshape(clips, -1, memory.shape[-1])
        view, grid, wide, block, work = self.cross_specs(q, clips, memory.shape[1])
        out = pl.pallas_call(
            cross_kernel,
            grid=grid,
            in_specs=[wide, block(0), block(1)],
            out_specs=wide,
            out_shape=jax.ShapeDtypeStruct(view.shape, BF),
            cost_estimate=pl.CostEstimate(
                flops=4 * work, transcendentals=work // HEAD_DIM, bytes_accessed=4 * q.size
            ),
            name="cross_attend",
        )(view, memory, memory)
        return out.reshape(q.shape), (q, memory)

    def cross_back(self, saved, grad, clips):
        q, memory = saved
        texts = memory.shape[1]
        view, grid, wide, block, work = self.cross_specs(q, clips, texts)
        dq, dkv = pl.pallas_call(
            cross_back_kernel,
            grid=grid,
            in_specs=[wide, block(0), block(1), wide],
            out_specs=[
                wide,
                pl.BlockSpec((1, texts, memory.shape[-1]), lambda c, j: (c, 0, 0)),
            ],
            out_shape=[
                jax.ShapeDtypeStruct(view.shape, BF),
                jax.ShapeDtypeStruct(memory.shape, BF),
            ],
            cost_estimate=pl.CostEstimate(
                flops=10 * work, transcendentals=work // HEAD_DIM, bytes_accessed=6 * q.size
            ),
            name="cross_back",
        )(view, memory, memory, grad.reshape(view.shape))
        return dq.reshape(q.shape), dkv.reshape(-1, memory.shape[-1])

    def feed(self, rows, weight):
        return feed(rows, weight)

    def slope_product(self, rows, weight, slope):
        return slope_product(rows, weight, slope)

    def sum_own(self, left, right, product, clips):
        n = left.shape[0] // 2
        far = self.other(product(left[n:], right).astype(BF))
        return product(left[:n], right) + far.astype(F32)

    def sum_all(self, values):
        return values + self.other(values.astype(BF)).astype(F32)


def layer(
    comm,
    frames,
    text_states,
    norm_gain,
    norm_shift,
    self_project,
    self_output,
    cross_query,
    cross_memory,
    cross_output,
    feed_input,
    feed_output,
    upstream,
):
    clips, own_frames, width = frames.shape
    texts = text_states.shape[1]
    cols = cross_query.shape[1]
    own_rows = clips * own_frames

    def catenate(parts):
        return jnp.concatenate(parts, axis=1)

    norms = comm.gather_norms(
        jnp.pad(jnp.concatenate([norm_gain, norm_shift]).T, ((0, 0), (0, 122)))
    )
    norms = norms.T.astype(F32)
    gain, shift = norms[0:3], norms[3:6]
    first_set = catenate([self_project[0], self_project[1], self_project[2]])
    second_set = catenate(
        [self_output.T, cross_query, cross_memory[0], cross_memory[1], cross_output.T]
    )
    values0 = comm.arrange(frames.reshape(own_rows, width)).astype(F32)
    stats0 = norm_stats(values0)
    own_n1 = norm_apply(values0, stats0, gain[0], shift[0])
    pieces, own_n1, rest = comm.gather_first_set(
        first_set, second_set, feed_input, feed_output.T, own_n1
    )
    up = comm.arrange(upstream.reshape(own_rows, width))
    text = comm.arrange(text_states.reshape(clips * texts, width))
    up_all = comm.spread(up, clips)

    n1 = comm.spread(own_n1, clips)

    def split_cross(weights):
        return jnp.split(weights, [cols, 2 * cols, 4 * cols], axis=1)

    def stage_self(pieces, n1):
        w_self = comm.place_pieces(pieces)
        return w_self, comm.self_attend(mm(n1, w_self).astype(BF), clips)

    w_self, (att, self_saved) = comm.stage(stage_self, pieces, n1)
    w_cross, w_in, mark_in, mark_out, out_pieces = comm.gather_rest(rest, att)

    def stage0(values0, att, w_cross, text):
        w_so, w_cq, w_cm, w_co = split_cross(w_cross)
        values1 = values0 + comm.sum_own(att, w_so, mm_t, clips)
        stats1 = norm_stats(values1)
        n2 = comm.spread(norm_apply(values1, stats1, gain[1], shift[1]), clips)
        cross, saved = comm.cross_attend(
            mm(n2, w_cq).astype(BF), mm(text, w_cm).astype(BF), clips
        )
        values2 = values1 + comm.sum_own(cross, w_co, mm_t, clips)
        stats2 = norm_stats(values2)
        n3 = comm.spread(norm_apply(values2, stats2, gain[2], shift[2]), clips)
        return values1, stats1, n2, cross, saved, values2, stats2, n3

    values1, stats1, n2, cross, cross_saved, values2, stats2, n3 = comm.stage(
        stage0, values0, att, w_cross, text
    )
    n3 = comm.after(n3, mark_in, mark_out)
    hidden, slope = comm.feed(n3, w_in)
    send_out = comm.sends(up_all, hidden)
    hidden, slope = comm.after((hidden, slope), out_pieces[1], send_out)
    far_out = comm.exchange(send_out)

    def stage1(pieces, rows, slope, n3, w_in):
        w_out = comm.feed_out(pieces)
        pre_grad = comm.slope_product(rows, w_out, slope)
        return w_out, pre_grad, comm.sends(n3, pre_grad), comm.sum_own(pre_grad, w_in, mm_t, clips)

    w_out, pre_grad, send_in, e3 = comm.stage(stage1, out_pieces, up_all, slope, n3, w_in)
    e3 = comm.after(e3, far_out)
    far_in = comm.exchange(send_in)

    def stage2(rows, hidden, far, e3, values2, stats2, own):
        sent = comm.middle(comm.adds((rows, hidden, far)), None)
        grads = norm_back(values2, stats2, gain[2], e3)
        r2 = own.astype(F32) + grads[0]
        return sent, r2, r2.astype(BF), grads[1], grads[2]

    sent_out, r2, r2_own, gain2, shift2 = comm.stage(
        stage2, up_all, hidden, far_out, e3, values2, stats2, up
    )
    half_out = comm.scatter_z(sent_out)

    def stage3(r2_own, saved, w_cross, n2, cross, text):
        w_co = split_cross(w_cross)[3]
        r2_all = comm.spread(r2_own, clips)
        dcq, dmem = comm.cross_back(saved, mm(r2_all, w_co).astype(BF), clips)
        pairs = (n2, dcq), (r2_all, cross), (text, dmem)
        return r2_all, dcq, dmem, comm.merged(*[comm.sends(*pair) for pair in pairs])

    r2_all, dcq, dmem, send_cross = comm.stage(
        stage3, r2_own, cross_saved, w_cross, n2, cross, text
    )
    dcq = comm.after(dcq, far_in)
    far_cross = comm.exchange(send_cross)
    cross_pairs = (n2, dcq), (r2_all, cross), (text, dmem)

    def stage4(n3, pre_grad, far, dcq, w_cross, values1, stats1, r2):
        w_so, w_cq, *_ = split_cross(w_cross)
        in_sums = comm.adds((n3, pre_grad, far))
        e2 = comm.sum_own(dcq, w_cq, mm_t, clips)
        grads = norm_back(values1, stats1, gain[1], e2)
        r1 = r2 + grads[0]
        r1_all = comm.spread(r1.astype(BF), clips)
        return in_sums, r1, r1_all, mm(r1_all, w_so).astype(BF), grads[1], grads[2]

    in_sums, r1, r1_all, datt, gain1, shift1 = comm.stage(
        stage4, n3, pre_grad, far_in, dcq, w_cross, values1, stats1, r2
    )
    datt = comm.after(datt, far_cross, half_out)
    in_second = comm.second(in_sums)

    def stage5(pairs, far, r1_all, att):
        far = comm.parted(far, cols, cols, 2 * cols)
        sums = comm.adds(*[(*pair, one) for pair, one in zip(pairs, far)])
        return sums, comm.sends(r1_all, att)

    cross_sums, send_so = comm.stage(stage5, cross_pairs, far_cross, r1_all, att)
    datt, in_late = comm.after((datt, in_sums), in_second, send_so)
    cross_second = comm.second(cross_sums)
    far_so = comm.exchange(send_so)
    half_in = comm.scatter_z(comm.closing(in_late, in_second))

    def stage_back(saved, datt, n1):
        dqkv = comm.self_back(saved, datt, clips)
        return dqkv, comm.sends(n1, dqkv)

    dqkv, send_self = comm.stage(stage_back, self_saved, datt, n1)
    dmem, hidden, send_self, cross_late, dqkv, far_so = comm.after(
        (dmem, hidden, send_self, cross_sums, dqkv, far_so), cross_second, half_in
    )
    far_self = comm.exchange(send_self)
    half_cross = comm.scatter_z(comm.closing(cross_late, cross_second))

    def stage6(dmem, w_cross, values2, hidden, w_out):
        w_cm = split_cross(w_cross)[2]
        text_grad = comm.sum_all(mm_t(dmem, w_cm))
        layer_out = (values2 + comm.sum_own(hidden, w_out, mm_t, clips)).astype(BF)
        return comm.restore(text_grad), comm.restore(layer_out)

    text_grad, layer_out = comm.stage(stage6, dmem, w_cross, values2, hidden, w_out)
    text_grad, layer_out, dqkv, half_out, half_in = comm.after(
        (text_grad, layer_out, dqkv, half_out, half_in), far_self, half_cross
    )
    self_sums = comm.adds((r1_all, att, far_so), (n1, dqkv, far_self))
    dqkv = comm.after(dqkv, self_sums)
    self_second = comm.second(self_sums)

    def stage7(dqkv, w_self):
        return comm.sum_own(dqkv, w_self, mm_t, clips)

    e1 = comm.stage(stage7, dqkv, w_self)
    e1, self_late = comm.after((e1, self_sums), self_second)
    half_self = comm.scatter_z(comm.closing(self_late, self_second))
    dv0, gain0, shift0 = norm_back(values0, stats0, gain[0], e1)
    input_grad = comm.restore(r1 + dv0)
    norm_grad = comm.norm_sums(jnp.stack([gain0, gain1, gain2, shift0, shift1, shift2]))
    input_grad = input_grad.reshape(clips, own_frames, width)
    text_grad = text_grad.reshape(clips, texts, width)
    layer_out = layer_out.reshape(clips, own_frames, width)
    grad_out = comm.close_middle(half_out)
    (grad_in,) = comm.close_last(half_in, pre_grad.shape[1])
    grad_cq, grad_co, grad_cm = comm.close_last(half_cross, cols, cols, 2 * cols)
    grad_so, grad_self = comm.close_last(half_self, cols, 3 * cols)
    return (
        layer_out,
        input_grad,
        text_grad,
        norm_grad[0:3],
        norm_grad[3:6],
        jnp.stack([grad_self[:, i * cols : (i + 1) * cols] for i in range(3)]),
        grad_so.T,
        grad_cq,
        jnp.stack([grad_cm[:, :cols], grad_cm[:, cols:]]),
        grad_co.T,
        grad_in,
        grad_out.T,
    )


def specs(dp, tensor):
    in_specs = (
        P(dp, tensor, None),
        P(dp, None, None),
        P(None, dp),
        P(None, dp),
        P(None, dp, tensor),
        P(tensor, dp),
        P(dp, tensor),
        P(None, dp, tensor),
        P(tensor, dp),
        P(dp, tensor),
        P(tensor, dp),
        P(dp, tensor, None),
    )
    out_specs = (
        P(dp, tensor, None),
        P(dp, tensor, None),
        P(dp, None, None),
        P(None, dp),
        P(None, dp),
        P(None, dp, tensor),
        P(tensor, dp),
        P(dp, tensor),
        P(None, dp, tensor),
        P(tensor, dp),
        P(dp, tensor),
        P(tensor, dp),
    )
    return in_specs, out_specs


def solution(mesh):
    if mesh.shape["dp"] == 16 and mesh.shape["tensor"] == 2:
        mesh = Mesh(mesh.devices.reshape(4, 2, 2, 2), ("z", "y", "x", "core"))
        in_specs, out_specs = specs(("z", "y", "x"), "core")

        def per_device(frames, *rest):
            return layer(Block(frames.shape[-1]), frames, *rest)
    else:
        in_specs, out_specs = specs("dp", "tensor")

        def per_device(frames, *rest):
            return layer(Whole("dp", "tensor"), frames, *rest)

    return jax.shard_map(
        per_device, mesh=mesh, in_specs=in_specs, out_specs=out_specs, check_vma=False
    )
```

```python
import math

import jax
import jax.numpy as jnp
from jax import lax
from jax.experimental import pallas as pl
from jax.experimental.pallas import tpu as pltpu
from jax.sharding import Mesh
from jax.sharding import PartitionSpec as P

HEAD_DIM = 64
EPS = 1e-05
BF = jnp.bfloat16
F32 = jnp.float32
SWAP = [(0, 1), (1, 0)]


def mm(left, right):
    return jnp.dot(left, right, preferred_element_type=F32)


def mm_t(left, right):
    return lax.dot_general(left, right, (((1,), (1,)), ((), ())), preferred_element_type=F32)


def mm_rows(left, right):
    return lax.dot_general(left, right, (((0,), (0,)), ((), ())), preferred_element_type=F32)


def tie(value, *others):
    return lax.optimization_barrier((value, others))[0]


def norm_stats(values):
    mean = jnp.mean(values, axis=-1, keepdims=True)
    centred = values - mean
    inv = lax.rsqrt(jnp.mean(centred * centred, axis=-1, keepdims=True) + EPS)
    return mean, inv


def norm_apply(values, stats, gain, shift):
    return ((values - stats[0]) * stats[1] * gain + shift).astype(BF)


def norm_back(values, stats, gain, grad):
    xhat = (values - stats[0]) * stats[1]
    scaled = grad * gain
    part = jnp.mean(scaled, axis=-1, keepdims=True)
    cross = jnp.mean(scaled * xhat, axis=-1, keepdims=True)
    value_grad = (scaled - part - xhat * cross) * stats[1]
    return value_grad, jnp.sum(grad * xhat, axis=0), jnp.sum(grad, axis=0)


def gelu_pair(pre):
    phi = 0.5 * (1.0 + lax.erf(pre * (1.0 / math.sqrt(2.0))))
    dens = jnp.exp(-0.5 * pre * pre) * (1.0 / math.sqrt(2.0 * math.pi))
    return (pre * phi).astype(BF), (phi + pre * dens).astype(BF)


def heads(matrix):
    return matrix.reshape(*matrix.shape[:-1], matrix.shape[-1] // HEAD_DIM, HEAD_DIM)


def flat(matrix):
    return matrix.reshape(*matrix.shape[:-2], -1)


SCALE = 1.0 / math.sqrt(HEAD_DIM)


def causal_scores(q, k):
    scores = jnp.einsum("bqhd,bkhd->bhqk", heads(q), heads(k), preferred_element_type=F32) * SCALE
    n = q.shape[1]
    allowed = jnp.arange(n)[None, :] <= jnp.arange(n)[:, None]
    return jnp.where(allowed, scores, -1e30)


def attend(q, k, v):
    scores = causal_scores(q, k)
    top = jnp.max(scores, axis=-1, keepdims=True)
    terms = jnp.exp(scores - top)
    total = jnp.sum(terms, axis=-1, keepdims=True)
    out = jnp.einsum(
        "bhqk,bkhd->bqhd", (terms / total).astype(BF), heads(v), preferred_element_type=F32
    )
    return flat(out).astype(BF), top + jnp.log(total)


def probs_back(chances, dp, q, k, grad):
    dot = jnp.sum(chances * dp, axis=-1, keepdims=True)
    ds = (chances * (dp - dot)).astype(BF)
    dv = jnp.einsum("bhqk,bqhd->bkhd", chances.astype(BF), grad, preferred_element_type=F32)
    dq = jnp.einsum("bhqk,bkhd->bqhd", ds, heads(k), preferred_element_type=F32) * SCALE
    dk = jnp.einsum("bhqk,bqhd->bkhd", ds, heads(q), preferred_element_type=F32) * SCALE
    return flat(dq).astype(BF), flat(dk).astype(BF), flat(dv).astype(BF)


def attend_back(q, k, v, log_total, grad):
    chances = jnp.exp(causal_scores(q, k) - log_total)
    grad = heads(grad)
    dp = jnp.einsum("bqhd,bkhd->bhqk", grad, heads(v), preferred_element_type=F32)
    return probs_back(chances, dp, q, k, grad)


def cross_attend(q, k, v):
    scores = jnp.einsum("bqhd,bkhd->bhqk", heads(q), heads(k), preferred_element_type=F32) * SCALE
    chances = jax.nn.softmax(scores, axis=-1)
    out = jnp.einsum("bhqk,bkhd->bqhd", chances.astype(BF), heads(v), preferred_element_type=F32)
    return flat(out).astype(BF), chances


def cross_attend_back(q, k, v, chances, grad):
    grad = heads(grad)
    dp = jnp.einsum("bqhd,bkhd->bhqk", grad, heads(v), preferred_element_type=F32)
    return probs_back(chances, dp, q, k, grad)

ANY = pl.BlockSpec(memory_space=pl.ANY)
NEG = -1e30


def place_kernel(*refs, spots):
    sources, out, sems = refs[: len(spots)], refs[len(spots)], refs[len(spots) + 1]
    copies = []
    for i, (source, (row, col)) in enumerate(zip(sources, spots)):
        rows, cols = source.shape
        copies.append(
            pltpu.make_async_copy(
                source, out.at[pl.ds(row, rows), pl.ds(col, cols)], sems.at[i]
            )
        )
    for copy in copies:
        copy.start()
    for copy in copies:
        copy.wait()


def place(pieces, shape):
    spots = tuple((row, col) for _, row, col in pieces)
    return pl.pallas_call(
        lambda *refs: place_kernel(*refs, spots=spots),
        out_shape=jax.ShapeDtypeStruct(shape, pieces[0][0].dtype),
        in_specs=[ANY] * len(pieces),
        out_specs=pl.BlockSpec(memory_space=pltpu.VMEM),
        scratch_shapes=[pltpu.SemaphoreType.DMA((len(pieces),))],
        name="place",
    )(*[piece for piece, _, _ in pieces])


def place_stacked_kernel(four, far_a, far_b, out, sems):
    n, half = four.shape[0] // 4, four.shape[1]
    spots = [
        (four, 0, 2 * n, 0, 0),
        (far_a, 0, 2 * n, 2 * n, 0),
        (four, 2 * n, n, 0, half),
        (far_b, 0, n, n, half),
        (four, 3 * n, n, 2 * n, half),
        (far_b, n, n, 3 * n, half),
    ]
    copies = [
        pltpu.make_async_copy(
            source.at[pl.ds(start, rows)], out.at[pl.ds(row, rows), pl.ds(col, half)], sems.at[i]
        )
        for i, (source, start, rows, row, col) in enumerate(spots)
    ]
    for copy in copies:
        copy.start()
    for copy in copies:
        copy.wait()


def place_stacked(four, far_a, far_b):
    return pl.pallas_call(
        place_stacked_kernel,
        out_shape=jax.ShapeDtypeStruct((four.shape[0], 2 * four.shape[1]), four.dtype),
        in_specs=[ANY] * 3,
        out_specs=pl.BlockSpec(memory_space=pltpu.VMEM),
        scratch_shapes=[pltpu.SemaphoreType.DMA((6,))],
        name="place_stacked",
    )(four, far_a, far_b)


def rows_of(matrix, grad):
    return lax.dot_general(matrix, grad, (((0,), (0,)), ((), ())), preferred_element_type=F32)


def head_of(ref, half, head):
    return ref[half, 0, :, head * HEAD_DIM : (head + 1) * HEAD_DIM]


def masked(scores):
    n = scores.shape[0]
    rows = lax.broadcasted_iota(jnp.int32, (n, n), 0)
    cols = lax.broadcasted_iota(jnp.int32, (n, n), 1)
    return jnp.where(cols <= rows, scores, NEG)


def self_kernel(core_ref, q_ref, k_ref, v_ref, out_ref, log_ref):
    halves = (core_ref[0], 1 - core_ref[0])
    outs, logs = ([], []), ([], [])
    for head in range(2):
        q = [head_of(q_ref, h, head) * BF(SCALE) for h in halves]
        k = [head_of(k_ref, h, head) for h in halves]
        v = [head_of(v_ref, h, head) for h in halves]
        first = masked(mm_t(q[0], k[0]))
        for half, scores in enumerate([[first], [mm_t(q[1], k[0]), masked(mm_t(q[1], k[1]))]]):
            top = jnp.max(scores[0], axis=-1, keepdims=True)
            if half:
                top = jnp.maximum(top, jnp.max(scores[1], axis=-1, keepdims=True))
            terms = [jnp.exp(part - top) for part in scores]
            total = sum(jnp.sum(part, axis=-1, keepdims=True) for part in terms)
            inverse = 1.0 / total
            out = sum(mm((part * inverse).astype(BF), v[i]) for i, part in enumerate(terms))
            outs[half].append(out.astype(BF))
            logs[half].append(jnp.broadcast_to(top + jnp.log(total), out.shape))
    for half, h in enumerate(halves):
        out_ref[h, 0] = jnp.concatenate(outs[half], axis=1)
        log_ref[h, 0] = jnp.concatenate(logs[half], axis=1)


def self_back_kernel(core_ref, q_ref, k_ref, v_ref, log_ref, grad_ref, out_ref):
    halves = (core_ref[0], 1 - core_ref[0])
    found = [[], [], [], [], [], []]
    for head in range(2):
        q = [head_of(q_ref, h, head) * BF(SCALE) for h in halves]
        k = [head_of(k_ref, h, head) for h in halves]
        ks = [part * BF(SCALE) for part in k]
        v = [head_of(v_ref, h, head) for h in halves]
        log = [head_of(log_ref, h, head)[:, :1] for h in halves]
        grad = [head_of(grad_ref, h, head) for h in halves]
        dq, dk, dv = [0.0, 0.0], [0.0, 0.0], [0.0, 0.0]
        for half, parts in enumerate([(0,), (0, 1)]):
            chances, dps = [], []
            for i in parts:
                scores = mm_t(q[half], k[i])
                if i == half:
                    scores = masked(scores)
                chances.append(jnp.exp(scores - log[half]))
                dps.append(mm_t(grad[half], v[i]))
            dot = sum(
                jnp.sum(c * dp, axis=-1, keepdims=True) for c, dp in zip(chances, dps)
            )
            for i, c, dp in zip(parts, chances, dps):
                ds = (c * (dp - dot)).astype(BF)
                dv[i] += rows_of(c.astype(BF), grad[half])
                dk[i] += rows_of(ds, q[half])
                dq[half] += mm(ds, ks[i])
        for i, part in enumerate(dq + dk + dv):
            found[i].append(part.astype(BF))
    width = out_ref.shape[-1] // 3
    for i in range(3):
        col = pl.multiple_of(i * width + pl.program_id(1) * 2 * HEAD_DIM, 2 * HEAD_DIM)
        for half, h in enumerate(halves):
            out_ref[h, 0, :, pl.ds(col, 2 * HEAD_DIM)] = jnp.concatenate(
                found[2 * i + half], axis=1
            )


def cross_parts(q_ref, k_ref, head):
    cs = slice(head * HEAD_DIM, (head + 1) * HEAD_DIM)
    q = jnp.concatenate([q_ref[0, 0, :, cs], q_ref[1, 0, :, cs]]) * BF(SCALE)
    scores = mm_t(q, k_ref[0, :, cs])
    terms = jnp.exp(scores - jnp.max(scores, axis=-1, keepdims=True))
    return q, terms * (1.0 / jnp.sum(terms, axis=-1, keepdims=True)), cs


def cross_kernel(q_ref, k_ref, v_ref, out_ref):
    outs = []
    for head in range(2):
        _, chances, cs = cross_parts(q_ref, k_ref, head)
        outs.append(mm(chances.astype(BF), v_ref[0, :, cs]).astype(BF))
    out = jnp.concatenate(outs, axis=1)
    n = out.shape[0] // 2
    out_ref[0, 0], out_ref[1, 0] = out[:n], out[n:]


def cross_back_kernel(q_ref, k_ref, v_ref, grad_ref, dq_ref, dkv_ref):
    found = [[], [], []]
    for head in range(2):
        q, chances, cs = cross_parts(q_ref, k_ref, head)
        grad = jnp.concatenate([grad_ref[0, 0, :, cs], grad_ref[1, 0, :, cs]])
        dp = mm_t(grad, v_ref[0, :, cs])
        ds = (chances * (dp - jnp.sum(chances * dp, axis=-1, keepdims=True))).astype(BF)
        found[0].append(mm(ds, k_ref[0, :, cs] * BF(SCALE)).astype(BF))
        found[1].append(rows_of(ds, q).astype(BF))
        found[2].append(rows_of(chances.astype(BF), grad).astype(BF))
    dq, dk, dv = [jnp.concatenate(parts, axis=1) for parts in found]
    n = dq.shape[0] // 2
    dq_ref[0, 0], dq_ref[1, 0] = dq[:n], dq[n:]
    width = dkv_ref.shape[-1] // 2
    for i, part in enumerate([dk, dv]):
        col = pl.multiple_of(i * width + pl.program_id(1) * 2 * HEAD_DIM, 2 * HEAD_DIM)
        dkv_ref[0, :, pl.ds(col, 2 * HEAD_DIM)] = part


def feed_kernel(rows_ref, weight_ref, hidden_ref, slope_ref):
    step = 256

    def body(i, carry):
        at = pl.ds(pl.multiple_of(i * step, step), step)
        hidden_ref[at], slope_ref[at] = gelu_pair(mm(rows_ref[at], weight_ref[...]))
        return carry

    lax.fori_loop(0, rows_ref.shape[0] // step, body, 0, unroll=True)


def feed(rows, weight):
    count, depth = rows.shape
    width = weight.shape[1]
    block = 256
    out = jax.ShapeDtypeStruct((count, width), BF)
    return pl.pallas_call(
        feed_kernel,
        grid=(width // block,),
        in_specs=[
            pl.BlockSpec((count, depth), lambda j: (0, 0)),
            pl.BlockSpec((depth, block), lambda j: (0, j)),
        ],
        out_specs=[pl.BlockSpec((count, block), lambda j: (0, j))] * 2,
        out_shape=[out, out],
        cost_estimate=pl.CostEstimate(
            flops=2 * count * depth * width,
            transcendentals=2 * count * width,
            bytes_accessed=2 * (count * depth + depth * width + 2 * count * width),
        ),
        name="feed",
    )(rows, weight)


def slope_kernel(rows_ref, weight_ref, slope_ref, out_ref):
    step = 256

    def body(i, carry):
        at = pl.ds(pl.multiple_of(i * step, step), step)
        grad = mm(rows_ref[at], weight_ref[...])
        out_ref[at] = (grad * slope_ref[at].astype(F32)).astype(BF)
        return carry

    lax.fori_loop(0, rows_ref.shape[0] // step, body, 0, unroll=True)


def slope_product(rows, weight, slope):
    count, depth = rows.shape
    width = weight.shape[1]
    block = 256
    tall = pl.BlockSpec((count, block), lambda j: (0, j))
    return pl.pallas_call(
        slope_kernel,
        grid=(width // block,),
        in_specs=[
            pl.BlockSpec((count, depth), lambda j: (0, 0)),
            pl.BlockSpec((depth, block), lambda j: (0, j)),
            tall,
        ],
        out_specs=tall,
        out_shape=jax.ShapeDtypeStruct((count, width), BF),
        cost_estimate=pl.CostEstimate(
            flops=2 * count * depth * width,
            transcendentals=0,
            bytes_accessed=2 * (count * depth + depth * width + 2 * count * width),
        ),
        name="slope_product",
    )(rows, weight, slope)


class Whole:
    def __init__(self, dp, tensor):
        self.dp, self.tensor = dp, tensor

    def arrange(self, values):
        return values

    def restore(self, values):
        return values

    def gather_norms(self, packed):
        return lax.all_gather(packed, self.dp, axis=0, tiled=True)

    def gather_first(self, shard):
        return lax.all_gather(shard, self.dp, axis=0, tiled=True)

    def gather_first_set(self, first, second, feed_in, feed_out, rows):
        return first, rows, (second, feed_in, feed_out)

    def place_pieces(self, first):
        return self.gather_first(first)

    def gather_rest(self, rest, value):
        second, feed_in, feed_out = [self.gather_first(shard) for shard in rest]
        return second, feed_in, None, None, (feed_out, None)

    def feed_out(self, pieces):
        return pieces[0]

    def after(self, value, *others):
        return value

    def stage(self, work, *values):
        return work(*values)

    def sends(self, left, right):
        return ()

    def exchange(self, sends):
        return ()

    def merged(self, *sends):
        return ()

    def parted(self, far, *widths):
        return [()] * len(widths)

    def adds(self, *products):
        wholes = [mm_rows(left, right).astype(BF) for left, right, _ in products]
        return jnp.concatenate(wholes, axis=1)

    def second(self, whole):
        return ()

    def closing(self, whole, far):
        return whole

    middle = closing

    def scatter_z(self, whole):
        return lax.psum_scatter(whole, self.dp, scatter_dimension=0, tiled=True)

    def close_middle(self, whole):
        return whole.astype(F32)

    def close_last(self, whole, *widths):
        found, at = [], 0
        for columns in widths:
            found.append(whole[:, at : at + columns].astype(F32))
            at += columns
        return found

    def norm_sums(self, sums):
        sums = jnp.pad(sums.T, ((0, 0), (0, 122))).astype(BF)
        sums = lax.psum_scatter(sums, self.dp, scatter_dimension=0, tiled=True)
        return self.sum_all(sums)[:, :6].T

    def spread(self, rows, clips):
        local = rows.reshape(clips, -1, rows.shape[-1])
        return lax.all_gather(local, self.tensor, axis=1, tiled=True).reshape(-1, rows.shape[-1])

    def sequence(self, rows, clips):
        return rows.reshape(clips, -1, rows.shape[-1])

    def unsequence(self, rows):
        return rows.reshape(-1, rows.shape[-1])

    def clip_rows(self, rows, clips):
        return rows.reshape(clips, -1, rows.shape[-1])

    unclip_rows = unsequence

    def self_attend(self, qkv, clips):
        qkv = self.sequence(qkv, clips)
        cols = qkv.shape[-1] // 3
        q, k, v = qkv[..., :cols], qkv[..., cols : 2 * cols], qkv[..., 2 * cols :]
        att, log_total = attend(q, k, v)
        return self.unsequence(att), (q, k, v, log_total)

    def self_back(self, saved, grad, clips):
        dq, dk, dv = attend_back(*saved, self.sequence(grad, clips))
        return self.unsequence(jnp.concatenate([dq, dk, dv], axis=-1))

    def cross_attend(self, q, memory, clips):
        q = self.clip_rows(q, clips)
        memory = memory.reshape(clips, -1, memory.shape[-1])
        cols = q.shape[-1]
        k, v = memory[..., :cols], memory[..., cols:]
        out, chances = cross_attend(q, k, v)
        return self.unclip_rows(out), (q, k, v, chances)

    def cross_back(self, saved, grad, clips):
        dq, dk, dv = cross_attend_back(*saved, self.clip_rows(grad, clips))
        return self.unclip_rows(dq), self.unsequence(jnp.concatenate([dk, dv], axis=-1))

    def feed(self, rows, weight):
        return gelu_pair(mm(rows, weight))

    def slope_product(self, rows, weight, slope):
        return (mm(rows, weight) * slope.astype(F32)).astype(BF)

    def sum_own(self, left, right, product, clips):
        part = product(left, right).astype(BF).reshape(clips, -1, right_width(product, right))
        own = lax.psum_scatter(part, self.tensor, scatter_dimension=1, tiled=True)
        return own.reshape(-1, part.shape[-1]).astype(F32)

    def sum_all(self, values):
        return lax.psum(values.astype(BF), self.tensor).astype(F32)


def right_width(product, right):
    return right.shape[0] if product is mm_t else right.shape[1]


class Block(Whole):
    def __init__(self, width):
        self.width = width
        self.shard = width // 16
        self.core = lax.axis_index("core")

    def after(self, value, *others):
        return tie(value, others)

    def order(self):
        own_y, own_x = lax.axis_index("y"), lax.axis_index("x")
        place = jnp.arange(self.width, dtype=jnp.int32)
        quarter, rest = place // (4 * self.shard), place % (4 * self.shard)
        z, row = rest // self.shard, rest % self.shard
        y, x = (quarter // 2) ^ own_y, (quarter % 2) ^ own_x
        source = ((z * 2 + y) * 2 + x) * self.shard + row
        return (jnp.arange(self.width, dtype=jnp.int32)[:, None] == source[None, :]).astype(BF)

    def arrange(self, values):
        return mm(values, self.order()).astype(BF)

    def restore(self, values):
        if values.dtype == BF:
            return mm_t(values, self.order()).astype(BF)
        high = lax.reduce_precision(values, 8, 7)
        low = (values - high).astype(BF)
        order = self.order()
        return mm_t(high.astype(BF), order) + mm_t(low, order)

    def x(self, v):
        return lax.ppermute(v, "x", SWAP)

    def y(self, v):
        return lax.ppermute(v, "y", SWAP)

    def other(self, v):
        return lax.ppermute(v, "core", SWAP)

    def gather_norms(self, packed):
        pair = jnp.stack([packed, lax.ppermute(packed, "z", [(0, 1), (1, 0), (2, 3), (3, 2)])])
        far = lax.ppermute(pair, "z", [(0, 2), (1, 3), (2, 0), (3, 1)])
        own = lax.axis_index("z")
        four = jnp.concatenate([pair, far])
        four = jnp.stack([lax.dynamic_index_in_dim(four, own ^ p, 0, False) for p in range(4)])
        two = jnp.stack([four, self.x(four)])
        whole = jnp.stack([two, self.y(two)])
        return whole.reshape(self.width, packed.shape[-1])

    def halves(self, shard):
        half = shard.shape[1] // 256 * 128
        return shard[:, :half], shard[:, half:]

    def gather_first_set(self, first, second, feed_in, feed_out, rows):
        opened = []
        for shard in (feed_in, feed_out):
            a, b = self.halves(shard)
            opened.append(jnp.stack([a, self.x(a), b, self.y(b)]))
        rows, opened = lax.optimization_barrier((rows, opened))
        sets = [lax.all_gather(shard, "z", axis=0, tiled=True) for shard in (first, second)]
        feeds = [lax.all_gather(four, "z", axis=1, tiled=True) for four in opened]
        pieces, last, _ = self.gather_pieces(sets[0], rows)
        pieces_next = self.gather_pieces(sets[1], last)
        return pieces, rows, (pieces_next, feeds)

    def gather_pieces(self, four, last):
        a, b = self.halves(tie(four, last))
        xa, yb, ya, xb = self.x(a), self.y(b), self.y(a), self.x(b)
        far_a, far_b = self.y(xa), self.x(yb)
        return (four, xa, ya, far_a, xb, yb, far_b), (far_a, far_b, ya, xb), (xa, yb)

    def place_pieces(self, pieces):
        four, xa, ya, far_a, xb, yb, far_b = pieces
        n, half = xa.shape
        return place(
            [
                (four, 0, 0),
                (xa, n, 0),
                (ya, 2 * n, 0),
                (far_a, 3 * n, 0),
                (xb, n, half),
                (yb, 2 * n, half),
                (far_b, 3 * n, half),
            ],
            (4 * n, four.shape[1]),
        )

    def gather_rest(self, rest, value):
        (pieces, last, _), feeds = rest
        feeds[0] = tie(feeds[0], value)
        in_sides = feeds[0][:2], feeds[0][2:]
        a, b = tie(in_sides, last)
        in_far = self.y(a), self.x(b)
        w_cross = self.place_pieces(pieces)
        w_in = self.place_feed(feeds[0], in_far)
        out_sides = feeds[1][:2], feeds[1][2:]
        a, b = tie(out_sides, in_far)
        return w_cross, w_in, in_far, out_sides, (feeds[1], (self.y(a), self.x(b)))

    def place_feed(self, four, far):
        _, n, half = four.shape
        return place_stacked(
            four.reshape(4 * n, half), far[0].reshape(2 * n, half), far[1].reshape(2 * n, half)
        )

    def feed_out(self, pieces):
        return self.place_feed(*pieces)

    def stage(self, work, *values):
        shapes = jax.eval_shape(work, *values)

        def nothing(*_):
            return jax.tree.map(lambda leaf: jnp.zeros(leaf.shape, leaf.dtype), shapes)

        return lax.cond(self.core < 2, work, nothing, *values)

    def sends(self, left, right):
        n, half = self.width // 4, right.shape[1] // 256 * 128
        far = jnp.concatenate([left[:, n : 2 * n], left[:, 3 * n :]], axis=1)
        return (
            mm_rows(left[:, 2 * n :], right[:, :half]).astype(BF),
            mm_rows(far, right[:, half:]).astype(BF),
        )

    def exchange(self, sends):
        return self.y(sends[0]), self.x(sends[1])

    def merged(self, *sends):
        return [jnp.concatenate(side, axis=1) for side in zip(*sends)]

    def parted(self, far, *widths):
        halves = [width // 256 * 128 for width in widths]
        ends = [sum(halves[: i + 1]) for i in range(len(halves) - 1)]
        lefts = jnp.split(far[0], ends, axis=1)
        halves = [width - half for width, half in zip(widths, halves)]
        ends = [sum(halves[: i + 1]) for i in range(len(halves) - 1)]
        return list(zip(lefts, jnp.split(far[1], ends, axis=1)))

    def adds(self, *products):
        n, parts = self.width // 4, []
        for left, right, (far_y, far_x) in products:
            half = right.shape[1] // 256 * 128
            first = (mm_rows(left[:, : 2 * n], right[:, :half]) + far_y.astype(F32)).astype(BF)
            near = jnp.concatenate([left[:, :n], left[:, 2 * n : 3 * n]], axis=1)
            last = (mm_rows(near, right[:, half:]) + far_x.astype(F32)).astype(BF)
            parts.append((first[:n], first[n:], last[:n], last[n:]))
        return [jnp.concatenate(part, axis=1) for part in zip(*parts)]

    def middle(self, parts, _):
        return jnp.stack(parts)

    def second(self, parts):
        return self.x(parts[1]), self.y(parts[3])

    def closing(self, parts, far):
        pairs = zip((parts[0], parts[2]), far)
        return jnp.stack([(own.astype(F32) + other.astype(F32)).astype(BF) for own, other in pairs])

    def scatter_z(self, parts):
        return lax.psum_scatter(parts, "z", scatter_dimension=1, tiled=True)

    def close_middle(self, four):
        left = four[0].astype(F32) + self.x(four[1]).astype(F32)
        right = four[2].astype(F32) + self.y(four[3]).astype(F32)
        return jnp.concatenate([left, right], axis=1)

    def close_last(self, both, *widths):
        found, left, right = [], 0, 0
        for columns in widths:
            a = columns // 256 * 128
            b = columns - a
            found.append(
                jnp.concatenate([both[0, :, left : left + a], both[1, :, right : right + b]], axis=1)
            )
            left, right = left + a, right + b
        return [part.astype(F32) for part in found]

    def norm_sums(self, sums):
        n = self.width // 4
        sums = self.sum_all(jnp.pad(sums.T, ((0, 0), (0, 122))))
        sums = sums[: 2 * n] + self.y(sums[2 * n :].astype(BF)).astype(F32)
        sums = sums[:n] + self.x(sums[n:].astype(BF)).astype(F32)
        own = lax.axis_index("z")
        for step, pairs, side in (
            (n // 2, [(0, 2), (1, 3), (2, 0), (3, 1)], own // 2),
            (n // 4, [(0, 1), (1, 0), (2, 3), (3, 2)], own % 2),
        ):
            near = lax.dynamic_slice_in_dim(sums, side * step, step)
            away = lax.dynamic_slice_in_dim(sums, (1 - side) * step, step)
            sums = near + lax.ppermute(away.astype(BF), "z", pairs).astype(F32)
        return sums[:, :6].T

    def spread(self, rows, clips):
        return jnp.concatenate([rows, self.other(rows)])

    def self_attend(self, qkv, clips):
        cols = qkv.shape[-1] // 3
        steps = cols // (2 * HEAD_DIM)
        view = qkv.reshape(2, clips, -1, qkv.shape[-1])
        frames = view.shape[2]

        def block(part):
            return pl.BlockSpec(
                (2, 1, frames, 2 * HEAD_DIM), lambda c, j, _: (0, c, 0, part * steps + j)
            )

        shape = (2, clips, frames, cols)
        core = self.core.reshape(1).astype(jnp.int32)
        scores = clips * steps * 2 * 3 * frames * frames
        out, log_total = pl.pallas_call(
            self_kernel,
            grid_spec=pltpu.PrefetchScalarGridSpec(
                num_scalar_prefetch=1,
                grid=(clips, steps),
                in_specs=[block(0), block(1), block(2)],
                out_specs=[block(0), block(0)],
            ),
            out_shape=[jax.ShapeDtypeStruct(shape, BF), jax.ShapeDtypeStruct(shape, F32)],
            cost_estimate=pl.CostEstimate(
                flops=4 * scores * HEAD_DIM,
                transcendentals=scores,
                bytes_accessed=2 * qkv.size + 6 * qkv.size // 3,
            ),
            name="self_attend",
        )(core, view, view, view)
        return out.reshape(-1, cols), (core, view, log_total)

    def self_back(self, saved, grad, clips):
        core, view, log_total = saved
        cols = view.shape[-1] // 3
        steps = cols // (2 * HEAD_DIM)
        frames = view.shape[2]

        def block(part):
            return pl.BlockSpec(
                (2, 1, frames, 2 * HEAD_DIM), lambda c, j, _: (0, c, 0, part * steps + j)
            )

        scores = clips * steps * 2 * 3 * frames * frames
        out = pl.pallas_call(
            self_back_kernel,
            grid_spec=pltpu.PrefetchScalarGridSpec(
                num_scalar_prefetch=1,
                grid=(clips, steps),
                in_specs=[block(0), block(1), block(2), block(0), block(0)],
                out_specs=pl.BlockSpec((2, 1, frames, 3 * cols), lambda c, j, _: (0, c, 0, 0)),
            ),
            out_shape=jax.ShapeDtypeStruct(view.shape, BF),
            cost_estimate=pl.CostEstimate(
                flops=10 * scores * HEAD_DIM,
                transcendentals=scores,
                bytes_accessed=4 * view.size + 6 * view.size // 3,
            ),
            name="self_back",
        )(core, view, view, view, log_total, grad.reshape(2, clips, frames, cols))
        return out.reshape(-1, 3 * cols)

    def cross_specs(self, q, clips, texts):
        cols = q.shape[-1]
        steps = cols // (2 * HEAD_DIM)
        view = q.reshape(2, clips, -1, cols)
        frames = view.shape[2]
        wide = pl.BlockSpec((2, 1, frames, 2 * HEAD_DIM), lambda c, j: (0, c, 0, j))

        def block(part):
            return pl.BlockSpec((1, texts, 2 * HEAD_DIM), lambda c, j: (c, 0, part * steps + j))

        return view, (clips, steps), wide, block, clips * 2 * frames * cols * texts

    def cross_attend(self, q, memory, clips):
        memory = memory.reshape(clips, -1, memory.shape[-1])
        view, grid, wide, block, work = self.cross_specs(q, clips, memory.shape[1])
        out = pl.pallas_call(
            cross_kernel,
            grid=grid,
            in_specs=[wide, block(0), block(1)],
            out_specs=wide,
            out_shape=jax.ShapeDtypeStruct(view.shape, BF),
            cost_estimate=pl.CostEstimate(
                flops=4 * work, transcendentals=work // HEAD_DIM, bytes_accessed=4 * q.size
            ),
            name="cross_attend",
        )(view, memory, memory)
        return out.reshape(q.shape), (q, memory)

    def cross_back(self, saved, grad, clips):
        q, memory = saved
        texts = memory.shape[1]
        view, grid, wide, block, work = self.cross_specs(q, clips, texts)
        dq, dkv = pl.pallas_call(
            cross_back_kernel,
            grid=grid,
            in_specs=[wide, block(0), block(1), wide],
            out_specs=[
                wide,
                pl.BlockSpec((1, texts, memory.shape[-1]), lambda c, j: (c, 0, 0)),
            ],
            out_shape=[
                jax.ShapeDtypeStruct(view.shape, BF),
                jax.ShapeDtypeStruct(memory.shape, BF),
            ],
            cost_estimate=pl.CostEstimate(
                flops=10 * work, transcendentals=work // HEAD_DIM, bytes_accessed=6 * q.size
            ),
            name="cross_back",
        )(view, memory, memory, grad.reshape(view.shape))
        return dq.reshape(q.shape), dkv.reshape(-1, memory.shape[-1])

    def feed(self, rows, weight):
        return feed(rows, weight)

    def slope_product(self, rows, weight, slope):
        return slope_product(rows, weight, slope)

    def sum_own(self, left, right, product, clips):
        n = left.shape[0] // 2
        far = self.other(product(left[n:], right).astype(BF))
        return product(left[:n], right) + far.astype(F32)

    def sum_all(self, values):
        return values + self.other(values.astype(BF)).astype(F32)


def layer(
    comm,
    frames,
    text_states,
    norm_gain,
    norm_shift,
    self_project,
    self_output,
    cross_query,
    cross_memory,
    cross_output,
    feed_input,
    feed_output,
    upstream,
):
    clips, own_frames, width = frames.shape
    texts = text_states.shape[1]
    cols = cross_query.shape[1]
    own_rows = clips * own_frames

    def catenate(parts):
        return jnp.concatenate(parts, axis=1)

    norms = comm.gather_norms(
        jnp.pad(jnp.concatenate([norm_gain, norm_shift]).T, ((0, 0), (0, 122)))
    )
    norms = norms.T.astype(F32)
    gain, shift = norms[0:3], norms[3:6]
    first_set = catenate([self_project[0], self_project[1], self_project[2]])
    second_set = catenate(
        [self_output.T, cross_query, cross_memory[0], cross_memory[1], cross_output.T]
    )
    values0 = comm.arrange(frames.reshape(own_rows, width)).astype(F32)
    stats0 = norm_stats(values0)
    own_n1 = norm_apply(values0, stats0, gain[0], shift[0])
    pieces, own_n1, rest = comm.gather_first_set(
        first_set, second_set, feed_input, feed_output.T, own_n1
    )
    up = comm.arrange(upstream.reshape(own_rows, width))
    text = comm.arrange(text_states.reshape(clips * texts, width))
    up_all = comm.spread(up, clips)

    n1 = comm.spread(own_n1, clips)

    def split_cross(weights):
        return jnp.split(weights, [cols, 2 * cols, 4 * cols], axis=1)

    def stage_self(pieces, n1):
        w_self = comm.place_pieces(pieces)
        return w_self, comm.self_attend(mm(n1, w_self).astype(BF), clips)

    w_self, (att, self_saved) = comm.stage(stage_self, pieces, n1)
    w_cross, w_in, mark_in, mark_out, out_pieces = comm.gather_rest(rest, att)

    def stage0(values0, att, w_cross, text):
        w_so, w_cq, w_cm, w_co = split_cross(w_cross)
        values1 = values0 + comm.sum_own(att, w_so, mm_t, clips)
        stats1 = norm_stats(values1)
        n2 = comm.spread(norm_apply(values1, stats1, gain[1], shift[1]), clips)
        cross, saved = comm.cross_attend(
            mm(n2, w_cq).astype(BF), mm(text, w_cm).astype(BF), clips
        )
        values2 = values1 + comm.sum_own(cross, w_co, mm_t, clips)
        stats2 = norm_stats(values2)
        n3 = comm.spread(norm_apply(values2, stats2, gain[2], shift[2]), clips)
        return values1, stats1, n2, cross, saved, values2, stats2, n3

    values1, stats1, n2, cross, cross_saved, values2, stats2, n3 = comm.stage(
        stage0, values0, att, w_cross, text
    )
    n3 = comm.after(n3, mark_in, mark_out)
    hidden, slope = comm.feed(n3, w_in)
    send_out = comm.sends(up_all, hidden)
    hidden, slope = comm.after((hidden, slope), out_pieces[1], send_out)
    far_out = comm.exchange(send_out)

    def stage1(pieces, rows, slope, n3, w_in):
        w_out = comm.feed_out(pieces)
        pre_grad = comm.slope_product(rows, w_out, slope)
        return w_out, pre_grad, comm.sends(n3, pre_grad), comm.sum_own(pre_grad, w_in, mm_t, clips)

    w_out, pre_grad, send_in, e3 = comm.stage(stage1, out_pieces, up_all, slope, n3, w_in)
    e3 = comm.after(e3, far_out)
    far_in = comm.exchange(send_in)

    def stage2(rows, hidden, far, e3, values2, stats2, own):
        sent = comm.middle(comm.adds((rows, hidden, far)), None)
        grads = norm_back(values2, stats2, gain[2], e3)
        r2 = own.astype(F32) + grads[0]
        return sent, r2, r2.astype(BF), grads[1], grads[2]

    sent_out, r2, r2_own, gain2, shift2 = comm.stage(
        stage2, up_all, hidden, far_out, e3, values2, stats2, up
    )
    half_out = comm.scatter_z(sent_out)

    def stage3(r2_own, saved, w_cross, n2, cross, text):
        w_co = split_cross(w_cross)[3]
        r2_all = comm.spread(r2_own, clips)
        dcq, dmem = comm.cross_back(saved, mm(r2_all, w_co).astype(BF), clips)
        pairs = (n2, dcq), (r2_all, cross), (text, dmem)
        return r2_all, dcq, dmem, comm.merged(*[comm.sends(*pair) for pair in pairs])

    r2_all, dcq, dmem, send_cross = comm.stage(
        stage3, r2_own, cross_saved, w_cross, n2, cross, text
    )
    dcq = comm.after(dcq, far_in)
    far_cross = comm.exchange(send_cross)
    cross_pairs = (n2, dcq), (r2_all, cross), (text, dmem)

    def stage4(n3, pre_grad, far, dcq, w_cross, values1, stats1, r2):
        w_so, w_cq, *_ = split_cross(w_cross)
        in_sums = comm.adds((n3, pre_grad, far))
        e2 = comm.sum_own(dcq, w_cq, mm_t, clips)
        grads = norm_back(values1, stats1, gain[1], e2)
        r1 = r2 + grads[0]
        r1_all = comm.spread(r1.astype(BF), clips)
        return in_sums, r1, r1_all, mm(r1_all, w_so).astype(BF), grads[1], grads[2]

    in_sums, r1, r1_all, datt, gain1, shift1 = comm.stage(
        stage4, n3, pre_grad, far_in, dcq, w_cross, values1, stats1, r2
    )
    datt = comm.after(datt, far_cross, half_out)
    in_second = comm.second(in_sums)

    def stage5(pairs, far, r1_all, att):
        far = comm.parted(far, cols, cols, 2 * cols)
        sums = comm.adds(*[(*pair, one) for pair, one in zip(pairs, far)])
        return sums, comm.sends(r1_all, att)

    cross_sums, send_so = comm.stage(stage5, cross_pairs, far_cross, r1_all, att)
    datt, in_late = comm.after((datt, in_sums), in_second, send_so)
    cross_second = comm.second(cross_sums)
    far_so = comm.exchange(send_so)
    half_in = comm.scatter_z(comm.closing(in_late, in_second))

    def stage_back(saved, datt, n1):
        dqkv = comm.self_back(saved, datt, clips)
        return dqkv, comm.sends(n1, dqkv)

    dqkv, send_self = comm.stage(stage_back, self_saved, datt, n1)
    dmem, hidden, send_self, cross_late, dqkv, far_so = comm.after(
        (dmem, hidden, send_self, cross_sums, dqkv, far_so), cross_second, half_in
    )
    far_self = comm.exchange(send_self)
    half_cross = comm.scatter_z(comm.closing(cross_late, cross_second))

    def stage6(dmem, w_cross, values2, hidden, w_out, r1_all, att, far):
        w_cm = split_cross(w_cross)[2]
        so_sums = comm.adds((r1_all, att, far))
        text_grad = comm.sum_all(mm_t(dmem, w_cm))
        layer_out = (values2 + comm.sum_own(hidden, w_out, mm_t, clips)).astype(BF)
        return comm.restore(text_grad), comm.restore(layer_out), so_sums

    text_grad, layer_out, so_sums = comm.stage(
        stage6, dmem, w_cross, values2, hidden, w_out, r1_all, att, far_so
    )
    text_grad, layer_out, dqkv, half_out, half_in, so_sums = comm.after(
        (text_grad, layer_out, dqkv, half_out, half_in, so_sums), far_self, half_cross
    )
    so_second = comm.second(so_sums)
    dqkv = comm.after(dqkv, so_second)
    self_sums = comm.adds((n1, dqkv, far_self))
    dqkv = comm.after(dqkv, self_sums)
    self_second = comm.second(self_sums)
    half_so = comm.scatter_z(comm.closing(so_sums, so_second))

    def stage7(dqkv, w_self):
        return comm.sum_own(dqkv, w_self, mm_t, clips)

    e1 = comm.stage(stage7, dqkv, w_self)
    e1, self_late = comm.after((e1, self_sums), self_second, half_so)
    closed = comm.closing(self_late, self_second)
    e1 = comm.after(e1, closed)
    half_self = comm.scatter_z(closed)
    dv0, gain0, shift0 = norm_back(values0, stats0, gain[0], e1)
    input_grad = comm.restore(r1 + dv0)
    norm_grad = comm.norm_sums(jnp.stack([gain0, gain1, gain2, shift0, shift1, shift2]))
    input_grad = input_grad.reshape(clips, own_frames, width)
    text_grad = text_grad.reshape(clips, texts, width)
    layer_out = layer_out.reshape(clips, own_frames, width)
    grad_out = comm.close_middle(half_out)
    (grad_in,) = comm.close_last(half_in, pre_grad.shape[1])
    grad_cq, grad_co, grad_cm = comm.close_last(half_cross, cols, cols, 2 * cols)
    (grad_so,) = comm.close_last(half_so, cols)
    (grad_self,) = comm.close_last(half_self, 3 * cols)
    return (
        layer_out,
        input_grad,
        text_grad,
        norm_grad[0:3],
        norm_grad[3:6],
        jnp.stack([grad_self[:, i * cols : (i + 1) * cols] for i in range(3)]),
        grad_so.T,
        grad_cq,
        jnp.stack([grad_cm[:, :cols], grad_cm[:, cols:]]),
        grad_co.T,
        grad_in,
        grad_out.T,
    )


def specs(dp, tensor):
    in_specs = (
        P(dp, tensor, None),
        P(dp, None, None),
        P(None, dp),
        P(None, dp),
        P(None, dp, tensor),
        P(tensor, dp),
        P(dp, tensor),
        P(None, dp, tensor),
        P(tensor, dp),
        P(dp, tensor),
        P(tensor, dp),
        P(dp, tensor, None),
    )
    out_specs = (
        P(dp, tensor, None),
        P(dp, tensor, None),
        P(dp, None, None),
        P(None, dp),
        P(None, dp),
        P(None, dp, tensor),
        P(tensor, dp),
        P(dp, tensor),
        P(None, dp, tensor),
        P(tensor, dp),
        P(dp, tensor),
        P(tensor, dp),
    )
    return in_specs, out_specs


def solution(mesh):
    if mesh.shape["dp"] == 16 and mesh.shape["tensor"] == 2:
        mesh = Mesh(mesh.devices.reshape(4, 2, 2, 2), ("z", "y", "x", "core"))
        in_specs, out_specs = specs(("z", "y", "x"), "core")

        def per_device(frames, *rest):
            return layer(Block(frames.shape[-1]), frames, *rest)
    else:
        in_specs, out_specs = specs("dp", "tensor")

        def per_device(frames, *rest):
            return layer(Whole("dp", "tensor"), frames, *rest)

    return jax.shard_map(
        per_device, mesh=mesh, in_specs=in_specs, out_specs=out_specs, check_vma=False
    )
```
